32 devices in a mesh: scene: 2 (over x), mrow: 8 (over z, y), mcol: 2 (over core).
Axes of the slice: x: 2, y: 2, z: 4, core: 2. Of those that a mesh axis runs over, the one named last changes fastest.
Arguments:
- pan_blocks: bfloat16 [2048, 128, 128], P(('scene', 'mrow', 'mcol')), parts along dimension 0, may hold values from -6 to 6
- ms_blocks: bfloat16 [2048, 32, 256], P(('scene', 'mrow', 'mcol')), parts along dimension 0, may hold values from -6 to 6
- send_list: int32 [3, 2048], P(None, ('scene', 'mrow', 'mcol')), parts along dimension 1, may hold values from 0 to 127, as said below
- tile_list: int32 [3, 4096], P(None, ('scene', 'mrow', 'mcol')), parts along dimension 1, may hold values from 0 to 9, as said below
- row_grid: float32 [48], P(('scene', 'mrow')), parts along dimension 0, may hold values from -32 to 288
- col_grid: float32 [16, 16], P(('scene', 'mrow'), 'mcol'), parts along dimension 0, may hold values from -32 to 1312
- band_mix: float32 [8, 8], replicated, may hold values from -1.5 to 1.5
- band_gain: float32 [8], replicated, may hold values from 0.4 to 1.2
- synth_weight: float32 [8], replicated, may hold values from 0.05 to 0.3
Outputs:
- sharpened: bfloat16 [8, 2048, 1024], P(None, ('scene', 'mrow'), 'mcol'), parts along dimension 1
The draws below stay inside these ranges and needn't reach their ends.
There are 2 independent parts, one for each index of `scene`. The reference program is written for one: setup_inputs(seed, part) draws one part's arguments, and reference() takes and returns one part's arrays. A program takes and returns all parts, laid end to end along the dimension named above; an argument that names none is the same for every part. Nothing has to cross between parts.
Inputs may be any that keep to these rules, and one draw needn't show every extreme that they name: `send_list`: row 0 gives each source block of a device a distinct send slot; slot p goes to map-row owner p // 16 in the device's own map column, so one device sends at most 16 blocks to one tile; in every draw one tile of each map column receives 16 blocks from every device of that column, and every device fills 16 slots of it. Row 1 is a cell row below 2; row 2 a cell column between mcol * 5 and mcol * 5 + 4. `tile_list`: row 0 is 1 exactly in the receive slots that send_list fills and 0 elsewhere; rows 1 and 2 repeat the cell row and column of the block sent there, and are 0 in empty slots.
All inputs are finite; a program needn't handle non-finite values.
Results may differ from the reference program's by a relative error of at most 0.0073.
Values may be sent and summed in bfloat16 or wider, within the bound.
A program may use at most 128 MiB of HBM per device.

```python
import math
import jax
import jax.numpy as jnp
from jax import lax

BANDS = 8
BS = 128
GRID = 64
TR = 128
TC = 512
SBD = 64
MB = 32
KR = 2
KC = 5
NR = 1024
NC = 1024
N_MROW = 8
N_MCOL = 2


def route_tables(key):
    devices = N_MROW * N_MCOL
    partition_total = 2 * SBD
    capacity = partition_total // N_MROW
    stochastic_seed_sequence = jax.random.split(jax.random.fold_in(key, 4242), 6)
    favoured = jax.random.randint(stochastic_seed_sequence[0], (N_MCOL,), 0, N_MROW)
    preference_extra_digits = jax.random.randint(stochastic_seed_sequence[1], (N_MCOL, N_MROW), 0, 4)
    stochastic_perturb_digits = jax.random.randint(stochastic_seed_sequence[2], (devices, partition_total), 0, 1024)
    partition_number = jnp.arange(partition_total, dtype=jnp.int32)
    keeper_line = partition_number // capacity
    horizontal_location = jnp.arange(devices, dtype=jnp.int32) % N_MCOL
    reached_capacity_flag = (keeper_line[None, :] == jnp.take(favoured, horizontal_location)[:, None]).astype(jnp.int32)
    preference_extra_order = jnp.take(jnp.take(preference_extra_digits, horizontal_location, axis=0), keeper_line, axis=1)
    preference_grades = ((reached_capacity_flag * 8 + preference_extra_order) * 1024 + stochastic_perturb_digits) * partition_total + partition_number[None, :]
    top_scores, chosen = lax.top_k(preference_grades, SBD)
    shuffle = jax.random.randint(stochastic_seed_sequence[5], (devices, SBD), 0, 4096) * SBD + jnp.arange(SBD, dtype=jnp.int32)[None, :]
    reorder = jnp.argsort(shuffle, axis=1)
    chosen = jnp.take_along_axis(chosen, reorder, axis=1).astype(jnp.int32)
    cell_rows = jax.random.randint(stochastic_seed_sequence[3], (devices, SBD), 0, KR)
    cell_cols = horizontal_location[:, None] * KC + jax.random.randint(stochastic_seed_sequence[4], (devices, SBD), 0, KC)
    flat_slots = chosen.reshape(-1)
    sender = jnp.repeat(jnp.arange(devices, dtype=jnp.int32), SBD)
    destination = (flat_slots // capacity * N_MCOL + sender % N_MCOL) * partition_total + sender // N_MCOL * capacity + flat_slots % capacity
    entries = jnp.stack([jnp.ones_like(flat_slots), cell_rows.reshape(-1), cell_cols.reshape(-1)]).astype(jnp.int32)
    tile_table = jnp.zeros((3, devices * partition_total), jnp.int32).at[:, destination].set(entries)
    send_table = jnp.stack([flat_slots, cell_rows.reshape(-1), cell_cols.reshape(-1)]).astype(jnp.int32)
    return (send_table, tile_table)


def draw_send_list(key, part):
    return route_tables(key)[0]


def draw_tile_list(key, part):
    return route_tables(key)[1]


def draw_row_grid(key, part):
    node_count = TR // GRID + 1
    stochastic_seed_sequence = jax.random.split(jax.random.fold_in(key, 11), 3)
    reach = float(KR * BS)
    lead_gap = jax.random.uniform(stochastic_seed_sequence[0], (N_MROW, 1), minval=1.0, maxval=6.0)
    tail_gap = jax.random.uniform(stochastic_seed_sequence[1], (N_MROW, 1), minval=1.0, maxval=6.0)
    shake = 0.15
    fraction = jnp.arange(node_count, dtype=jnp.int32).astype(jnp.float32) / (node_count - 1)
    jitter = jax.random.uniform(stochastic_seed_sequence[2], (N_MROW, node_count), minval=-1.0, maxval=1.0) * (shake * GRID)
    nodes_all = lead_gap + (reach - lead_gap - tail_gap) * fraction[None, :] + jitter
    return nodes_all.reshape(-1).astype(jnp.float32)


def draw_col_grid(key, part):
    node_count = NC // GRID
    stochastic_seed_sequence = jax.random.split(jax.random.fold_in(key, 23), 3)
    reach = float(N_MCOL * KC * BS)
    lead_gap = jax.random.uniform(stochastic_seed_sequence[0], (N_MROW, 1), minval=1.0, maxval=6.0)
    tail_gap = jax.random.uniform(stochastic_seed_sequence[1], (N_MROW, 1), minval=1.0, maxval=6.0)
    shake = 0.15
    fraction = (GRID * jnp.arange(node_count, dtype=jnp.int32)).astype(jnp.float32) / NC
    jitter = jax.random.uniform(stochastic_seed_sequence[2], (N_MROW, node_count), minval=-1.0, maxval=1.0) * (shake * GRID)
    return (lead_gap + (reach - lead_gap - tail_gap) * fraction[None, :] + jitter).astype(jnp.float32)


def shard_levels(own_key, extent, shards, smallest, high):
    gain = 1.0
    for dim, shards_of in shards:
        heights = jax.random.uniform(jax.random.fold_in(jax.random.fold_in(own_key, 6), dim), (shards_of,), jnp.float32, smallest / len(shards), high / len(shards))
        gain = gain * jnp.repeat(jnp.exp(heights), extent[dim] // shards_of).reshape((-1,) + (1,) * (len(extent) - 1 - dim))
    return gain


def bell_draw(stream_key, shape, spread, most, pieces=(), kind=jnp.bfloat16):
    values = jax.random.normal(stream_key, shape, jnp.float32) * spread
    if len(pieces) > 0:
        values = shard_levels(stream_key, shape, pieces, -0.22, 0.18) * values
    return jnp.clip(values, min=-most, max=most).astype(kind)


def setup_inputs(seed: int = 0, part: int = 0) -> dict:
    streams_of = jax.random.split(jax.random.key(seed), 10)
    part_splits = jax.random.split(jax.random.fold_in(streams_of[9], part), 10)
    return {
        "pan_blocks": bell_draw(part_splits[0], (N_MROW * N_MCOL * SBD, BS, BS), 1.0, 6.0, ((0, 16),)),
        "ms_blocks": bell_draw(part_splits[1], (N_MROW * N_MCOL * SBD, MB, BANDS * MB), 1.0, 6.0, ((0, 16),)),
        "send_list": draw_send_list(jax.random.fold_in(jax.random.fold_in(streams_of[9], part), 71), part),
        "tile_list": draw_tile_list(jax.random.fold_in(jax.random.fold_in(streams_of[9], part), 71), part),
        "row_grid": draw_row_grid(jax.random.fold_in(jax.random.fold_in(streams_of[9], part), 71), part),
        "col_grid": draw_col_grid(jax.random.fold_in(jax.random.fold_in(streams_of[9], part), 71), part),
        "band_mix": bell_draw(streams_of[6], (BANDS, BANDS), 0.3, 1.5, (), jnp.float32),
        "band_gain": jnp.clip(jax.random.uniform(streams_of[7], (BANDS,), jnp.float32, 0.4, 1.2), 0.4, 1.2),
        "synth_weight": jnp.clip(jnp.exp(jax.random.uniform(streams_of[8], (BANDS,), jnp.float32, math.log(0.05), math.log(0.3))), 0.05, 0.3),
    }


highest = lax.Precision.HIGHEST


def cubic_weight(offset):
    distance = jnp.abs(offset)
    near_part = (1.5 * distance - 2.5) * distance * distance + 1.0
    far_part = ((-0.5 * distance + 2.5) * distance - 4.0) * distance + 2.0
    return jnp.where(distance <= 1.0, near_part, jnp.where(distance < 2.0, far_part, jnp.zeros_like(distance)))


def along_nodes(node_values, position, offset, spacing):
    segment = jnp.minimum(position // spacing, node_values.shape[-1] - 2)
    left_node = jnp.take(node_values, segment, axis=-1)
    right_node = jnp.take(node_values, segment + 1, axis=-1)
    within = ((position - segment * spacing).astype(jnp.float32) + offset) / spacing
    return left_node + (right_node - left_node) * within


def source_weights(coords, cell_ids, block_size):
    pixels = (cell_ids[:, None, None] * block_size + jnp.arange(block_size, dtype=jnp.int32)[None, None, :]).astype(jnp.float32)
    return cubic_weight(coords[:, :, None] - pixels).astype(jnp.bfloat16)


def row_weights(coords, cell_ids, is_valid, block_size):
    pixels = (cell_ids[None, :, None] * block_size + jnp.arange(block_size, dtype=jnp.int32)[None, None, :]).astype(jnp.float32)
    return (cubic_weight(coords[:, None, None] - pixels) * is_valid[None, :, None]).astype(jnp.bfloat16)


def upsample_table(length, coarse):
    position = (jnp.arange(length, dtype=jnp.int32).astype(jnp.float32) - 1.5) * 0.25 + 2.0
    taps = jnp.arange(coarse + 4, dtype=jnp.int32).astype(jnp.float32)
    return cubic_weight(position[:, None] - taps[None, :]).astype(jnp.bfloat16)


def combine(upsampled, pan_map, band_mix, band_gain, synth_weight):
    mixture = jnp.transpose(upsampled, (1, 0, 2)) + jnp.einsum("bk,rkc->brc", band_mix, upsampled, precision=highest)
    synthetic = jnp.einsum("k,rkc->rc", synth_weight, upsampled, precision=highest)
    return (mixture + band_gain[:, None, None] * (pan_map - synthetic)[None, :, :]).astype(jnp.bfloat16)


def reference(pan_blocks, ms_blocks, send_list, tile_list, row_grid, col_grid, band_mix, band_gain, synth_weight):
    devices = N_MROW * N_MCOL
    partition_total = 2 * SBD
    capacity = partition_total // N_MROW
    node_count = TR // GRID + 1
    coarse_rows = TR // 4
    coarse_cols = TC // 4
    block_ids = jnp.arange(devices * SBD, dtype=jnp.int32)
    sender = block_ids // SBD
    partition_number = send_list[0]
    target = ((partition_number // capacity) * N_MCOL + sender % N_MCOL) * partition_total + (sender // N_MCOL) * capacity + partition_number % capacity
    receive = jnp.zeros((devices * partition_total,), jnp.int32).at[target].set(block_ids)

    def one_tile(device):
        row_band = device // N_MCOL
        horizontal_location = device % N_MCOL
        slot_index = lax.dynamic_slice_in_dim(receive, device * partition_total, partition_total)
        tile_lists = lax.dynamic_slice_in_dim(tile_list, device * partition_total, partition_total, 1)
        is_valid = tile_lists[0].astype(jnp.float32)
        cell_rows = tile_lists[1]
        cell_cols = tile_lists[2]
        pan_data = jnp.take(pan_blocks, slot_index, axis=0).astype(jnp.float32)
        ms_data = jnp.take(ms_blocks, slot_index, axis=0).astype(jnp.float32).reshape(partition_total, MB, BANDS, MB)
        row_nodes = lax.dynamic_slice_in_dim(row_grid, row_band * node_count, node_count)
        col_nodes = lax.dynamic_index_in_dim(col_grid, row_band, 0, False)
        map_rows = jnp.arange(TR, dtype=jnp.int32)
        map_cols = horizontal_location * TC + jnp.arange(TC, dtype=jnp.int32)
        y_pan = along_nodes(row_nodes, map_rows, 0.0, GRID)
        x_pan = along_nodes(col_nodes, map_cols, 0.0, GRID)
        y_ms = (along_nodes(row_nodes, 4 * jnp.arange(coarse_rows, dtype=jnp.int32) + 1, 0.5, GRID) - 1.5) * 0.25
        x_ms = (along_nodes(col_nodes, horizontal_location * TC + 4 * jnp.arange(coarse_cols, dtype=jnp.int32) + 1, 0.5, GRID) - 1.5) * 0.25
        col_weight = source_weights(x_pan[None, :], cell_cols, BS)
        pan_cols = jnp.einsum("sij,scj->sic", pan_data, col_weight.astype(jnp.float32), precision=highest).astype(jnp.bfloat16)
        row_weight = row_weights(y_pan, cell_rows, is_valid, BS)
        pan_map = jnp.dot(row_weight.reshape(TR, partition_total * BS), pan_cols.reshape(partition_total * BS, TC), preferred_element_type=jnp.float32)
        ms_col_weight = source_weights(x_ms[None, :], cell_cols, MB)
        ms_cols = jnp.einsum("sibj,scj->sibc", ms_data, ms_col_weight.astype(jnp.float32), precision=highest).astype(jnp.bfloat16)
        ms_row_weight = row_weights(y_ms, cell_rows, is_valid, MB)
        ms_map = jnp.dot(ms_row_weight.reshape(coarse_rows, partition_total * MB), ms_cols.reshape(partition_total * MB, BANDS * coarse_cols), preferred_element_type=jnp.float32).astype(jnp.bfloat16)
        return pan_map, ms_map.reshape(coarse_rows, BANDS, coarse_cols)

    pan_maps, ms_maps = lax.map(one_tile, jnp.arange(devices, dtype=jnp.int32))
    strip_map = ms_maps.reshape(N_MROW, N_MCOL, coarse_rows, BANDS, coarse_cols).transpose(0, 2, 3, 1, 4).reshape(N_MROW * coarse_rows, BANDS, N_MCOL * coarse_cols)
    padded = jnp.pad(strip_map, ((2, 2), (0, 0), (2, 2)))
    up_rows = upsample_table(TR, coarse_rows)
    up_cols = upsample_table(TC, coarse_cols)

    def sharpen(device):
        row_band = device // N_MCOL
        horizontal_location = device % N_MCOL
        window = lax.dynamic_slice(padded, (row_band * coarse_rows, jnp.zeros((), jnp.int32), horizontal_location * coarse_cols), (coarse_rows + 4, BANDS, coarse_cols + 4))
        across = jnp.einsum("mbn,cn->mbc", window.astype(jnp.float32), up_cols.astype(jnp.float32), precision=highest).astype(jnp.bfloat16)
        upsampled = jnp.dot(up_rows, across.reshape(coarse_rows + 4, BANDS * TC), preferred_element_type=jnp.float32).reshape(TR, BANDS, TC)
        pan_map = lax.dynamic_index_in_dim(pan_maps, device, 0, False)
        return combine(upsampled, pan_map, band_mix, band_gain, synth_weight)

    tiles = lax.map(sharpen, jnp.arange(devices, dtype=jnp.int32))
    return tiles.reshape(N_MROW, N_MCOL, BANDS, TR, TC).transpose(2, 0, 3, 1, 4).reshape(BANDS, NR, NC)
```

```python
import functools

import jax
import jax.numpy as jnp
from jax import lax
from jax.experimental import pallas as pl
from jax.experimental.pallas import tpu as pltpu
from jax.sharding import PartitionSpec as P

GRID = 64
TR = 128
TC = 512
KR = 2
KC = 5
LANES = 128
PACK = 16
HALVES = 2
MESH = pl.DeviceIdType.MESH
F32 = jnp.float32
BF16 = jnp.bfloat16
I32 = jnp.int32


def cubic_weight(offset):
    outer = jnp.maximum(2.0 - jnp.abs(offset), 0.0)
    shifted = outer - 1.0
    inner = jnp.maximum(shifted, 0.0)
    return outer * outer * (0.5 * shifted) + inner * inner * (1.0 - 2.0 * inner)


def iota(shape, dim):
    return lax.broadcasted_iota(I32, shape, dim)


def row_coord(nodes, position, offset):
    first = position < GRID
    a = jnp.where(first, nodes[0:1, 0:1], nodes[0:1, 1:2])
    b = jnp.where(first, nodes[0:1, 1:2], nodes[0:1, 2:3])
    within = (jnp.where(first, position, position - GRID).astype(F32) + offset) / GRID
    return a + (b - a) * within


def col_coord(nodes, after, is_last, count, position, offset):
    segment = position // GRID
    coord = jnp.zeros(position.shape, F32)
    for s in range(count):
        left, shift = nodes[1:2, s : s + 1], s * GRID
        if s + 1 < count:
            right = nodes[1:2, s + 1 : s + 2]
        else:
            right = jnp.where(is_last, left, after)
            left = jnp.where(is_last, nodes[1:2, s - 1 : s], left)
            shift = jnp.where(is_last, shift - GRID, shift)
        within = ((position - shift).astype(F32) + offset) / GRID
        coord = jnp.where(segment == s, left + (right - left) * within, coord)
    return coord


def mapping(
    capacity,
    col_nodes,
    send_ref,
    row_ref,
    col_ref,
    pan_hbm,
    ms_hbm,
    mix_ref,
    gain_ref,
    synth_ref,
    out_ref,
    pan_ref,
    ms_ref,
    pan_sum,
    ms_sum,
    table_ref,
    table,
    nodes_ref,
    nodes_all,
    ms_y_send,
    ms_y_recv,
    pan_y_send,
    pan_y_recv,
    ms_z_send,
    ms_z_recv,
    pan_z_send,
    pan_z_recv,
    ms_total,
    pan_total,
    col_weight,
    ms_col_weight,
    window,
    beside,
    up_cols,
    up_rows,
    mixed,
    load_sem,
    nodes_ss,
    nodes_rs,
    ms_y_ss,
    ms_y_rs,
    pan_y_ss,
    pan_y_rs,
    ms_z_ss,
    ms_z_rs,
    pan_z_ss,
    pan_z_rs,
    halo_ss,
    halo_rs,
):
    n = lax.axis_size("mrow")
    lines = n // 2
    blocks = lines // 2
    scene = lax.axis_index("scene")
    m = lax.axis_index("mrow")
    c = lax.axis_index("mcol")
    z, y = m // 2, m % 2
    twin = z * 2 + (1 - y)
    other = 1 - c
    pair = z // 2
    partner = pair * 2 + (1 - z % 2)
    own_blocks, size, _ = pan_ref.shape
    _, coarse_size, coarse_width = ms_ref.shape
    cells = n * KR * KC
    bands = mixed.shape[0]
    coarse_rows = TR // 4
    coarse_cols = TC // 4
    half = coarse_rows // 2
    mid = half + coarse_rows
    part_rows = TR // HALVES
    first_col = c * KC
    is_last = c == lax.axis_size("mcol") - 1

    def at(row, col):
        return (scene, row, col)

    def remote(src, dst, ss, rs, row, col):
        return pltpu.make_async_remote_copy(
            src_ref=src,
            dst_ref=dst,
            send_sem=ss,
            recv_sem=rs,
            device_id=at(row, col),
            device_id_type=MESH,
        )

    barrier = pltpu.get_barrier_semaphore()

    def greet(k, carry):
        row = lax.rem(m + k, n)
        pl.semaphore_signal(barrier, inc=1, device_id=at(row, c), device_id_type=MESH)
        pl.semaphore_signal(barrier, inc=1, device_id=at(row, other), device_id_type=MESH)
        return carry

    pl.semaphore_signal(barrier, inc=1, device_id=at(m, other), device_id_type=MESH)
    lax.fori_loop(1, n, greet, 0)
    ms_load = pltpu.make_async_copy(ms_hbm, ms_ref, load_sem.at[0])
    pan_load = pltpu.make_async_copy(pan_hbm, pan_ref, load_sem.at[1])
    ms_load.start()
    pan_load.start()

    nodes_ref[...] = jnp.zeros_like(nodes_ref)
    nodes_ref[0:1, 0 : row_ref.shape[1]] = row_ref[...]
    nodes_ref[1:2, 0 : col_ref.shape[1]] = col_ref[...]
    nodes_all[c, m] = nodes_ref[...]

    square = (own_blocks, own_blocks)
    wide = (own_blocks, LANES)
    owner = send_ref[0:1, :] // capacity
    key_row = (owner * KR + send_ref[1:2, :]) * KC + send_ref[2:3, :] - first_col
    key_row = jnp.broadcast_to(key_row, square)
    diagonal = iota(square, 0) == iota(square, 1)
    key_col = jnp.sum(jnp.where(diagonal, key_row, 0), axis=1, keepdims=True)
    same = key_row == key_col
    before = (key_row < key_col) | (same & (iota(square, 1) < iota(square, 0)))
    rank = jnp.sum(jnp.where(before, 1, 0), axis=1, keepdims=True)
    joined = jnp.sum(jnp.where(before & same, 1, 0), axis=1, keepdims=True)
    hit = rank == iota(wide, 1)
    order = jnp.sum(jnp.where(hit, iota(wide, 0), 0), axis=0, keepdims=True)
    keep = jnp.sum(jnp.where(hit & (joined > 0), 1, 0), axis=0, keepdims=True)
    table_ref[0:1, :] = order
    table_ref[1:2, :] = keep
    for g in range(pl.cdiv(cells, LANES)):
        cell = iota(wide, 1) + g * LANES
        ends = jnp.sum(jnp.where(key_col <= cell, 1, 0), axis=0, keepdims=True)
        count = jnp.sum(jnp.where(key_col == cell, 1, 0), axis=0, keepdims=True)
        table_ref[2 + g : 3 + g, :] = jnp.where(count > 0, ends, 0)
    table_copy = pltpu.make_async_copy(table_ref, table, load_sem.at[2])
    table_copy.start()

    tap = iota((TR, 2 * coarse_rows), 1) - (half - 2)
    spot = (iota((TR, 2 * coarse_rows), 0).astype(F32) - 1.5) * 0.25 + 2.0
    up_rows[...] = cubic_weight(spot - tap.astype(F32)).astype(BF16)
    ms_col_weight[...] = jnp.zeros_like(ms_col_weight)
    pan_sum[0] = jnp.zeros((size, size), BF16)
    ms_sum[0] = jnp.zeros((coarse_size, coarse_width), BF16)
    pl.semaphore_wait(barrier, 2 * n - 1)

    def nodes_copy(slot_row, slot_col, row, col):
        return remote(
            nodes_ref,
            nodes_all.at[slot_col, slot_row],
            nodes_ss.at[col, row],
            nodes_rs.at[slot_col, slot_row],
            row,
            col,
        )

    def send_nodes(k, carry):
        row = lax.rem(m + k, n)
        nodes_copy(m, c, row, c).start()
        nodes_copy(m, c, row, other).start()
        return carry

    lax.fori_loop(1, n, send_nodes, 0)
    nodes_copy(m, c, m, other).start()
    table_copy.wait()

    def running(source, sums):
        def step(p, total):
            total = total * table[1, p].astype(F32) + source[table[0, p]].astype(F32)
            sums[p + 1] = total.astype(BF16)
            return total

        start = jnp.zeros(source.shape[1:], F32)
        lax.fori_loop(0, own_blocks, step, start, unroll=2)

    ms_load.wait()
    running(ms_ref, ms_sum)
    pan_load.wait()
    running(pan_ref, pan_sum)

    def wait_nodes(k, carry):
        row = lax.rem(m + k, n)
        nodes_copy(row, c, row, c).wait()
        nodes_copy(row, other, row, other).wait()
        return carry

    lax.fori_loop(1, n, wait_nodes, 0)
    nodes_copy(m, other, m, other).wait()

    def cell_of(sums, tile, row, col):
        cell = (tile * KR + row) * KC + col
        return sums[table[2 + cell // LANES, cell % LANES]]

    def stacked(sums, tile, col):
        return jnp.concatenate([cell_of(sums, tile, row, col) for row in range(KR)], axis=0)

    def ms_part(tile):
        nodes = nodes_all[c, tile]
        after = nodes_all[1, tile][1:2, 0:1]
        x_ms = col_coord(
            nodes, after, is_last, col_nodes, 4 * iota((1, coarse_cols), 1) + 1, 0.5
        )
        x_ms = (x_ms - 1.5) * 0.25
        for k in range(KC):
            pixel = (first_col + k) * coarse_size + iota((coarse_size, coarse_cols), 0)
            weight = cubic_weight(x_ms - pixel.astype(F32)).astype(BF16)
            for b in range(bands):
                row = (k * bands + b) * coarse_size
                lanes = slice(b * coarse_cols, (b + 1) * coarse_cols)
                ms_col_weight[row : row + coarse_size, lanes] = weight
        spots = (row_coord(nodes, 4 * iota((coarse_rows, 1), 0) + 1, 0.5) - 1.5) * 0.25
        taps = iota((coarse_rows, KR * coarse_size), 1).astype(F32)
        weight = cubic_weight(spots - taps).astype(BF16)
        rows = [
            jnp.dot(weight, stacked(ms_sum, tile, k), preferred_element_type=F32).astype(BF16)
            for k in range(KC)
        ]
        return jnp.dot(
            jnp.concatenate(rows, axis=1), ms_col_weight[...], preferred_element_type=F32
        )

    def pan_part(tile):
        nodes = nodes_all[c, tile]
        after = nodes_all[1, tile][1:2, 0:1]
        x_pan = col_coord(nodes, after, is_last, col_nodes, iota((1, TC), 1), 0.0)
        base = jnp.floor(x_pan)
        taps = [
            jnp.broadcast_to(cubic_weight(x_pan - (base + float(t))), (PACK, TC)).astype(BF16)
            for t in range(-1, 3)
        ]
        none = jnp.zeros((PACK, TC), BF16)
        for k in range(KC):
            origin = ((first_col + k) * size).astype(F32)
            begin = jnp.clip(base - origin, -4.0, size + 3.0)
            away = (iota((PACK, TC), 0).astype(F32) - begin).astype(BF16)
            for g in range(size // PACK):
                value = none
                for t in range(4):
                    value = jnp.where(away == BF16(t - 1 - g * PACK), taps[t], value)
                row = k * size + g * PACK
                col_weight[row : row + PACK, :] = value
        spots = row_coord(nodes, iota((TR, 1), 0), 0.0)
        pixels = iota((TR, KR * size), 1).astype(F32)
        weight = cubic_weight(spots - pixels).astype(BF16)
        rows = [
            jnp.dot(weight, stacked(pan_sum, tile, k), preferred_element_type=F32).astype(BF16)
            for k in range(KC)
        ]
        return jnp.dot(jnp.concatenate(rows, axis=1), col_weight[...], preferred_element_type=F32)

    def line_of(k):
        up = lax.rem(pair * 2 + 2 + k, lines)
        down = lax.rem(pair * 2 + lines - 1 - k, lines)
        far = jnp.where(pair % 2 == 0, down, up)
        return jnp.where(k < lines - 2, far, jnp.where(k == lines - 2, partner, z))

    def ms_y(k):
        return remote(ms_y_send.at[k], ms_y_recv.at[k], ms_y_ss.at[k], ms_y_rs.at[k], twin, c)

    def pan_y(k, h):
        part = pl.ds(h * part_rows, part_rows)
        return remote(
            pan_y_send.at[k, part],
            pan_y_recv.at[k, part],
            pan_y_ss.at[k, h],
            pan_y_rs.at[k, h],
            twin,
            c,
        )

    def route(line):
        far = line // 2 != pair
        above = line // 2 > pair
        lower = z % 2 == 0
        inner = far & jnp.logical_xor(above, lower)
        outer = far & jnp.logical_not(jnp.logical_xor(above, lower))
        target = jnp.where(outer, partner, line)
        slot = jnp.where(outer, blocks + line, pair)
        return inner, target * 2 + y, slot

    def ms_z(k, row, slot):
        return remote(
            ms_z_send.at[k], ms_z_recv.at[slot], ms_z_ss.at[k], ms_z_rs.at[slot], row, c
        )

    def pan_z(k, h, row, slot):
        part = pl.ds(h * part_rows, part_rows)
        return remote(
            pan_z_send.at[k, part],
            pan_z_recv.at[slot, part],
            pan_z_ss.at[k, h],
            pan_z_rs.at[slot, h],
            row,
            c,
        )

    def each(first, last, step):
        def body(k, carry):
            step(k, line_of(k))
            return carry

        lax.fori_loop(first, last, body, 0)

    def ms_to_twin(k, line):
        ms_y_send[k] = ms_part(line * 2 + 1 - y).astype(BF16)
        ms_y(k).start()

    def pan_to_twin(k, line):
        pan_y_send[k] = pan_part(line * 2 + 1 - y).astype(BF16)
        for h in range(HALVES):
            pan_y(k, h).start()

    def ms_onward(k, line):
        inner, row, slot = route(line)
        ms_total[...] = ms_part(line * 2 + y)
        ms_y(k).wait_recv()
        ms_total[...] += ms_y_recv[k].astype(F32)

        @pl.when(inner)
        def _():
            ms_z(0, row, blocks + line).wait_recv()
            ms_total[...] += ms_z_recv[blocks + line].astype(F32)

        ms_z_send[k] = ms_total[...].astype(BF16)
        ms_z(k, row, slot).start()

    def pan_onward(k, line):
        inner, row, slot = route(line)
        pan_total[...] = pan_part(line * 2 + y)
        for h in range(HALVES):
            rows = slice(h * part_rows, (h + 1) * part_rows)
            pan_y(k, h).wait_recv()
            pan_total[rows, :] += pan_y_recv[k, rows].astype(F32)

            @pl.when(inner)
            def _():
                pan_z(0, h, row, blocks + line).wait_recv()
                pan_total[rows, :] += pan_z_recv[blocks + line, rows].astype(F32)

            pan_z_send[k, rows] = pan_total[rows, :].astype(BF16)
            pan_z(k, h, row, slot).start()

    each(0, lines, ms_to_twin)
    each(0, 2, pan_to_twin)
    each(0, lines - 1, ms_onward)
    each(2, lines, pan_to_twin)

    spot = (iota((coarse_cols, TC), 1).astype(F32) - 1.5) * 0.25 + 2.0
    tap = iota((coarse_cols, TC), 0) + 2
    up_cols[0:coarse_cols, :] = cubic_weight(spot - tap.astype(F32)).astype(BF16)
    tap = tap + jnp.where(c == 0, coarse_cols, -coarse_cols)
    up_cols[coarse_cols : 2 * coarse_cols, :] = cubic_weight(spot - tap.astype(F32)).astype(BF16)

    each(0, 1, pan_onward)

    ms_total[...] = ms_part(m)
    ms_y(lines - 1).wait_recv()
    ms_total[...] += ms_y_recv[lines - 1].astype(F32)

    def ms_arrived(slot, carry):
        ms_z(0, m, slot).wait_recv()
        ms_total[...] += ms_z_recv[slot].astype(F32)
        return carry

    lax.fori_loop(0, blocks, ms_arrived, 0)
    values = [ms_total[:, b * coarse_cols : (b + 1) * coarse_cols] for b in range(bands)]
    synthetic = sum(synth_ref[b] * values[b] for b in range(bands))
    for b in range(bands):
        result = values[b] - gain_ref[b] * synthetic
        for k in range(bands):
            result = result + mix_ref[b, k] * values[k]
        window[half:mid, b * coarse_cols : (b + 1) * coarse_cols] = result.astype(BF16)

    has_above, has_below = m > 0, m < n - 1

    def halo_copy(k, src, rows, dst, start, row, col):
        return remote(
            window.at[pl.ds(src, rows)],
            dst.at[pl.ds(start, rows)],
            halo_ss.at[k],
            halo_rs.at[k],
            row,
            col,
        )

    across_copy = halo_copy(0, half, coarse_rows, beside, half, m, other)
    up_copies = [
        halo_copy(1, half, half, window, mid, m - 1, c),
        halo_copy(2, half, half, beside, mid, m - 1, other),
    ]
    down_copies = [
        halo_copy(3, coarse_rows, half, window, 0, m + 1, c),
        halo_copy(4, coarse_rows, half, beside, 0, m + 1, other),
    ]
    across_copy.start()

    @pl.when(has_above)
    def _():
        for copy in up_copies:
            copy.start()

    @pl.when(has_below)
    def _():
        for copy in down_copies:
            copy.start()

    each(1, lines - 1, pan_onward)
    pan_total[...] = pan_part(m)
    across_copy.wait()

    @pl.when(has_above)
    def _():
        for copy in up_copies:
            copy.wait_send()
        for copy in down_copies:
            copy.wait_recv()

    @pl.when(has_below)
    def _():
        for copy in down_copies:
            copy.wait_send()
        for copy in up_copies:
            copy.wait_recv()

    edge = jnp.zeros((half, window.shape[1]), BF16)

    @pl.when(jnp.logical_not(has_above))
    def _():
        window[0:half, :] = edge
        beside[0:half, :] = edge

    @pl.when(jnp.logical_not(has_below))
    def _():
        window[mid : mid + half, :] = edge
        beside[mid : mid + half, :] = edge

    for b in range(bands):
        lanes = slice(b * coarse_cols, (b + 1) * coarse_cols)
        source = jnp.concatenate([window[:, lanes], beside[:, lanes]], axis=1)
        across = jnp.dot(source, up_cols[...], preferred_element_type=F32)
        mixed[b] = jnp.dot(up_rows[...], across.astype(BF16), preferred_element_type=F32)

    for h in range(HALVES):
        rows = slice(h * part_rows, (h + 1) * part_rows)
        pan_y(lines - 1, h).wait_recv()
        pan_total[rows, :] += pan_y_recv[lines - 1, rows].astype(F32)

        def pan_arrived(slot, carry):
            pan_z(0, h, m, slot).wait_recv()
            pan_total[rows, :] += pan_z_recv[slot, rows].astype(F32)
            return carry

        lax.fori_loop(0, blocks, pan_arrived, 0)
        for b in range(bands):
            out_ref[b, rows, :] = (mixed[b, rows, :] + gain_ref[b] * pan_total[rows, :]).astype(
                BF16
            )

    def y_sent(k, carry):
        ms_y(k).wait_send()
        for h in range(HALVES):
            pan_y(k, h).wait_send()
        return carry

    def z_sent(k, carry):
        ms_z(k, m, 0).wait_send()
        for h in range(HALVES):
            pan_z(k, h, m, 0).wait_send()
        return carry

    lax.fori_loop(0, lines, y_sent, 0)
    lax.fori_loop(0, lines - 1, z_sent, 0)


def local(
    pan_blocks,
    ms_blocks,
    send_list,
    tile_list,
    row_grid,
    col_grid,
    band_mix,
    band_gain,
    synth_weight,
):
    n = lax.axis_size("mrow")
    lines = n // 2
    own_blocks, size, _ = pan_blocks.shape
    _, coarse_size, coarse_width = ms_blocks.shape
    capacity = tile_list.shape[1] // n
    bands = band_gain.shape[0]
    coarse_rows, coarse_cols = TR // 4, TC // 4
    ms_width = bands * coarse_cols
    table_rows = pl.cdiv(2 + pl.cdiv(n * KR * KC, LANES), 8) * 8
    smem = pl.BlockSpec(memory_space=pltpu.SMEM)
    vmem = pl.BlockSpec(memory_space=pltpu.VMEM)
    hbm = pl.BlockSpec(memory_space=pl.ANY)
    dma = pltpu.SemaphoreType.DMA
    slots = lines // 2 + lines

    def ms_slots(count):
        return pltpu.VMEM((count, coarse_rows, ms_width), BF16)

    def pan_slots(count):
        return pltpu.VMEM((count, TR, TC), BF16)

    return pl.pallas_call(
        functools.partial(mapping, capacity, col_grid.shape[1]),
        out_shape=jax.ShapeDtypeStruct((bands, TR, TC), BF16),
        in_specs=[vmem, vmem, vmem, hbm, hbm, smem, smem, smem],
        out_specs=vmem,
        scratch_shapes=[
            pltpu.VMEM(pan_blocks.shape, BF16),
            pltpu.VMEM(ms_blocks.shape, BF16),
            pltpu.VMEM((own_blocks + 1, size, size), BF16),
            pltpu.VMEM((own_blocks + 1, coarse_size, coarse_width), BF16),
            pltpu.VMEM((table_rows, LANES), I32),
            pltpu.SMEM((table_rows, LANES), I32),
            pltpu.VMEM((8, LANES), F32),
            pltpu.VMEM((2, n, 8, LANES), F32),
            ms_slots(lines),
            ms_slots(lines),
            pan_slots(lines),
            pan_slots(lines),
            ms_slots(lines - 1),
            ms_slots(slots),
            pan_slots(lines - 1),
            pan_slots(slots),
            pltpu.VMEM((coarse_rows, ms_width), F32),
            pltpu.VMEM((TR, TC), F32),
            pltpu.VMEM((KC * size, TC), BF16),
            pltpu.VMEM((KC * bands * coarse_size, ms_width), BF16),
            pltpu.VMEM((2 * coarse_rows, ms_width), BF16),
            pltpu.VMEM((2 * coarse_rows, ms_width), BF16),
            pltpu.VMEM((2 * coarse_cols, TC), BF16),
            pltpu.VMEM((TR, 2 * coarse_rows), BF16),
            pltpu.VMEM((bands, TR, TC), F32),
            dma((3,)),
            dma((2, n)),
            dma((2, n)),
            dma((lines,)),
            dma((lines,)),
            dma((lines, HALVES)),
            dma((lines, HALVES)),
            dma((lines - 1,)),
            dma((slots,)),
            dma((lines - 1, HALVES)),
            dma((slots, HALVES)),
            dma((5,)),
            dma((5,)),
        ],
        compiler_params=pltpu.CompilerParams(
            collective_id=0, has_side_effects=True, vmem_limit_bytes=40 * 1024 * 1024
        ),
        name="mapping",
    )(
        send_list,
        row_grid[None, :],
        col_grid,
        pan_blocks,
        ms_blocks,
        band_mix,
        band_gain,
        synth_weight,
    )


def solution(mesh):
    return jax.shard_map(
        local,
        mesh=mesh,
        in_specs=(
            P(("scene", "mrow", "mcol"), None, None),
            P(("scene", "mrow", "mcol"), None, None),
            P(None, ("scene", "mrow", "mcol")),
            P(None, ("scene", "mrow", "mcol")),
            P(("scene", "mrow")),
            P(("scene", "mrow"), "mcol"),
            P(),
            P(),
            P(),
        ),
        out_specs=P(None, ("scene", "mrow"), "mcol"),
        check_vma=False,
    )
```

```python
import functools

import jax
import jax.numpy as jnp
from jax import lax
from jax.experimental import pallas as pl
from jax.experimental.pallas import tpu as pltpu
from jax.sharding import PartitionSpec as P

GRID = 64
TR = 128
TC = 512
KR = 2
KC = 5
LANES = 128
PACK = 16
HALVES = 2
GROUP = 4
MESH = pl.DeviceIdType.MESH
F32 = jnp.float32
BF16 = jnp.bfloat16
I32 = jnp.int32


def cubic_weight(offset):
    outer = jnp.maximum(2.0 - jnp.abs(offset), 0.0)
    shifted = outer - 1.0
    inner = jnp.maximum(shifted, 0.0)
    return outer * outer * (0.5 * shifted) + inner * inner * (1.0 - 2.0 * inner)


def iota(shape, dim):
    return lax.broadcasted_iota(I32, shape, dim)


def row_coord(nodes, position, offset):
    first = position < GRID
    a = jnp.where(first, nodes[0:1, 0:1], nodes[0:1, 1:2])
    b = jnp.where(first, nodes[0:1, 1:2], nodes[0:1, 2:3])
    within = (jnp.where(first, position, position - GRID).astype(F32) + offset) / GRID
    return a + (b - a) * within


def col_coord(nodes, after, is_last, count, position, offset):
    segment = position // GRID
    coord = jnp.zeros(position.shape, F32)
    for s in range(count):
        left, shift = nodes[1:2, s : s + 1], s * GRID
        if s + 1 < count:
            right = nodes[1:2, s + 1 : s + 2]
        else:
            right = jnp.where(is_last, left, after)
            left = jnp.where(is_last, nodes[1:2, s - 1 : s], left)
            shift = jnp.where(is_last, shift - GRID, shift)
        within = ((position - shift).astype(F32) + offset) / GRID
        coord = jnp.where(segment == s, left + (right - left) * within, coord)
    return coord


def spread(x, origin, size):
    base = jnp.floor(x)
    shape = (PACK, x.shape[1])
    taps = [
        jnp.broadcast_to(cubic_weight(x - (base + t)), shape).astype(BF16)
        for t in (-1.0, 0.0, 1.0, 2.0)
    ]
    groups = size // PACK
    first = base - 1.0 - origin
    group = jnp.floor(first * (1.0 / PACK))
    away = (iota(shape, 0).astype(F32) - (first - group * PACK)).astype(BF16)
    group = jnp.broadcast_to(jnp.clip(group, -2.0, groups + 1.0), shape).astype(BF16)
    none = jnp.zeros(shape, BF16)
    low, high = none, none
    for t in range(4):
        low = jnp.where(away == BF16(t), taps[t], low)
        high = jnp.where(away == BF16(t - PACK), taps[t], high)
    here = [group == BF16(g) for g in range(-1, groups)]
    return jnp.concatenate(
        [jnp.where(here[g + 1], low, jnp.where(here[g], high, none)) for g in range(groups)],
        axis=0,
    )


def mapping(
    capacity,
    col_nodes,
    send_hbm,
    row_hbm,
    col_hbm,
    pan_hbm,
    ms_hbm,
    mix_hbm,
    gain_hbm,
    synth_hbm,
    mixed_hbm,
    pan_total,
    send_ref,
    row_ref,
    col_ref,
    mix_ref,
    gain_ref,
    synth_ref,
    pan_ref,
    ms_ref,
    pan_sum,
    ms_sum,
    table_ref,
    table,
    nodes_ref,
    nodes_all,
    ms_y_send,
    ms_y_recv,
    pan_y_send,
    pan_y_recv,
    ms_z_send,
    ms_z_recv,
    pan_z_send,
    pan_z_recv,
    ms_total,
    window,
    edge_own,
    edge_all,
    up_cols,
    up_rows,
    mixed,
    load_sem,
    nodes_ss,
    nodes_rs,
    ms_y_ss,
    ms_y_rs,
    pan_y_ss,
    pan_y_rs,
    ms_z_ss,
    ms_z_rs,
    pan_z_ss,
    pan_z_rs,
    halo_ss,
    halo_rs,
):
    n = lax.axis_size("mrow")
    lines = n // 2
    blocks = lines // 2
    scene = lax.axis_index("scene")
    m = lax.axis_index("mrow")
    c = lax.axis_index("mcol")
    z, y = m // 2, m % 2
    twin = z * 2 + (1 - y)
    other = 1 - c
    pair = z // 2
    partner = pair * 2 + (1 - z % 2)
    own_blocks, size, _ = pan_ref.shape
    _, coarse_size, coarse_width = ms_ref.shape
    cells = n * KR * KC
    bands = mixed.shape[0]
    coarse_rows = TR // 4
    coarse_cols = TC // 4
    half = coarse_rows // 2
    mid = half + coarse_rows
    part_rows = TR // HALVES
    first_col = c * KC
    is_last = c == lax.axis_size("mcol") - 1

    def at(row, col):
        return (scene, row, col)

    def remote(src, dst, ss, rs, row, col):
        return pltpu.make_async_remote_copy(
            src_ref=src,
            dst_ref=dst,
            send_sem=ss,
            recv_sem=rs,
            device_id=at(row, col),
            device_id_type=MESH,
        )

    barrier = pltpu.get_barrier_semaphore()

    def greet(k, carry):
        row = lax.rem(m + k, n)
        pl.semaphore_signal(barrier, inc=1, device_id=at(row, c), device_id_type=MESH)
        pl.semaphore_signal(barrier, inc=1, device_id=at(row, other), device_id_type=MESH)
        return carry

    pl.semaphore_signal(barrier, inc=1, device_id=at(m, other), device_id_type=MESH)
    lax.fori_loop(1, n, greet, 0)
    loads = [
        pltpu.make_async_copy(src, dst, load_sem.at[k])
        for k, (src, dst) in enumerate(
            (
                (row_hbm, row_ref),
                (col_hbm, col_ref),
                (send_hbm, send_ref),
                (ms_hbm, ms_ref),
                (pan_hbm, pan_ref),
                (mix_hbm, mix_ref),
                (gain_hbm, gain_ref),
                (synth_hbm, synth_ref),
            )
        )
    ]
    for load in loads:
        load.start()
    row_load, col_load, send_load, ms_load, pan_load, *late_loads = loads

    nodes_ref[...] = jnp.zeros_like(nodes_ref)
    row_load.wait()
    col_load.wait()
    nodes_ref[0:1, 0 : row_ref.shape[1]] = row_ref[...]
    nodes_ref[1:2, 0 : col_ref.shape[1]] = col_ref[...]
    nodes_all[c, m] = nodes_ref[...]
    pl.semaphore_wait(barrier, 2 * n - 1)

    def nodes_copy(slot_row, slot_col, row, col):
        return remote(
            nodes_ref,
            nodes_all.at[slot_col, slot_row],
            nodes_ss.at[col, row],
            nodes_rs.at[slot_col, slot_row],
            row,
            col,
        )

    def send_nodes(k, carry):
        row = lax.rem(m + k, n)
        nodes_copy(m, c, row, c).start()
        nodes_copy(m, c, row, other).start()
        return carry

    lax.fori_loop(1, n, send_nodes, 0)
    nodes_copy(m, c, m, other).start()
    send_load.wait()

    square = (own_blocks, own_blocks)
    wide = (own_blocks, LANES)
    owner = send_ref[0:1, :] // capacity
    key_row = (owner * KR + send_ref[1:2, :]) * KC + send_ref[2:3, :] - first_col
    key_row = jnp.broadcast_to(key_row, square)
    diagonal = iota(square, 0) == iota(square, 1)
    key_col = jnp.sum(jnp.where(diagonal, key_row, 0), axis=1, keepdims=True)
    same = key_row == key_col
    before = (key_row < key_col) | (same & (iota(square, 1) < iota(square, 0)))
    rank = jnp.sum(jnp.where(before, 1, 0), axis=1, keepdims=True)
    joined = jnp.sum(jnp.where(before & same, 1, 0), axis=1, keepdims=True)
    hit = rank == iota(wide, 1)
    order = jnp.sum(jnp.where(hit, iota(wide, 0), 0), axis=0, keepdims=True)
    keep = jnp.sum(jnp.where(hit & (joined > 0), 1, 0), axis=0, keepdims=True)
    table_ref[0:1, :] = order
    table_ref[1:2, :] = keep
    for g in range(pl.cdiv(cells, LANES)):
        cell = iota(wide, 1) + g * LANES
        ends = jnp.sum(jnp.where(key_col <= cell, 1, 0), axis=0, keepdims=True)
        count = jnp.sum(jnp.where(key_col == cell, 1, 0), axis=0, keepdims=True)
        table_ref[2 + g : 3 + g, :] = jnp.where(count > 0, ends, 0)
    table_copy = pltpu.make_async_copy(table_ref, table, load_sem.at[8])
    table_copy.start()

    tap = iota((TR, 2 * coarse_rows), 1) - (half - 2)
    spot = (iota((TR, 2 * coarse_rows), 0).astype(F32) - 1.5) * 0.25 + 2.0
    up_rows[...] = cubic_weight(spot - tap.astype(F32)).astype(BF16)
    pan_sum[0] = jnp.zeros((size, size), BF16)
    ms_sum[0] = jnp.zeros((coarse_size, coarse_width), BF16)
    table_copy.wait()

    def running(source, sums):
        def step(p, total):
            total = total * table[1, p].astype(F32) + source[table[0, p]].astype(F32)
            sums[p + 1] = total.astype(BF16)
            return total

        start = jnp.zeros(source.shape[1:], F32)
        lax.fori_loop(0, own_blocks, step, start, unroll=2)

    ms_load.wait()
    running(ms_ref, ms_sum)
    pan_load.wait()
    running(pan_ref, pan_sum)

    def wait_nodes(k, carry):
        row = lax.rem(m + k, n)
        nodes_copy(row, c, row, c).wait()
        nodes_copy(row, other, row, other).wait()
        return carry

    lax.fori_loop(1, n, wait_nodes, 0)
    nodes_copy(m, other, m, other).wait()

    def cell_of(sums, tile, row, col):
        cell = (tile * KR + row) * KC + col
        return sums[table[2 + cell // LANES, cell % LANES]]

    def stacked(sums, tile, col):
        return jnp.concatenate([cell_of(sums, tile, row, col) for row in range(KR)], axis=0)

    def ms_part(tile):
        nodes = nodes_all[c, tile]
        after = nodes_all[1, tile][1:2, 0:1]
        x_ms = col_coord(
            nodes, after, is_last, col_nodes, 4 * iota((1, coarse_cols), 1) + 1, 0.5
        )
        x_ms = (x_ms - 1.5) * 0.25
        col = spread(x_ms, (first_col * coarse_size).astype(F32), KC * coarse_size)
        spots = (row_coord(nodes, 4 * iota((coarse_rows, 1), 0) + 1, 0.5) - 1.5) * 0.25
        taps = iota((coarse_rows, KR * coarse_size), 1).astype(F32)
        weight = cubic_weight(spots - taps).astype(BF16)
        rows = [
            jnp.dot(weight, stacked(ms_sum, tile, k), preferred_element_type=F32).astype(BF16)
            for k in range(KC)
        ]
        by_band = [
            jnp.concatenate(
                [row[:, b * coarse_size : (b + 1) * coarse_size] for row in rows], axis=1
            )
            for b in range(bands)
        ]
        return jnp.dot(jnp.concatenate(by_band, axis=0), col, preferred_element_type=F32)

    def pan_part(tile):
        nodes = nodes_all[c, tile]
        after = nodes_all[1, tile][1:2, 0:1]
        x_pan = col_coord(nodes, after, is_last, col_nodes, iota((1, TC), 1), 0.0)
        col = spread(x_pan, (first_col * size).astype(F32), KC * size)
        row = spread(row_coord(nodes, iota((1, TR), 1), 0.0), 0.0, KR * size)
        rows = []
        for k in range(0, KC, 2):
            source = jnp.concatenate(
                [stacked(pan_sum, tile, j) for j in range(k, min(k + 2, KC))], axis=1
            )
            rows.append(
                lax.dot_general(
                    row, source, (((0,), (0,)), ((), ())), preferred_element_type=F32
                ).astype(BF16)
            )
        return jnp.dot(jnp.concatenate(rows, axis=1), col, preferred_element_type=F32)

    def line_of(k):
        up = lax.rem(pair * 2 + 2 + k, lines)
        down = lax.rem(pair * 2 + lines - 1 - k, lines)
        far = jnp.where(pair % 2 == 0, down, up)
        return jnp.where(k < lines - 2, far, jnp.where(k == lines - 2, partner, z))

    def ms_y(k):
        return remote(ms_y_send.at[k], ms_y_recv.at[k], ms_y_ss.at[k], ms_y_rs.at[k], twin, c)

    def pan_y(k, h):
        part = pl.ds(h * part_rows, part_rows)
        return remote(
            pan_y_send.at[k, part],
            pan_y_recv.at[k, part],
            pan_y_ss.at[k, h],
            pan_y_rs.at[k, h],
            twin,
            c,
        )

    def route(line):
        far = line // 2 != pair
        above = line // 2 > pair
        lower = z % 2 == 0
        inner = far & jnp.logical_xor(above, lower)
        outer = far & jnp.logical_not(jnp.logical_xor(above, lower))
        target = jnp.where(outer, partner, line)
        slot = jnp.where(outer, blocks + line, pair)
        return inner, target * 2 + y, slot

    def ms_z(k, row, slot):
        return remote(
            ms_z_send.at[k], ms_z_recv.at[slot], ms_z_ss.at[k], ms_z_rs.at[slot], row, c
        )

    def pan_z(k, h, row, slot):
        part = pl.ds(h * part_rows, part_rows)
        return remote(
            pan_z_send.at[k, part],
            pan_z_recv.at[slot, part],
            pan_z_ss.at[k, h],
            pan_z_rs.at[slot, h],
            row,
            c,
        )

    def each(first, last, step):
        if last - first == 1:
            step(first)
            return

        def body(k, carry):
            step(k)
            return carry

        lax.fori_loop(first, last, body, 0)

    def ms_to_twin(k):
        parts = [ms_part(line_of(k + i) * 2 + 1 - y) for i in range(2)]
        for i, part in enumerate(parts):
            ms_y_send[k + i] = part.astype(BF16)

    def pan_to_twin(k):
        pan_y_send[k] = pan_part(line_of(k) * 2 + 1 - y).astype(BF16)
        for h in range(HALVES):
            pan_y(k, h).start()

    def ms_own_parts(k):
        parts = [ms_part(line_of(k + i) * 2 + y) for i in range(2)]
        for i, part in enumerate(parts):
            ms_total[i] = part

    def ms_onward(k, i):
        line = line_of(k)
        inner, row, slot = route(line)
        ms_y(k).wait_recv()
        ms_total[i] += ms_y_recv[k].astype(F32)

        @pl.when(inner)
        def _():
            ms_z(0, row, blocks + line).wait_recv()
            ms_total[i] += ms_z_recv[blocks + line].astype(F32)

        ms_z_send[k] = ms_total[i].astype(BF16)
        ms_z(k, row, slot).start()

    def pan_onward(k):
        line = line_of(k)
        inner, row, slot = route(line)
        pan_total[...] = pan_part(line * 2 + y)
        for h in range(HALVES):
            rows = slice(h * part_rows, (h + 1) * part_rows)
            pan_y(k, h).wait_recv()
            pan_total[rows, :] += pan_y_recv[k, rows].astype(F32)

            @pl.when(inner)
            def _():
                pan_z(0, h, row, blocks + line).wait_recv()
                pan_total[rows, :] += pan_z_recv[blocks + line, rows].astype(F32)

            pan_z_send[k, rows] = pan_total[rows, :].astype(BF16)
            pan_z(k, h, row, slot).start()

    far = lines - 2

    def ms_far_to_twin(p):
        ms_to_twin(2 * p)
        ms_y(2 * p).start()
        ms_y(2 * p + 1).start()

    def ms_far_onward(p):
        ms_own_parts(2 * p)
        ms_onward(2 * p, 0)
        ms_onward(2 * p + 1, 1)

    each(0, far // 2, ms_far_to_twin)
    pan_to_twin(0)
    ms_to_twin(far)
    ms_y(far).start()
    each(1, far, pan_to_twin)
    ms_y(far + 1).start()
    each(0, far // 2, ms_far_onward)
    each(far, lines, pan_to_twin)
    each(0, far - 1, pan_onward)
    ms_own_parts(far)
    ms_onward(far, 0)
    pan_onward(far - 1)

    spot = (iota((coarse_cols, TC), 1).astype(F32) - 1.5) * 0.25 + 2.0
    tap = iota((coarse_cols, TC), 0) + 2
    up_cols[0:coarse_cols, :] = cubic_weight(spot - tap.astype(F32)).astype(BF16)
    tap = iota((LANES, TC), 0) % 2 + jnp.where(c == 0, coarse_cols + 2, 0)
    up_cols[coarse_cols : coarse_cols + LANES, :] = cubic_weight(spot - tap.astype(F32)).astype(BF16)

    ms_y(lines - 1).wait_recv()
    ms_total[1] += ms_y_recv[lines - 1].astype(F32)

    def ms_arrived(slot, carry):
        ms_z(0, m, slot).wait_recv()
        ms_total[1] += ms_z_recv[slot].astype(F32)
        return carry

    lax.fori_loop(0, blocks, ms_arrived, 0)
    for load in late_loads:
        load.wait()
    values = [ms_total[1, b * coarse_rows : (b + 1) * coarse_rows, :] for b in range(bands)]
    synthetic = sum(synth_ref[b] * values[b] for b in range(bands))
    spot = iota((coarse_rows, LANES), 1) // 2
    edges = jnp.zeros((coarse_rows, LANES), F32)
    for b in range(bands):
        result = values[b] - gain_ref[b] * synthetic
        for k in range(bands):
            result = result + mix_ref[b, k] * values[k]
        window[b, half:mid, :] = result.astype(BF16)
        moved = pltpu.roll(result, jnp.where(c == 0, 2 * b + 2, 2 * b), 1)
        edges = jnp.where(spot == b, moved, edges)
    edge_own[half:mid, :] = edges.astype(BF16)

    has_above, has_below = m > 0, m < n - 1

    def halo_copy(k, src, dst, row, col):
        return remote(src, dst, halo_ss.at[k], halo_rs.at[k], row, col)

    def rows_copy(k, src, dst, row):
        return halo_copy(
            k, window.at[:, pl.ds(src, half)], window.at[:, pl.ds(dst, half)], row, c
        )

    def edge_copy(k, src, dst, rows, row):
        return halo_copy(
            k, edge_own.at[pl.ds(src, rows)], edge_all.at[pl.ds(dst, rows)], row, other
        )

    across_copy = edge_copy(0, half, half, coarse_rows, m)
    up_copies = [rows_copy(1, half, mid, m - 1), edge_copy(2, half, mid, half, m - 1)]
    down_copies = [
        rows_copy(3, coarse_rows, 0, m + 1),
        edge_copy(4, coarse_rows, 0, half, m + 1),
    ]
    across_copy.start()

    @pl.when(has_above)
    def _():
        for copy in up_copies:
            copy.start()

    @pl.when(has_below)
    def _():
        for copy in down_copies:
            copy.start()

    pan_onward(far)
    pan_total[...] = pan_part(m)
    across_copy.wait()

    @pl.when(has_above)
    def _():
        for copy in up_copies:
            copy.wait_send()
        for copy in down_copies:
            copy.wait_recv()

    @pl.when(has_below)
    def _():
        for copy in down_copies:
            copy.wait_send()
        for copy in up_copies:
            copy.wait_recv()

    blank = jnp.zeros((bands, half, coarse_cols), BF16)
    blank_edge = jnp.zeros((half, LANES), BF16)

    @pl.when(jnp.logical_not(has_above))
    def _():
        window[:, 0:half, :] = blank
        edge_all[0:half, :] = blank_edge

    @pl.when(jnp.logical_not(has_below))
    def _():
        window[:, mid : mid + half, :] = blank
        edge_all[mid : mid + half, :] = blank_edge

    edges = edge_all[...]
    spot = iota(edges.shape, 1) // 2
    for first in range(0, bands, GROUP):
        group = range(first, min(first + GROUP, bands))
        source = jnp.concatenate(
            [
                jnp.concatenate(
                    [window[b], jnp.where(spot == b, edges, jnp.zeros_like(edges))], axis=1
                )
                for b in group
            ],
            axis=0,
        )
        across = jnp.dot(source, up_cols[...], preferred_element_type=F32).astype(BF16)
        for b in group:
            begin = (b - first) * 2 * coarse_rows
            mixed[b] = jnp.dot(
                up_rows[...],
                across[begin : begin + 2 * coarse_rows, :],
                preferred_element_type=F32,
            ).astype(BF16)

    store = pltpu.make_async_copy(mixed, mixed_hbm, load_sem.at[9])
    store.start()
    for h in range(HALVES):
        rows = slice(h * part_rows, (h + 1) * part_rows)
        pan_y(lines - 1, h).wait_recv()
        pan_total[rows, :] += pan_y_recv[lines - 1, rows].astype(F32)

        def pan_arrived(slot, carry):
            pan_z(0, h, m, slot).wait_recv()
            pan_total[rows, :] += pan_z_recv[slot, rows].astype(F32)
            return carry

        lax.fori_loop(0, blocks, pan_arrived, 0)

    def y_sent(k, carry):
        ms_y(k).wait_send()
        for h in range(HALVES):
            pan_y(k, h).wait_send()
        return carry

    def z_sent(k, carry):
        ms_z(k, m, 0).wait_send()
        for h in range(HALVES):
            pan_z(k, h, m, 0).wait_send()
        return carry

    lax.fori_loop(0, lines, y_sent, 0)
    lax.fori_loop(0, lines - 1, z_sent, 0)
    store.wait()


def local(
    pan_blocks,
    ms_blocks,
    send_list,
    tile_list,
    row_grid,
    col_grid,
    band_mix,
    band_gain,
    synth_weight,
):
    n = lax.axis_size("mrow")
    lines = n // 2
    own_blocks, size, _ = pan_blocks.shape
    _, coarse_size, coarse_width = ms_blocks.shape
    capacity = tile_list.shape[1] // n
    bands = band_gain.shape[0]
    coarse_rows, coarse_cols = TR // 4, TC // 4
    table_rows = pl.cdiv(2 + pl.cdiv(n * KR * KC, LANES), 8) * 8
    vmem = pl.BlockSpec(memory_space=pltpu.VMEM)
    hbm = pl.BlockSpec(memory_space=pl.ANY)
    dma = pltpu.SemaphoreType.DMA
    slots = lines // 2 + lines

    def ms_slots(count):
        return pltpu.VMEM((count, bands * coarse_rows, coarse_cols), BF16)

    def pan_slots(count):
        return pltpu.VMEM((count, TR, TC), BF16)

    mixed, pan_map = pl.pallas_call(
        functools.partial(mapping, capacity, col_grid.shape[1]),
        out_shape=(
            jax.ShapeDtypeStruct((bands, TR, TC), BF16),
            jax.ShapeDtypeStruct((TR, TC), F32),
        ),
        in_specs=[hbm] * 8,
        out_specs=(hbm, vmem),
        scratch_shapes=[
            pltpu.VMEM(send_list.shape, I32),
            pltpu.VMEM((1, row_grid.shape[0]), F32),
            pltpu.VMEM(col_grid.shape, F32),
            pltpu.SMEM(band_mix.shape, F32),
            pltpu.SMEM(band_gain.shape, F32),
            pltpu.SMEM(synth_weight.shape, F32),
            pltpu.VMEM(pan_blocks.shape, BF16),
            pltpu.VMEM(ms_blocks.shape, BF16),
            pltpu.VMEM((own_blocks + 1, size, size), BF16),
            pltpu.VMEM((own_blocks + 1, coarse_size, coarse_width), BF16),
            pltpu.VMEM((table_rows, LANES), I32),
            pltpu.SMEM((table_rows, LANES), I32),
            pltpu.VMEM((8, LANES), F32),
            pltpu.VMEM((2, n, 8, LANES), F32),
            ms_slots(lines),
            ms_slots(lines),
            pan_slots(lines),
            pan_slots(lines),
            ms_slots(lines - 1),
            ms_slots(slots),
            pan_slots(lines - 1),
            pan_slots(slots),
            pltpu.VMEM((2, bands * coarse_rows, coarse_cols), F32),
            pltpu.VMEM((bands, 2 * coarse_rows, coarse_cols), BF16),
            pltpu.VMEM((2 * coarse_rows, LANES), BF16),
            pltpu.VMEM((2 * coarse_rows, LANES), BF16),
            pltpu.VMEM((coarse_cols + LANES, TC), BF16),
            pltpu.VMEM((TR, 2 * coarse_rows), BF16),
            pltpu.VMEM((bands, TR, TC), BF16),
            dma((10,)),
            dma((2, n)),
            dma((2, n)),
            dma((lines,)),
            dma((lines,)),
            dma((lines, HALVES)),
            dma((lines, HALVES)),
            dma((lines - 1,)),
            dma((slots,)),
            dma((lines - 1, HALVES)),
            dma((slots, HALVES)),
            dma((5,)),
            dma((5,)),
        ],
        compiler_params=pltpu.CompilerParams(
            collective_id=0, has_side_effects=True, vmem_limit_bytes=60 * 1024 * 1024
        ),
        name="mapping",
    )(
        send_list,
        row_grid[None, :],
        col_grid,
        pan_blocks,
        ms_blocks,
        band_mix,
        band_gain,
        synth_weight,
    )
    detail = band_gain[:, None, None] * pan_map[None]
    return (mixed.astype(F32) + detail).astype(BF16)


def solution(mesh):
    return jax.shard_map(
        local,
        mesh=mesh,
        in_specs=(
            P(("scene", "mrow", "mcol"), None, None),
            P(("scene", "mrow", "mcol"), None, None),
            P(None, ("scene", "mrow", "mcol")),
            P(None, ("scene", "mrow", "mcol")),
            P(("scene", "mrow")),
            P(("scene", "mrow"), "mcol"),
            P(),
            P(),
            P(),
        ),
        out_specs=P(None, ("scene", "mrow"), "mcol"),
        check_vma=False,
    )
```

```python
import functools

import jax
import jax.numpy as jnp
from jax import lax
from jax.experimental import pallas as pl
from jax.experimental.pallas import tpu as pltpu
from jax.sharding import PartitionSpec as P

GRID = 64
TR = 128
TC = 512
KR = 2
KC = 5
LANES = 128
PACK = 16
HALVES = 2
MESH = pl.DeviceIdType.MESH
F32 = jnp.float32
BF16 = jnp.bfloat16
I32 = jnp.int32


def cubic_weight(offset):
    outer = jnp.maximum(2.0 - jnp.abs(offset), 0.0)
    shifted = outer - 1.0
    inner = jnp.maximum(shifted, 0.0)
    return outer * outer * (0.5 * shifted) + inner * inner * (1.0 - 2.0 * inner)


def iota(shape, dim):
    return lax.broadcasted_iota(I32, shape, dim)


def row_coord(nodes, position, offset):
    first = position < GRID
    a = jnp.where(first, nodes[:, 0:1], nodes[:, 1:2])
    b = jnp.where(first, nodes[:, 1:2], nodes[:, 2:3])
    within = (jnp.where(first, position, position - GRID).astype(F32) + offset) / GRID
    return a + (b - a) * within


def col_coord(nodes, after, is_last, count, position, offset):
    segment = position // GRID
    coord = jnp.zeros(position.shape, F32)
    for s in range(count):
        left, shift = nodes[:, s : s + 1], s * GRID
        if s + 1 < count:
            right = nodes[:, s + 1 : s + 2]
        else:
            right = jnp.where(is_last, left, after)
            left = jnp.where(is_last, nodes[:, s - 1 : s], left)
            shift = jnp.where(is_last, shift - GRID, shift)
        within = ((position - shift).astype(F32) + offset) / GRID
        coord = jnp.where(segment == s, left + (right - left) * within, coord)
    return coord


def spread(x, origin, size):
    base = jnp.floor(x)
    shape = (PACK, x.shape[1])
    taps = [
        jnp.broadcast_to(cubic_weight(x - (base + t)), shape).astype(BF16)
        for t in (-1.0, 0.0, 1.0, 2.0)
    ]
    groups = size // PACK
    first = base - 1.0 - origin
    group = jnp.floor(first * (1.0 / PACK))
    away = (iota(shape, 0).astype(F32) - (first - group * PACK)).astype(BF16)
    group = jnp.broadcast_to(jnp.clip(group, -2.0, groups + 1.0), shape).astype(BF16)
    none = jnp.zeros(shape, BF16)
    low, high = none, none
    for t in range(4):
        low = jnp.where(away == BF16(t), taps[t], low)
        high = jnp.where(away == BF16(t - PACK), taps[t], high)
    here = [group == BF16(g) for g in range(-1, groups)]
    return jnp.concatenate(
        [jnp.where(here[g + 1], low, jnp.where(here[g], high, none)) for g in range(groups)],
        axis=0,
    )


def mapping(
    capacity,
    col_nodes,
    send_hbm,
    row_hbm,
    col_hbm,
    pan_hbm,
    ms_hbm,
    mix_hbm,
    gain_hbm,
    synth_hbm,
    mixed_hbm,
    pan_total,
    send_ref,
    mix_ref,
    gain_ref,
    synth_ref,
    pan_ref,
    ms_ref,
    pan_sum,
    ms_sum,
    table_ref,
    table,
    rows_all,
    cols_all,
    ms_y_send,
    ms_y_recv,
    pan_y_send,
    pan_y_recv,
    ms_z_send,
    ms_z_recv,
    pan_z_send,
    pan_z_recv,
    near_ms_send,
    near_ms_recv,
    near_pan_send,
    near_pan_recv,
    ms_total,
    ms_hold,
    pan_part_sum,
    pan_hold,
    window,
    rim_send,
    rim_recv,
    edge_send,
    edge_recv,
    edge_own,
    edge_all,
    up_cols,
    up_rows,
    across,
    mixed,
    load_sem,
    rows_ss,
    rows_rs,
    cols_ss,
    cols_rs,
    ms_y_ss,
    ms_y_rs,
    pan_y_ss,
    pan_y_rs,
    ms_z_ss,
    ms_z_rs,
    pan_z_ss,
    pan_z_rs,
    near_ss,
    near_rs,
    halo_ss,
    halo_rs,
):
    n = lax.axis_size("mrow")
    lines = n // 2
    blocks = lines // 2
    scene = lax.axis_index("scene")
    m = lax.axis_index("mrow")
    c = lax.axis_index("mcol")
    z, y = m // 2, m % 2
    twin = z * 2 + (1 - y)
    other = 1 - c
    pair = z // 2
    partner = pair * 2 + (1 - z % 2)
    own_blocks, size, _ = pan_ref.shape
    _, coarse_size, coarse_width = ms_ref.shape
    cells = n * KR * KC
    bands = mixed.shape[0]
    coarse_rows = TR // 4
    coarse_cols = TC // 4
    part_rows = TR // HALVES
    first_col = c * KC
    is_last = c == lax.axis_size("mcol") - 1

    def at(row, col):
        return (scene, row, col)

    def remote(src, dst, ss, rs, row, col):
        return pltpu.make_async_remote_copy(
            src_ref=src,
            dst_ref=dst,
            send_sem=ss,
            recv_sem=rs,
            device_id=at(row, col),
            device_id_type=MESH,
        )

    barrier = pltpu.get_barrier_semaphore()

    def greet(k, carry):
        row = lax.rem(m + k, n)
        pl.semaphore_signal(barrier, inc=1, device_id=at(row, c), device_id_type=MESH)
        pl.semaphore_signal(barrier, inc=1, device_id=at(row, other), device_id_type=MESH)
        return carry

    pl.semaphore_signal(barrier, inc=1, device_id=at(m, other), device_id_type=MESH)
    lax.fori_loop(1, n, greet, 0)
    loads = [
        pltpu.make_async_copy(src, dst, load_sem.at[k])
        for k, (src, dst) in enumerate(
            (
                (row_hbm, rows_all.at[m]),
                (col_hbm, cols_all.at[c, m]),
                (send_hbm, send_ref),
                (ms_hbm, ms_ref),
                (pan_hbm, pan_ref),
                (mix_hbm, mix_ref),
                (gain_hbm, gain_ref),
                (synth_hbm, synth_ref),
            )
        )
    ]
    for load in loads:
        load.start()
    row_load, col_load, send_load, ms_load, pan_load, *late_loads = loads

    pl.semaphore_wait(barrier, 2 * n - 1)

    def rows_copy(slot, row):
        return remote(row_hbm, rows_all.at[slot], rows_ss.at[row], rows_rs.at[slot], row, c)

    def cols_copy(slot_row, slot_col, row, col):
        return remote(
            col_hbm,
            cols_all.at[slot_col, slot_row],
            cols_ss.at[col, row],
            cols_rs.at[slot_col, slot_row],
            row,
            col,
        )

    def send_nodes(k, carry):
        row = lax.rem(m + k, n)
        cols_copy(m, c, row, other).start()
        cols_copy(m, c, row, c).start()
        rows_copy(m, row).start()
        return carry

    lax.fori_loop(1, n, send_nodes, 0)
    cols_copy(m, c, m, other).start()
    send_load.wait()

    square = (own_blocks, own_blocks)
    wide = (own_blocks, LANES)
    owner = send_ref[0:1, :] // capacity
    key_row = (owner * KR + send_ref[1:2, :]) * KC + send_ref[2:3, :] - first_col
    key_row = jnp.broadcast_to(key_row, square)
    diagonal = iota(square, 0) == iota(square, 1)
    key_col = jnp.sum(jnp.where(diagonal, key_row, 0), axis=1, keepdims=True)
    same = key_row == key_col
    before = (key_row < key_col) | (same & (iota(square, 1) < iota(square, 0)))
    rank = jnp.sum(jnp.where(before, 1, 0), axis=1, keepdims=True)
    joined = jnp.sum(jnp.where(before & same, 1, 0), axis=1, keepdims=True)
    hit = rank == iota(wide, 1)
    order = jnp.sum(jnp.where(hit, iota(wide, 0), 0), axis=0, keepdims=True)
    keep = jnp.sum(jnp.where(hit & (joined > 0), 1, 0), axis=0, keepdims=True)
    table_ref[0:1, :] = order
    table_ref[1:2, :] = keep
    for g in range(pl.cdiv(cells, LANES)):
        cell = iota(wide, 1) + g * LANES
        ends = jnp.sum(jnp.where(key_col <= cell, 1, 0), axis=0, keepdims=True)
        count = jnp.sum(jnp.where(key_col == cell, 1, 0), axis=0, keepdims=True)
        table_ref[2 + g : 3 + g, :] = jnp.where(count > 0, ends, 0)
    table_copy = pltpu.make_async_copy(table_ref, table, load_sem.at[8])
    table_copy.start()

    column = iota(up_rows.shape, 1)
    rim = column - coarse_rows
    tap = jnp.where(
        column < coarse_rows, column + 2, rim % 2 + jnp.where(rim < 2 * bands, 0, coarse_rows + 2)
    )
    spot = (iota(up_rows.shape, 0).astype(F32) - 1.5) * 0.25 + 2.0
    up_rows[...] = cubic_weight(spot - tap.astype(F32)).astype(BF16)
    pan_sum[0] = jnp.zeros((size, size), BF16)
    ms_sum[0] = jnp.zeros((coarse_size, coarse_width), BF16)
    table_copy.wait()

    def running(source, sums):
        def step(p, total):
            total = total * table[1, p].astype(F32) + source[table[0, p]].astype(F32)
            sums[p + 1] = total.astype(BF16)
            return total

        start = jnp.zeros(source.shape[1:], F32)
        lax.fori_loop(0, own_blocks, step, start, unroll=2)

    ms_load.wait()
    running(ms_ref, ms_sum)
    pan_load.wait()
    running(pan_ref, pan_sum)

    def wait_nodes(k, carry):
        row = lax.rem(m + k, n)
        cols_copy(row, c, row, c).wait()
        cols_copy(row, other, row, other).wait()
        rows_copy(row, row).wait()
        return carry

    row_load.wait()
    col_load.wait()
    lax.fori_loop(1, n, wait_nodes, 0)
    cols_copy(m, other, m, other).wait()

    def cell_of(sums, tile, row, col):
        cell = (tile * KR + row) * KC + col
        return sums[table[2 + cell // LANES, cell % LANES]]

    def stacked(sums, tile, col):
        return jnp.concatenate([cell_of(sums, tile, row, col) for row in range(KR)], axis=0)

    def ms_part(tile):
        row_nodes, nodes = rows_all[tile], cols_all[c, tile]
        after = cols_all[1, tile][:, 0:1]
        x_ms = col_coord(
            nodes, after, is_last, col_nodes, 4 * iota((1, coarse_cols), 1) + 1, 0.5
        )
        x_ms = (x_ms - 1.5) * 0.25
        col = spread(x_ms, (first_col * coarse_size).astype(F32), KC * coarse_size)
        spots = (row_coord(row_nodes, 4 * iota((coarse_rows, 1), 0) + 1, 0.5) - 1.5) * 0.25
        taps = iota((coarse_rows, KR * coarse_size), 1).astype(F32)
        weight = cubic_weight(spots - taps).astype(BF16)
        rows = [
            jnp.dot(weight, stacked(ms_sum, tile, k), preferred_element_type=F32).astype(BF16)
            for k in range(KC)
        ]
        by_band = [
            jnp.concatenate(
                [row[:, b * coarse_size : (b + 1) * coarse_size] for row in rows], axis=1
            )
            for b in range(bands)
        ]
        return jnp.dot(jnp.concatenate(by_band, axis=0), col, preferred_element_type=F32)

    def pan_part(tile):
        row_nodes, nodes = rows_all[tile], cols_all[c, tile]
        after = cols_all[1, tile][:, 0:1]
        x_pan = col_coord(nodes, after, is_last, col_nodes, iota((1, TC), 1), 0.0)
        col = spread(x_pan, (first_col * size).astype(F32), KC * size)
        row = spread(row_coord(row_nodes, iota((1, TR), 1), 0.0), 0.0, KR * size)
        rows = []
        for k in range(0, KC, 2):
            source = jnp.concatenate(
                [stacked(pan_sum, tile, j) for j in range(k, min(k + 2, KC))], axis=1
            )
            rows.append(
                lax.dot_general(
                    row, source, (((0,), (0,)), ((), ())), preferred_element_type=F32
                ).astype(BF16)
            )
        return jnp.dot(jnp.concatenate(rows, axis=1), col, preferred_element_type=F32)

    def line_of(k):
        up = lax.rem(pair * 2 + 2 + k, lines)
        down = lax.rem(pair * 2 + lines - 1 - k, lines)
        far = jnp.where(pair % 2 == 0, down, up)
        return jnp.where(k < lines - 2, far, jnp.where(k == lines - 2, partner, z))

    def ms_y(k):
        return remote(ms_y_send.at[k], ms_y_recv.at[k], ms_y_ss.at[k], ms_y_rs.at[k], twin, c)

    def pan_y(k, h):
        part = pl.ds(h * part_rows, part_rows)
        return remote(
            pan_y_send.at[k, part],
            pan_y_recv.at[k, part],
            pan_y_ss.at[k, h],
            pan_y_rs.at[k, h],
            twin,
            c,
        )

    def route(line):
        far = line // 2 != pair
        above = line // 2 > pair
        lower = z % 2 == 0
        inner = far & jnp.logical_xor(above, lower)
        outer = far & jnp.logical_not(jnp.logical_xor(above, lower))
        target = jnp.where(outer, partner, line)
        slot = jnp.where(outer, blocks + line, pair)
        return inner, target * 2 + y, slot

    def ms_z(k, row, slot):
        return remote(
            ms_z_send.at[k], ms_z_recv.at[slot], ms_z_ss.at[k], ms_z_rs.at[slot], row, c
        )

    def pan_z(k, h, row, slot):
        part = pl.ds(h * part_rows, part_rows)
        return remote(
            pan_z_send.at[k, part],
            pan_z_recv.at[slot, part],
            pan_z_ss.at[k, h],
            pan_z_rs.at[slot, h],
            row,
            c,
        )

    def each(first, last, step):
        if last - first == 1:
            step(first)
            return

        def body(k, carry):
            step(k)
            return carry

        lax.fori_loop(first, last, body, 0)

    near_row = partner * 2 + y

    def near(k, src, dst):
        return remote(src, dst, near_ss.at[k], near_rs.at[k], near_row, c)

    near_ms = near(0, near_ms_send, near_ms_recv)
    near_pan = near(1, near_pan_send, near_pan_recv)
    first_rows = slice(0, part_rows)

    def ms_twin_parts(k):
        return [ms_part(line_of(k + i) * 2 + 1 - y) for i in range(2)]

    def pan_twin_part(k):
        return pan_part(line_of(k) * 2 + 1 - y)

    def pan_to_twin(k):
        pan_y_send[k] = pan_twin_part(k).astype(BF16)
        for h in range(HALVES):
            pan_y(k, h).start()

    def ms_own_parts(k):
        parts = [ms_part(line_of(k + i) * 2 + y) for i in range(2)]
        for i, part in enumerate(parts):
            ms_total[i] = part

    def ms_onward(k, i):
        line = line_of(k)
        inner, row, slot = route(line)
        ms_y(k).wait_recv()
        ms_total[i] += ms_y_recv[k].astype(F32)

        @pl.when(inner)
        def _():
            ms_z(0, row, blocks + line).wait_recv()
            ms_total[i] += ms_z_recv[blocks + line].astype(F32)

        ms_z_send[k] = ms_total[i].astype(BF16)
        ms_z(k, row, slot).start()

    def pan_onward(k):
        line = line_of(k)
        inner, row, slot = route(line)
        pan_part_sum[...] = pan_part(line * 2 + y)
        for h in range(HALVES):
            rows = slice(h * part_rows, (h + 1) * part_rows)
            pan_y(k, h).wait_recv()
            pan_part_sum[rows, :] += pan_y_recv[k, rows].astype(F32)

            @pl.when(inner)
            def _():
                pan_z(0, h, row, blocks + line).wait_recv()
                pan_part_sum[rows, :] += pan_z_recv[blocks + line, rows].astype(F32)

            pan_z_send[k, rows] = pan_part_sum[rows, :].astype(BF16)
            pan_z(k, h, row, slot).start()

    far = lines - 2
    last = lines - 1

    def ms_far_to_twin(p):
        for i, part in enumerate(ms_twin_parts(2 * p)):
            ms_y_send[2 * p + i] = part.astype(BF16)
        ms_y(2 * p).start()
        ms_y(2 * p + 1).start()

    def ms_far_onward(p):
        ms_own_parts(2 * p)
        ms_onward(2 * p, 0)
        ms_onward(2 * p + 1, 1)

    each(0, far // 2, ms_far_to_twin)
    parts = ms_twin_parts(far)
    near_ms_send[...] = parts[0].astype(BF16)
    ms_hold[...] = parts[1]
    near_ms.start()
    pan_to_twin(0)
    pan_y_send[far] = pan_twin_part(far).astype(BF16)
    near_pan_send[...] = pan_y_send[far, first_rows]
    near_pan.start()
    each(1, far, pan_to_twin)
    for h in range(1, HALVES):
        pan_y(far, h).start()
    pan_hold[...] = pan_twin_part(last)
    near_ms.wait_recv()
    ms_y_send[last] = (ms_hold[...] + near_ms_recv[...].astype(F32)).astype(BF16)
    ms_y(last).start()
    near_pan.wait_recv()
    pan_hold[first_rows, :] += near_pan_recv[...].astype(F32)
    pan_y_send[last] = pan_hold[...].astype(BF16)
    for h in range(HALVES):
        pan_y(last, h).start()
    each(0, far // 2, ms_far_onward)

    early = route(line_of(far - 1))[0]
    ms_own_parts(far)
    ms_z_send[far] = ms_total[0].astype(BF16)
    pan_hold[...] = pan_part(near_row)
    pan_z_send[far, first_rows] = pan_hold[first_rows, :].astype(BF16)

    def near_start():
        ms_z(far, near_row, pair).start()
        pan_z(far, 0, near_row, pair).start()

    pl.when(early)(near_start)
    each(0, far, pan_onward)
    pl.when(jnp.logical_not(early))(near_start)

    spot = (iota((coarse_cols, TC), 1).astype(F32) - 1.5) * 0.25 + 2.0
    tap = iota((coarse_cols, TC), 0) + 2
    up_cols[0:coarse_cols, :] = cubic_weight(spot - tap.astype(F32)).astype(BF16)
    tap = iota((LANES, TC), 0) % 2 + jnp.where(c == 0, coarse_cols + 2, 0)
    up_cols[coarse_cols : coarse_cols + LANES, :] = cubic_weight(spot - tap.astype(F32)).astype(BF16)

    ms_y(last).wait_recv()
    ms_total[1] += ms_y_recv[last].astype(F32)

    def ms_arrived(slot, carry):
        ms_z(0, m, slot).wait_recv()
        ms_total[1] += ms_z_recv[slot].astype(F32)
        return carry

    lax.fori_loop(0, blocks, ms_arrived, 0)
    for load in late_loads:
        load.wait()
    values = [ms_total[1, b * coarse_rows : (b + 1) * coarse_rows, :] for b in range(bands)]
    synthetic = sum(synth_ref[b] * values[b] for b in range(bands))
    spot = iota((coarse_rows, LANES), 1) // 2
    edges = jnp.zeros((coarse_rows, LANES), F32)
    tops, bottoms = [], []
    for b in range(bands):
        result = values[b] - gain_ref[b] * synthetic
        for k in range(bands):
            result = result + mix_ref[b, k] * values[k]
        window[b] = result.astype(BF16)
        moved = pltpu.roll(result, jnp.where(c == 0, 2 * b + 2, 2 * b), 1)
        edges = jnp.where(spot == b, moved, edges)
        tops.append(result[0:2, :])
        bottoms.append(result[coarse_rows - 2 : coarse_rows, :])
    edge_own[...] = edges.astype(BF16)
    rim_send[0] = jnp.concatenate(tops, axis=0).astype(BF16)
    rim_send[1] = jnp.concatenate(bottoms, axis=0).astype(BF16)
    edge_send[0] = jnp.concatenate([edges[0:2, :]] * bands, axis=0).astype(BF16)
    bottom = edges[coarse_rows - 2 : coarse_rows, :]
    edge_send[1] = jnp.concatenate([bottom] * bands, axis=0).astype(BF16)

    has_above, has_below = m > 0, m < n - 1

    def halo_copy(k, src, dst, row, col):
        return remote(src, dst, halo_ss.at[k], halo_rs.at[k], row, col)

    across_copy = halo_copy(0, edge_own, edge_all, m, other)
    up_copies = [
        halo_copy(1, rim_send.at[0], rim_recv.at[1], m - 1, c),
        halo_copy(2, edge_send.at[0], edge_recv.at[1], m - 1, other),
    ]
    down_copies = [
        halo_copy(3, rim_send.at[1], rim_recv.at[0], m + 1, c),
        halo_copy(4, edge_send.at[1], edge_recv.at[0], m + 1, other),
    ]
    across_copy.start()

    @pl.when(has_above)
    def _():
        for copy in up_copies:
            copy.start()

    @pl.when(has_below)
    def _():
        for copy in down_copies:
            copy.start()

    for h in range(1, HALVES):
        rows = slice(h * part_rows, (h + 1) * part_rows)
        pan_y(far, h).wait_recv()
        pan_hold[rows, :] += pan_y_recv[far, rows].astype(F32)
        pan_z_send[far, rows] = pan_hold[rows, :].astype(BF16)
        pan_z(far, h, near_row, pair).start()
    pan_total[...] = pan_part(m)
    across_copy.wait()

    edges = edge_all[...]
    spot = iota(edges.shape, 1) // 2
    source = jnp.concatenate(
        [
            jnp.concatenate(
                [window[b], jnp.where(spot == b, edges, jnp.zeros_like(edges))], axis=1
            )
            for b in range(bands)
        ],
        axis=0,
    )
    across[0 : bands * coarse_rows, :] = jnp.dot(
        source, up_cols[...], preferred_element_type=F32
    ).astype(BF16)
    for b in range(bands):
        own = slice(b * coarse_rows, (b + 1) * coarse_rows)
        mixed[b, PACK : TR - PACK, :] = jnp.dot(
            up_rows[PACK : TR - PACK, 0:coarse_rows],
            across[own, :],
            preferred_element_type=F32,
        ).astype(BF16)

    @pl.when(has_above)
    def _():
        for copy in up_copies:
            copy.wait_send()
        for copy in down_copies:
            copy.wait_recv()

    @pl.when(has_below)
    def _():
        for copy in down_copies:
            copy.wait_send()
        for copy in up_copies:
            copy.wait_recv()

    blank = jnp.zeros((2 * bands, LANES), BF16)

    @pl.when(jnp.logical_not(has_above))
    def _():
        rim_recv[0] = blank
        edge_recv[0] = blank

    @pl.when(jnp.logical_not(has_below))
    def _():
        rim_recv[1] = blank
        edge_recv[1] = blank

    spot = iota((2 * bands, LANES), 1) // 2
    mine = spot == iota((2 * bands, LANES), 0) // 2
    source = jnp.concatenate(
        [
            jnp.concatenate([rim_recv[i], jnp.where(mine, edge_recv[i], blank)], axis=1)
            for i in range(2)
        ],
        axis=0,
    )
    rims = jnp.dot(source, up_cols[...], preferred_element_type=F32).astype(BF16)
    outer = jnp.concatenate([up_rows[0:PACK, :], up_rows[TR - PACK : TR, :]], axis=0)
    column = iota(outer.shape, 1)
    owner_band = (column - coarse_rows) % (2 * bands) // 2
    for b in range(bands):
        weight = jnp.where((column < coarse_rows) | (owner_band == b), outer, jnp.zeros_like(outer))
        own = slice(b * coarse_rows, (b + 1) * coarse_rows)
        ends = jnp.dot(
            weight, jnp.concatenate([across[own, :], rims], axis=0), preferred_element_type=F32
        ).astype(BF16)
        mixed[b, 0:PACK, :] = ends[0:PACK, :]
        mixed[b, TR - PACK : TR, :] = ends[PACK : 2 * PACK, :]

    store = pltpu.make_async_copy(mixed, mixed_hbm, load_sem.at[9])
    store.start()
    for h in range(HALVES):
        rows = slice(h * part_rows, (h + 1) * part_rows)
        pan_y(last, h).wait_recv()
        pan_total[rows, :] += pan_y_recv[last, rows].astype(F32)

        def pan_arrived(slot, carry):
            pan_z(0, h, m, slot).wait_recv()
            pan_total[rows, :] += pan_z_recv[slot, rows].astype(F32)
            return carry

        lax.fori_loop(0, blocks, pan_arrived, 0)

    def y_sent(k, carry):
        ms_y(k).wait_send()
        pan_y(k, 0).wait_send()
        return carry

    def y_rest_sent(k, carry):
        for h in range(1, HALVES):
            pan_y(k, h).wait_send()
        return carry

    def z_sent(k, carry):
        ms_z(k, m, 0).wait_send()
        for h in range(HALVES):
            pan_z(k, h, m, 0).wait_send()
        return carry

    near_ms.wait_send()
    near_pan.wait_send()
    lax.fori_loop(0, far, y_sent, 0)
    lax.fori_loop(last, lines, y_sent, 0)
    lax.fori_loop(0, lines, y_rest_sent, 0)
    lax.fori_loop(0, lines - 1, z_sent, 0)
    store.wait()


def local(
    pan_blocks,
    ms_blocks,
    send_list,
    tile_list,
    row_grid,
    col_grid,
    band_mix,
    band_gain,
    synth_weight,
):
    n = lax.axis_size("mrow")
    lines = n // 2
    own_blocks, size, _ = pan_blocks.shape
    _, coarse_size, coarse_width = ms_blocks.shape
    capacity = tile_list.shape[1] // n
    bands = band_gain.shape[0]
    coarse_rows, coarse_cols = TR // 4, TC // 4
    table_rows = pl.cdiv(2 + pl.cdiv(n * KR * KC, LANES), 8) * 8
    vmem = pl.BlockSpec(memory_space=pltpu.VMEM)
    hbm = pl.BlockSpec(memory_space=pl.ANY)
    dma = pltpu.SemaphoreType.DMA
    slots = lines // 2 + lines

    def ms_slots(count):
        return pltpu.VMEM((count, bands * coarse_rows, coarse_cols), BF16)

    def pan_slots(count):
        return pltpu.VMEM((count, TR, TC), BF16)

    mixed, pan_map = pl.pallas_call(
        functools.partial(mapping, capacity, col_grid.shape[1]),
        out_shape=(
            jax.ShapeDtypeStruct((bands, TR, TC), BF16),
            jax.ShapeDtypeStruct((TR, TC), F32),
        ),
        in_specs=[hbm] * 8,
        out_specs=(hbm, vmem),
        scratch_shapes=[
            pltpu.VMEM(send_list.shape, I32),
            pltpu.SMEM(band_mix.shape, F32),
            pltpu.SMEM(band_gain.shape, F32),
            pltpu.SMEM(synth_weight.shape, F32),
            pltpu.VMEM(pan_blocks.shape, BF16),
            pltpu.VMEM(ms_blocks.shape, BF16),
            pltpu.VMEM((own_blocks + 1, size, size), BF16),
            pltpu.VMEM((own_blocks + 1, coarse_size, coarse_width), BF16),
            pltpu.VMEM((table_rows, LANES), I32),
            pltpu.SMEM((table_rows, LANES), I32),
            pltpu.VMEM((n, 1, row_grid.shape[0]), F32),
            pltpu.VMEM((2, n) + col_grid.shape, F32),
            ms_slots(lines),
            ms_slots(lines),
            pan_slots(lines),
            pan_slots(lines),
            ms_slots(lines - 1),
            ms_slots(slots),
            pan_slots(lines - 1),
            pan_slots(slots),
            pltpu.VMEM((bands * coarse_rows, coarse_cols), BF16),
            pltpu.VMEM((bands * coarse_rows, coarse_cols), BF16),
            pltpu.VMEM((TR // HALVES, TC), BF16),
            pltpu.VMEM((TR // HALVES, TC), BF16),
            pltpu.VMEM((2, bands * coarse_rows, coarse_cols), F32),
            pltpu.VMEM((bands * coarse_rows, coarse_cols), F32),
            pltpu.VMEM((TR, TC), F32),
            pltpu.VMEM((TR, TC), F32),
            pltpu.VMEM((bands, coarse_rows, coarse_cols), BF16),
            pltpu.VMEM((2, 2 * bands, LANES), BF16),
            pltpu.VMEM((2, 2 * bands, LANES), BF16),
            pltpu.VMEM((2, 2 * bands, LANES), BF16),
            pltpu.VMEM((2, 2 * bands, LANES), BF16),
            pltpu.VMEM((coarse_rows, LANES), BF16),
            pltpu.VMEM((coarse_rows, LANES), BF16),
            pltpu.VMEM((coarse_cols + LANES, TC), BF16),
            pltpu.VMEM((TR, coarse_rows + 4 * bands), BF16),
            pltpu.VMEM((bands * coarse_rows, TC), BF16),
            pltpu.VMEM((bands, TR, TC), BF16),
            dma((10,)),
            dma((n,)),
            dma((n,)),
            dma((2, n)),
            dma((2, n)),
            dma((lines,)),
            dma((lines,)),
            dma((lines, HALVES)),
            dma((lines, HALVES)),
            dma((lines - 1,)),
            dma((slots,)),
            dma((lines - 1, HALVES)),
            dma((slots, HALVES)),
            dma((2,)),
            dma((2,)),
            dma((5,)),
            dma((5,)),
        ],
        compiler_params=pltpu.CompilerParams(
            collective_id=0, has_side_effects=True, vmem_limit_bytes=60 * 1024 * 1024
        ),
        name="mapping",
    )(
        send_list,
        row_grid[None, :],
        col_grid,
        pan_blocks,
        ms_blocks,
        band_mix,
        band_gain,
        synth_weight,
    )
    detail = band_gain[:, None, None] * pan_map[None]
    return (mixed.astype(F32) + detail).astype(BF16)


def solution(mesh):
    return jax.shard_map(
        local,
        mesh=mesh,
        in_specs=(
            P(("scene", "mrow", "mcol"), None, None),
            P(("scene", "mrow", "mcol"), None, None),
            P(None, ("scene", "mrow", "mcol")),
            P(None, ("scene", "mrow", "mcol")),
            P(("scene", "mrow")),
            P(("scene", "mrow"), "mcol"),
            P(),
            P(),
            P(),
        ),
        out_specs=P(None, ("scene", "mrow"), "mcol"),
        check_vma=False,
    )
```

```python
import functools

import jax
import jax.numpy as jnp
from jax import lax
from jax.experimental import pallas as pl
from jax.experimental.pallas import tpu as pltpu
from jax.sharding import PartitionSpec as P

GRID = 64
TR = 128
TC = 512
KR = 2
KC = 5
LANES = 128
PACK = 16
HALVES = 2
MESH = pl.DeviceIdType.MESH
F32 = jnp.float32
BF16 = jnp.bfloat16
I32 = jnp.int32


def cubic_weight(offset):
    outer = jnp.maximum(2.0 - jnp.abs(offset), 0.0)
    shifted = outer - 1.0
    inner = jnp.maximum(shifted, 0.0)
    return outer * outer * (0.5 * shifted) + inner * inner * (1.0 - 2.0 * inner)


def iota(shape, dim):
    return lax.broadcasted_iota(I32, shape, dim)


def row_coord(nodes, position, offset):
    first = position < GRID
    a = jnp.where(first, nodes[:, 0:1], nodes[:, 1:2])
    b = jnp.where(first, nodes[:, 1:2], nodes[:, 2:3])
    within = (jnp.where(first, position, position - GRID).astype(F32) + offset) / GRID
    return a + (b - a) * within


def col_coord(nodes, after, is_last, count, position, offset):
    segment = position // GRID
    coord = jnp.zeros(position.shape, F32)
    for s in range(count):
        left, shift = nodes[:, s : s + 1], s * GRID
        if s + 1 < count:
            right = nodes[:, s + 1 : s + 2]
        else:
            right = jnp.where(is_last, left, after)
            left = jnp.where(is_last, nodes[:, s - 1 : s], left)
            shift = jnp.where(is_last, shift - GRID, shift)
        within = ((position - shift).astype(F32) + offset) / GRID
        coord = jnp.where(segment == s, left + (right - left) * within, coord)
    return coord


def spread(x, origin, size):
    base = jnp.floor(x)
    shape = (PACK, x.shape[1])
    taps = [
        jnp.broadcast_to(cubic_weight(x - (base + t)), shape).astype(BF16)
        for t in (-1.0, 0.0, 1.0, 2.0)
    ]
    groups = size // PACK
    first = base - 1.0 - origin
    group = jnp.floor(first * (1.0 / PACK))
    away = (iota(shape, 0).astype(F32) - (first - group * PACK)).astype(BF16)
    group = jnp.broadcast_to(jnp.clip(group, -2.0, groups + 1.0), shape).astype(BF16)
    none = jnp.zeros(shape, BF16)
    low, high = none, none
    for t in range(4):
        low = jnp.where(away == BF16(t), taps[t], low)
        high = jnp.where(away == BF16(t - PACK), taps[t], high)
    here = [group == BF16(g) for g in range(-1, groups)]
    return jnp.concatenate(
        [jnp.where(here[g + 1], low, jnp.where(here[g], high, none)) for g in range(groups)],
        axis=0,
    )


def mapping(
    capacity,
    col_nodes,
    send_hbm,
    row_hbm,
    col_hbm,
    pan_hbm,
    ms_hbm,
    mix_hbm,
    gain_hbm,
    synth_hbm,
    mixed_hbm,
    pan_total,
    send_ref,
    row_ref,
    col_ref,
    mix_ref,
    gain_ref,
    synth_ref,
    pan_ref,
    ms_ref,
    pan_sum,
    ms_sum,
    table_ref,
    table,
    nodes_ref,
    nodes_all,
    ms_y_send,
    ms_y_recv,
    pan_y_send,
    pan_y_recv,
    ms_z_send,
    ms_z_recv,
    pan_z_send,
    pan_z_recv,
    near_ms_send,
    near_ms_recv,
    ms_total,
    ms_hold,
    ms_mine,
    window,
    rim_send,
    rim_recv,
    edge_send,
    edge_recv,
    edge_own,
    edge_all,
    up_cols,
    up_rows,
    across,
    mixed,
    load_sem,
    nodes_ss,
    nodes_rs,
    ms_y_ss,
    ms_y_rs,
    pan_y_ss,
    pan_y_rs,
    ms_z_ss,
    ms_z_rs,
    pan_z_ss,
    pan_z_rs,
    near_ss,
    near_rs,
    halo_ss,
    halo_rs,
):
    n = lax.axis_size("mrow")
    lines = n // 2
    blocks = lines // 2
    scene = lax.axis_index("scene")
    m = lax.axis_index("mrow")
    c = lax.axis_index("mcol")
    z, y = m // 2, m % 2
    twin = z * 2 + (1 - y)
    other = 1 - c
    pair = z // 2
    partner = pair * 2 + (1 - z % 2)
    own_blocks, size, _ = pan_ref.shape
    _, coarse_size, coarse_width = ms_ref.shape
    cells = n * KR * KC
    bands = mixed.shape[0]
    coarse_rows = TR // 4
    coarse_cols = TC // 4
    part_rows = TR // HALVES
    first_col = c * KC
    is_last = c == lax.axis_size("mcol") - 1

    def at(row, col):
        return (scene, row, col)

    def remote(src, dst, ss, rs, row, col):
        return pltpu.make_async_remote_copy(
            src_ref=src,
            dst_ref=dst,
            send_sem=ss,
            recv_sem=rs,
            device_id=at(row, col),
            device_id_type=MESH,
        )

    barrier = pltpu.get_barrier_semaphore()

    def greet(k, carry):
        row = lax.rem(m + k, n)
        pl.semaphore_signal(barrier, inc=1, device_id=at(row, c), device_id_type=MESH)
        pl.semaphore_signal(barrier, inc=1, device_id=at(row, other), device_id_type=MESH)
        return carry

    pl.semaphore_signal(barrier, inc=1, device_id=at(m, other), device_id_type=MESH)
    lax.fori_loop(1, n, greet, 0)
    loads = [
        pltpu.make_async_copy(src, dst, load_sem.at[k])
        for k, (src, dst) in enumerate(
            (
                (row_hbm, row_ref),
                (col_hbm, col_ref),
                (send_hbm, send_ref),
                (ms_hbm, ms_ref),
                (pan_hbm, pan_ref),
                (mix_hbm, mix_ref),
                (gain_hbm, gain_ref),
                (synth_hbm, synth_ref),
            )
        )
    ]
    for load in loads:
        load.start()
    row_load, col_load, send_load, ms_load, pan_load, *late_loads = loads

    nodes_ref[...] = jnp.zeros_like(nodes_ref)
    row_load.wait()
    col_load.wait()
    nodes_ref[0:1, 0 : row_ref.shape[1]] = row_ref[...]
    nodes_ref[1:2, 0 : col_ref.shape[1]] = col_ref[...]
    nodes_all[c, m] = nodes_ref[...]
    pl.semaphore_wait(barrier, 2 * n - 1)

    def nodes_copy(slot_row, slot_col, row, col):
        return remote(
            nodes_ref,
            nodes_all.at[slot_col, slot_row],
            nodes_ss.at[col, row],
            nodes_rs.at[slot_col, slot_row],
            row,
            col,
        )

    def send_nodes(k, carry):
        row = lax.rem(m + k, n)
        nodes_copy(m, c, row, c).start()
        nodes_copy(m, c, row, other).start()
        return carry

    lax.fori_loop(1, n, send_nodes, 0)
    nodes_copy(m, c, m, other).start()
    send_load.wait()

    square = (own_blocks, own_blocks)
    wide = (own_blocks, LANES)
    owner = send_ref[0:1, :] // capacity
    key_row = (owner * KR + send_ref[1:2, :]) * KC + send_ref[2:3, :] - first_col
    key_row = jnp.broadcast_to(key_row, square)
    diagonal = iota(square, 0) == iota(square, 1)
    key_col = jnp.sum(jnp.where(diagonal, key_row, 0), axis=1, keepdims=True)
    same = key_row == key_col
    before = (key_row < key_col) | (same & (iota(square, 1) < iota(square, 0)))
    rank = jnp.sum(jnp.where(before, 1, 0), axis=1, keepdims=True)
    joined = jnp.sum(jnp.where(before & same, 1, 0), axis=1, keepdims=True)
    hit = rank == iota(wide, 1)
    order = jnp.sum(jnp.where(hit, iota(wide, 0), 0), axis=0, keepdims=True)
    keep = jnp.sum(jnp.where(hit & (joined > 0), 1, 0), axis=0, keepdims=True)
    table_ref[0:1, :] = order
    table_ref[1:2, :] = keep
    for g in range(pl.cdiv(cells, LANES)):
        cell = iota(wide, 1) + g * LANES
        ends = jnp.sum(jnp.where(key_col <= cell, 1, 0), axis=0, keepdims=True)
        count = jnp.sum(jnp.where(key_col == cell, 1, 0), axis=0, keepdims=True)
        table_ref[2 + g : 3 + g, :] = jnp.where(count > 0, ends, 0)
    table_copy = pltpu.make_async_copy(table_ref, table, load_sem.at[8])
    table_copy.start()

    column = iota(up_rows.shape, 1)
    rim = column - coarse_rows
    tap = jnp.where(
        column < coarse_rows, column + 2, rim % 2 + jnp.where(rim < 2 * bands, 0, coarse_rows + 2)
    )
    spot = (iota(up_rows.shape, 0).astype(F32) - 1.5) * 0.25 + 2.0
    up_rows[...] = cubic_weight(spot - tap.astype(F32)).astype(BF16)
    pan_sum[0] = jnp.zeros((size, size), BF16)
    ms_sum[0] = jnp.zeros((coarse_size, coarse_width), BF16)
    table_copy.wait()

    def running(source, sums):
        def step(p, total):
            total = total * table[1, p].astype(F32) + source[table[0, p]].astype(F32)
            sums[p + 1] = total.astype(BF16)
            return total

        start = jnp.zeros(source.shape[1:], F32)
        lax.fori_loop(0, own_blocks, step, start, unroll=2)

    ms_load.wait()
    running(ms_ref, ms_sum)
    pan_load.wait()
    running(pan_ref, pan_sum)

    def wait_nodes(k, carry):
        row = lax.rem(m + k, n)
        nodes_copy(row, c, row, c).wait()
        nodes_copy(row, other, row, other).wait()
        return carry

    lax.fori_loop(1, n, wait_nodes, 0)
    nodes_copy(m, other, m, other).wait()

    def cell_of(sums, tile, row, col):
        cell = (tile * KR + row) * KC + col
        return sums[table[2 + cell // LANES, cell % LANES]]

    def stacked(sums, tile, col):
        return jnp.concatenate([cell_of(sums, tile, row, col) for row in range(KR)], axis=0)

    def ms_part(tile):
        row_nodes, nodes = nodes_all[c, tile, 0:1], nodes_all[c, tile, 1:2]
        after = nodes_all[1, tile, 1:2, 0:1]
        x_ms = col_coord(
            nodes, after, is_last, col_nodes, 4 * iota((1, coarse_cols), 1) + 1, 0.5
        )
        x_ms = (x_ms - 1.5) * 0.25
        col = spread(x_ms, (first_col * coarse_size).astype(F32), KC * coarse_size)
        spots = (row_coord(row_nodes, 4 * iota((coarse_rows, 1), 0) + 1, 0.5) - 1.5) * 0.25
        taps = iota((coarse_rows, KR * coarse_size), 1).astype(F32)
        weight = cubic_weight(spots - taps).astype(BF16)
        rows = [
            jnp.dot(weight, stacked(ms_sum, tile, k), preferred_element_type=F32).astype(BF16)
            for k in range(KC)
        ]
        by_band = [
            jnp.concatenate(
                [row[:, b * coarse_size : (b + 1) * coarse_size] for row in rows], axis=1
            )
            for b in range(bands)
        ]
        return jnp.dot(jnp.concatenate(by_band, axis=0), col, preferred_element_type=F32)

    def pan_part(tile):
        row_nodes, nodes = nodes_all[c, tile, 0:1], nodes_all[c, tile, 1:2]
        after = nodes_all[1, tile, 1:2, 0:1]
        x_pan = col_coord(nodes, after, is_last, col_nodes, iota((1, TC), 1), 0.0)
        col = spread(x_pan, (first_col * size).astype(F32), KC * size)
        row = spread(row_coord(row_nodes, iota((1, TR), 1), 0.0), 0.0, KR * size)
        rows = []
        for k in range(0, KC, 2):
            source = jnp.concatenate(
                [stacked(pan_sum, tile, j) for j in range(k, min(k + 2, KC))], axis=1
            )
            rows.append(
                lax.dot_general(
                    row, source, (((0,), (0,)), ((), ())), preferred_element_type=F32
                ).astype(BF16)
            )
        return jnp.dot(jnp.concatenate(rows, axis=1), col, preferred_element_type=F32)

    def line_of(k):
        up = lax.rem(pair * 2 + 2 + k, lines)
        down = lax.rem(pair * 2 + lines - 1 - k, lines)
        far = jnp.where(pair % 2 == 0, down, up)
        return jnp.where(k < lines - 2, far, jnp.where(k == lines - 2, partner, z))

    def ms_y(k):
        return remote(ms_y_send.at[k], ms_y_recv.at[k], ms_y_ss.at[k], ms_y_rs.at[k], twin, c)

    def pan_y(k, h):
        part = pl.ds(h * part_rows, part_rows)
        return remote(
            pan_y_send.at[k, part],
            pan_y_recv.at[k, part],
            pan_y_ss.at[k, h],
            pan_y_rs.at[k, h],
            twin,
            c,
        )

    def route(line):
        far = line // 2 != pair
        above = line // 2 > pair
        lower = z % 2 == 0
        inner = far & jnp.logical_xor(above, lower)
        outer = far & jnp.logical_not(jnp.logical_xor(above, lower))
        target = jnp.where(outer, partner, line)
        slot = jnp.where(outer, blocks + line, pair)
        return inner, target * 2 + y, slot

    def ms_z(k, row, slot):
        return remote(
            ms_z_send.at[k], ms_z_recv.at[slot], ms_z_ss.at[k], ms_z_rs.at[slot], row, c
        )

    def pan_z(k, h, row, slot):
        part = pl.ds(h * part_rows, part_rows)
        return remote(
            pan_z_send.at[k, part],
            pan_z_recv.at[slot, part],
            pan_z_ss.at[k, h],
            pan_z_rs.at[slot, h],
            row,
            c,
        )

    def each(first, last, step):
        if last - first == 1:
            step(first)
            return

        def body(k, carry):
            step(k)
            return carry

        lax.fori_loop(first, last, body, 0)

    near_row = partner * 2 + y

    near_ms = remote(near_ms_send, near_ms_recv, near_ss, near_rs, near_row, c)

    def ms_twin_parts(k):
        return [ms_part(line_of(k + i) * 2 + 1 - y) for i in range(2)]

    def pan_twin_part(k):
        return pan_part(line_of(k) * 2 + 1 - y)

    def pan_to_twin(k):
        pan_y_send[k] = pan_twin_part(k).astype(BF16)
        for h in range(HALVES):
            pan_y(k, h).start()

    def ms_own_parts(k):
        parts = [ms_part(line_of(k + i) * 2 + y) for i in range(2)]
        for i, part in enumerate(parts):
            ms_total[i] = part

    def ms_onward(k, i):
        line = line_of(k)
        inner, row, slot = route(line)
        ms_y(k).wait_recv()
        ms_total[i] += ms_y_recv[k].astype(F32)

        @pl.when(inner)
        def _():
            ms_z(0, row, blocks + line).wait_recv()
            ms_total[i] += ms_z_recv[blocks + line].astype(F32)

        ms_z_send[k] = ms_total[i].astype(BF16)
        ms_z(k, row, slot).start()

    def pan_onward(k):
        line = line_of(k)
        inner, row, slot = route(line)
        pan_total[...] = pan_part(line * 2 + y)
        for h in range(HALVES):
            rows = slice(h * part_rows, (h + 1) * part_rows)
            pan_y(k, h).wait_recv()
            pan_total[rows, :] += pan_y_recv[k, rows].astype(F32)

            @pl.when(inner)
            def _():
                pan_z(0, h, row, blocks + line).wait_recv()
                pan_total[rows, :] += pan_z_recv[blocks + line, rows].astype(F32)

            pan_z_send[k, rows] = pan_total[rows, :].astype(BF16)
            pan_z(k, h, row, slot).start()

    far = lines - 2
    last = lines - 1

    def ms_far_to_twin(p):
        for i, part in enumerate(ms_twin_parts(2 * p)):
            ms_y_send[2 * p + i] = part.astype(BF16)
        ms_y(2 * p).start()
        ms_y(2 * p + 1).start()

    def ms_far_onward(p):
        ms_own_parts(2 * p)
        ms_onward(2 * p, 0)
        ms_onward(2 * p + 1, 1)

    each(0, far // 2, ms_far_to_twin)
    parts = ms_twin_parts(far)
    near_ms_send[...] = parts[0].astype(BF16)
    ms_hold[...] = parts[1]
    near_ms.start()
    ms_own_parts(far)
    ms_z_send[far] = ms_total[0].astype(BF16)
    ms_z(far, near_row, pair).start()
    ms_mine[...] = ms_total[1]
    each(0, far, pan_to_twin)
    near_ms.wait_recv()
    ms_y_send[last] = (ms_hold[...] + near_ms_recv[...].astype(F32)).astype(BF16)
    ms_y(last).start()
    each(0, far // 2, ms_far_onward)
    each(far, lines, pan_to_twin)
    each(0, far, pan_onward)

    spot = (iota((coarse_cols, TC), 1).astype(F32) - 1.5) * 0.25 + 2.0
    tap = iota((coarse_cols, TC), 0) + 2
    up_cols[0:coarse_cols, :] = cubic_weight(spot - tap.astype(F32)).astype(BF16)
    tap = iota((LANES, TC), 0) % 2 + jnp.where(c == 0, coarse_cols + 2, 0)
    up_cols[coarse_cols : coarse_cols + LANES, :] = cubic_weight(spot - tap.astype(F32)).astype(BF16)

    ms_y(last).wait_recv()
    ms_mine[...] += ms_y_recv[last].astype(F32)

    def ms_arrived(slot, carry):
        ms_z(0, m, slot).wait_recv()
        ms_mine[...] += ms_z_recv[slot].astype(F32)
        return carry

    lax.fori_loop(0, blocks, ms_arrived, 0)
    for load in late_loads:
        load.wait()
    values = [ms_mine[b * coarse_rows : (b + 1) * coarse_rows, :] for b in range(bands)]
    synthetic = sum(synth_ref[b] * values[b] for b in range(bands))
    spot = iota((coarse_rows, LANES), 1) // 2
    edges = jnp.zeros((coarse_rows, LANES), F32)
    tops, bottoms = [], []
    for b in range(bands):
        result = values[b] - gain_ref[b] * synthetic
        for k in range(bands):
            result = result + mix_ref[b, k] * values[k]
        window[b] = result.astype(BF16)
        moved = pltpu.roll(result, jnp.where(c == 0, 2 * b + 2, 2 * b), 1)
        edges = jnp.where(spot == b, moved, edges)
        tops.append(result[0:2, :])
        bottoms.append(result[coarse_rows - 2 : coarse_rows, :])
    edge_own[...] = edges.astype(BF16)
    rim_send[0] = jnp.concatenate(tops, axis=0).astype(BF16)
    rim_send[1] = jnp.concatenate(bottoms, axis=0).astype(BF16)
    edge_send[0] = jnp.concatenate([edges[0:2, :]] * bands, axis=0).astype(BF16)
    bottom = edges[coarse_rows - 2 : coarse_rows, :]
    edge_send[1] = jnp.concatenate([bottom] * bands, axis=0).astype(BF16)

    has_above, has_below = m > 0, m < n - 1

    def halo_copy(k, src, dst, row, col):
        return remote(src, dst, halo_ss.at[k], halo_rs.at[k], row, col)

    across_copy = halo_copy(0, edge_own, edge_all, m, other)
    up_copies = [
        halo_copy(1, rim_send.at[0], rim_recv.at[1], m - 1, c),
        halo_copy(2, edge_send.at[0], edge_recv.at[1], m - 1, other),
    ]
    down_copies = [
        halo_copy(3, rim_send.at[1], rim_recv.at[0], m + 1, c),
        halo_copy(4, edge_send.at[1], edge_recv.at[0], m + 1, other),
    ]
    across_copy.start()

    @pl.when(has_above)
    def _():
        for copy in up_copies:
            copy.start()

    @pl.when(has_below)
    def _():
        for copy in down_copies:
            copy.start()

    pan_onward(far)
    pan_total[...] = pan_part(m)
    across_copy.wait()

    edges = edge_all[...]
    spot = iota(edges.shape, 1) // 2
    source = jnp.concatenate(
        [
            jnp.concatenate(
                [window[b], jnp.where(spot == b, edges, jnp.zeros_like(edges))], axis=1
            )
            for b in range(bands)
        ],
        axis=0,
    )
    across[0 : bands * coarse_rows, :] = jnp.dot(
        source, up_cols[...], preferred_element_type=F32
    ).astype(BF16)
    for b in range(bands):
        own = slice(b * coarse_rows, (b + 1) * coarse_rows)
        mixed[b, PACK : TR - PACK, :] = jnp.dot(
            up_rows[PACK : TR - PACK, 0:coarse_rows],
            across[own, :],
            preferred_element_type=F32,
        ).astype(BF16)

    @pl.when(has_above)
    def _():
        for copy in up_copies:
            copy.wait_send()
        for copy in down_copies:
            copy.wait_recv()

    @pl.when(has_below)
    def _():
        for copy in down_copies:
            copy.wait_send()
        for copy in up_copies:
            copy.wait_recv()

    blank = jnp.zeros((2 * bands, LANES), BF16)

    @pl.when(jnp.logical_not(has_above))
    def _():
        rim_recv[0] = blank
        edge_recv[0] = blank

    @pl.when(jnp.logical_not(has_below))
    def _():
        rim_recv[1] = blank
        edge_recv[1] = blank

    spot = iota((2 * bands, LANES), 1) // 2
    mine = spot == iota((2 * bands, LANES), 0) // 2
    source = jnp.concatenate(
        [
            jnp.concatenate([rim_recv[i], jnp.where(mine, edge_recv[i], blank)], axis=1)
            for i in range(2)
        ],
        axis=0,
    )
    rims = jnp.dot(source, up_cols[...], preferred_element_type=F32).astype(BF16)
    outer = jnp.concatenate([up_rows[0:PACK, :], up_rows[TR - PACK : TR, :]], axis=0)
    column = iota(outer.shape, 1)
    owner_band = (column - coarse_rows) % (2 * bands) // 2
    for b in range(bands):
        weight = jnp.where((column < coarse_rows) | (owner_band == b), outer, jnp.zeros_like(outer))
        own = slice(b * coarse_rows, (b + 1) * coarse_rows)
        ends = jnp.dot(
            weight, jnp.concatenate([across[own, :], rims], axis=0), preferred_element_type=F32
        ).astype(BF16)
        mixed[b, 0:PACK, :] = ends[0:PACK, :]
        mixed[b, TR - PACK : TR, :] = ends[PACK : 2 * PACK, :]

    store = pltpu.make_async_copy(mixed, mixed_hbm, load_sem.at[9])
    store.start()
    for h in range(HALVES):
        rows = slice(h * part_rows, (h + 1) * part_rows)
        pan_y(last, h).wait_recv()
        pan_total[rows, :] += pan_y_recv[last, rows].astype(F32)

        def pan_arrived(slot, carry):
            pan_z(0, h, m, slot).wait_recv()
            pan_total[rows, :] += pan_z_recv[slot, rows].astype(F32)
            return carry

        lax.fori_loop(0, blocks, pan_arrived, 0)

    def ms_y_sent(k, carry):
        ms_y(k).wait_send()
        return carry

    def pan_y_sent(k, carry):
        for h in range(HALVES):
            pan_y(k, h).wait_send()
        return carry

    def z_sent(k, carry):
        ms_z(k, m, 0).wait_send()
        for h in range(HALVES):
            pan_z(k, h, m, 0).wait_send()
        return carry

    near_ms.wait_send()
    lax.fori_loop(0, far, ms_y_sent, 0)
    ms_y(last).wait_send()
    lax.fori_loop(0, lines, pan_y_sent, 0)
    lax.fori_loop(0, lines - 1, z_sent, 0)
    store.wait()


def local(
    pan_blocks,
    ms_blocks,
    send_list,
    tile_list,
    row_grid,
    col_grid,
    band_mix,
    band_gain,
    synth_weight,
):
    n = lax.axis_size("mrow")
    lines = n // 2
    own_blocks, size, _ = pan_blocks.shape
    _, coarse_size, coarse_width = ms_blocks.shape
    capacity = tile_list.shape[1] // n
    bands = band_gain.shape[0]
    coarse_rows, coarse_cols = TR // 4, TC // 4
    table_rows = pl.cdiv(2 + pl.cdiv(n * KR * KC, LANES), 8) * 8
    vmem = pl.BlockSpec(memory_space=pltpu.VMEM)
    hbm = pl.BlockSpec(memory_space=pl.ANY)
    dma = pltpu.SemaphoreType.DMA
    slots = lines // 2 + lines

    def ms_slots(count):
        return pltpu.VMEM((count, bands * coarse_rows, coarse_cols), BF16)

    def pan_slots(count):
        return pltpu.VMEM((count, TR, TC), BF16)

    mixed, pan_map = pl.pallas_call(
        functools.partial(mapping, capacity, col_grid.shape[1]),
        out_shape=(
            jax.ShapeDtypeStruct((bands, TR, TC), BF16),
            jax.ShapeDtypeStruct((TR, TC), F32),
        ),
        in_specs=[hbm] * 8,
        out_specs=(hbm, vmem),
        scratch_shapes=[
            pltpu.VMEM(send_list.shape, I32),
            pltpu.VMEM((1, row_grid.shape[0]), F32),
            pltpu.VMEM(col_grid.shape, F32),
            pltpu.SMEM(band_mix.shape, F32),
            pltpu.SMEM(band_gain.shape, F32),
            pltpu.SMEM(synth_weight.shape, F32),
            pltpu.VMEM(pan_blocks.shape, BF16),
            pltpu.VMEM(ms_blocks.shape, BF16),
            pltpu.VMEM((own_blocks + 1, size, size), BF16),
            pltpu.VMEM((own_blocks + 1, coarse_size, coarse_width), BF16),
            pltpu.VMEM((table_rows, LANES), I32),
            pltpu.SMEM((table_rows, LANES), I32),
            pltpu.VMEM((8, LANES), F32),
            pltpu.VMEM((2, n, 8, LANES), F32),
            ms_slots(lines),
            ms_slots(lines),
            pan_slots(lines),
            pan_slots(lines),
            ms_slots(lines - 1),
            ms_slots(slots),
            pan_slots(lines - 1),
            pan_slots(slots),
            pltpu.VMEM((bands * coarse_rows, coarse_cols), BF16),
            pltpu.VMEM((bands * coarse_rows, coarse_cols), BF16),
            pltpu.VMEM((2, bands * coarse_rows, coarse_cols), F32),
            pltpu.VMEM((bands * coarse_rows, coarse_cols), F32),
            pltpu.VMEM((bands * coarse_rows, coarse_cols), F32),
            pltpu.VMEM((bands, coarse_rows, coarse_cols), BF16),
            pltpu.VMEM((2, 2 * bands, LANES), BF16),
            pltpu.VMEM((2, 2 * bands, LANES), BF16),
            pltpu.VMEM((2, 2 * bands, LANES), BF16),
            pltpu.VMEM((2, 2 * bands, LANES), BF16),
            pltpu.VMEM((coarse_rows, LANES), BF16),
            pltpu.VMEM((coarse_rows, LANES), BF16),
            pltpu.VMEM((coarse_cols + LANES, TC), BF16),
            pltpu.VMEM((TR, coarse_rows + 4 * bands), BF16),
            pltpu.VMEM((bands * coarse_rows, TC), BF16),
            pltpu.VMEM((bands, TR, TC), BF16),
            dma((10,)),
            dma((2, n)),
            dma((2, n)),
            dma((lines,)),
            dma((lines,)),
            dma((lines, HALVES)),
            dma((lines, HALVES)),
            dma((lines - 1,)),
            dma((slots,)),
            dma((lines - 1, HALVES)),
            dma((slots, HALVES)),
            dma,
            dma,
            dma((5,)),
            dma((5,)),
        ],
        compiler_params=pltpu.CompilerParams(
            collective_id=0, has_side_effects=True, vmem_limit_bytes=60 * 1024 * 1024
        ),
        name="mapping",
    )(
        send_list,
        row_grid[None, :],
        col_grid,
        pan_blocks,
        ms_blocks,
        band_mix,
        band_gain,
        synth_weight,
    )
    detail = band_gain[:, None, None] * pan_map[None]
    return (mixed.astype(F32) + detail).astype(BF16)


def solution(mesh):
    return jax.shard_map(
        local,
        mesh=mesh,
        in_specs=(
            P(("scene", "mrow", "mcol"), None, None),
            P(("scene", "mrow", "mcol"), None, None),
            P(None, ("scene", "mrow", "mcol")),
            P(None, ("scene", "mrow", "mcol")),
            P(("scene", "mrow")),
            P(("scene", "mrow"), "mcol"),
            P(),
            P(),
            P(),
        ),
        out_specs=P(None, ("scene", "mrow"), "mcol"),
        check_vma=False,
    )
```

```python
import functools

import jax
import jax.numpy as jnp
from jax import lax
from jax.experimental import pallas as pl
from jax.experimental.pallas import tpu as pltpu
from jax.sharding import PartitionSpec as P

GRID = 64
TR = 128
TC = 512
KR = 2
KC = 5
LANES = 128
PACK = 16
HALVES = 2
MESH = pl.DeviceIdType.MESH
F32 = jnp.float32
BF16 = jnp.bfloat16
I32 = jnp.int32


def cubic_weight(offset):
    outer = jnp.maximum(2.0 - jnp.abs(offset), 0.0)
    shifted = outer - 1.0
    inner = jnp.maximum(shifted, 0.0)
    return outer * outer * (0.5 * shifted) + inner * inner * (1.0 - 2.0 * inner)


def iota(shape, dim):
    return lax.broadcasted_iota(I32, shape, dim)


def row_coord(nodes, position, offset):
    first = position < GRID
    a = jnp.where(first, nodes[:, 0:1], nodes[:, 1:2])
    b = jnp.where(first, nodes[:, 1:2], nodes[:, 2:3])
    within = (jnp.where(first, position, position - GRID).astype(F32) + offset) / GRID
    return a + (b - a) * within


def col_coord(nodes, after, is_last, count, position, offset):
    segment = position // GRID
    coord = jnp.zeros(position.shape, F32)
    for s in range(count):
        left, shift = nodes[:, s : s + 1], s * GRID
        if s + 1 < count:
            right = nodes[:, s + 1 : s + 2]
        else:
            right = jnp.where(is_last, left, after)
            left = jnp.where(is_last, nodes[:, s - 1 : s], left)
            shift = jnp.where(is_last, shift - GRID, shift)
        within = ((position - shift).astype(F32) + offset) / GRID
        coord = jnp.where(segment == s, left + (right - left) * within, coord)
    return coord


def spread(x, origin, size):
    base = jnp.floor(x)
    shape = (PACK, x.shape[1])
    taps = [
        jnp.broadcast_to(cubic_weight(x - (base + t)), shape).astype(BF16)
        for t in (-1.0, 0.0, 1.0, 2.0)
    ]
    groups = size // PACK
    first = base - 1.0 - origin
    group = jnp.floor(first * (1.0 / PACK))
    away = (iota(shape, 0).astype(F32) - (first - group * PACK)).astype(BF16)
    group = jnp.broadcast_to(jnp.clip(group, -2.0, groups + 1.0), shape).astype(BF16)
    none = jnp.zeros(shape, BF16)
    low, high = none, none
    for t in range(4):
        low = jnp.where(away == BF16(t), taps[t], low)
        high = jnp.where(away == BF16(t - PACK), taps[t], high)
    here = [group == BF16(g) for g in range(-1, groups)]
    return jnp.concatenate(
        [jnp.where(here[g + 1], low, jnp.where(here[g], high, none)) for g in range(groups)],
        axis=0,
    )


def mapping(
    capacity,
    col_nodes,
    send_hbm,
    row_hbm,
    col_hbm,
    pan_hbm,
    ms_hbm,
    mix_hbm,
    gain_hbm,
    synth_hbm,
    mixed_hbm,
    pan_hbm_out,
    send_ref,
    row_ref,
    col_ref,
    mix_ref,
    gain_ref,
    synth_ref,
    pan_ref,
    ms_ref,
    pan_sum,
    ms_sum,
    table_ref,
    table,
    nodes_ref,
    nodes_all,
    ms_y_send,
    ms_y_recv,
    pan_y_send,
    pan_y_recv,
    ms_z_send,
    ms_z_recv,
    pan_z_send,
    pan_z_recv,
    near_ms_send,
    near_ms_recv,
    pan_total,
    ms_total,
    ms_hold,
    ms_mine,
    pan_mine,
    window,
    rim_send,
    rim_recv,
    edge_send,
    edge_recv,
    edge_own,
    edge_all,
    up_cols,
    up_rows,
    across,
    mixed,
    load_sem,
    nodes_ss,
    nodes_rs,
    ms_y_ss,
    ms_y_rs,
    pan_y_ss,
    pan_y_rs,
    ms_z_ss,
    ms_z_rs,
    pan_z_ss,
    pan_z_rs,
    near_ss,
    near_rs,
    halo_ss,
    halo_rs,
):
    n = lax.axis_size("mrow")
    lines = n // 2
    blocks = lines // 2
    scene = lax.axis_index("scene")
    m = lax.axis_index("mrow")
    c = lax.axis_index("mcol")
    z, y = m // 2, m % 2
    twin = z * 2 + (1 - y)
    other = 1 - c
    pair = z // 2
    partner = pair * 2 + (1 - z % 2)
    own_blocks, size, _ = pan_ref.shape
    _, coarse_size, coarse_width = ms_ref.shape
    cells = n * KR * KC
    bands = mixed.shape[0]
    coarse_rows = TR // 4
    coarse_cols = TC // 4
    part_rows = TR // HALVES
    first_col = c * KC
    is_last = c == lax.axis_size("mcol") - 1

    def at(row, col):
        return (scene, row, col)

    def remote(src, dst, ss, rs, row, col):
        return pltpu.make_async_remote_copy(
            src_ref=src,
            dst_ref=dst,
            send_sem=ss,
            recv_sem=rs,
            device_id=at(row, col),
            device_id_type=MESH,
        )

    barrier = pltpu.get_barrier_semaphore()

    def greet(k, carry):
        row = lax.rem(m + k, n)
        pl.semaphore_signal(barrier, inc=1, device_id=at(row, c), device_id_type=MESH)
        pl.semaphore_signal(barrier, inc=1, device_id=at(row, other), device_id_type=MESH)
        return carry

    def greet_all():
        pl.semaphore_signal(barrier, inc=1, device_id=at(m, other), device_id_type=MESH)
        lax.fori_loop(1, n, greet, 0)

    loads = [
        pltpu.make_async_copy(src, dst, load_sem.at[k])
        for k, (src, dst) in enumerate(
            (
                (row_hbm, row_ref),
                (col_hbm, col_ref),
                (send_hbm, send_ref),
                (ms_hbm, ms_ref),
                (pan_hbm, pan_ref),
                (mix_hbm, mix_ref),
                (gain_hbm, gain_ref),
                (synth_hbm, synth_ref),
            )
        )
    ]
    row_load, col_load, send_load, ms_load, pan_load, *late_loads = loads
    row_load.start()
    col_load.start()
    greet_all()
    for load in loads[2:]:
        load.start()

    nodes_ref[...] = jnp.zeros_like(nodes_ref)
    row_load.wait()
    col_load.wait()
    nodes_ref[0:1, 0 : row_ref.shape[1]] = row_ref[...]
    nodes_ref[1:2, 0 : col_ref.shape[1]] = col_ref[...]
    nodes_all[c, m] = nodes_ref[...]
    pl.semaphore_wait(barrier, 2 * n - 1)

    def nodes_copy(slot_row, slot_col, row, col):
        return remote(
            nodes_ref,
            nodes_all.at[slot_col, slot_row],
            nodes_ss.at[col, row],
            nodes_rs.at[slot_col, slot_row],
            row,
            col,
        )

    def send_nodes(k, carry):
        row = lax.rem(m + k, n)
        nodes_copy(m, c, row, c).start()
        nodes_copy(m, c, row, other).start()
        return carry

    lax.fori_loop(1, n, send_nodes, 0)
    nodes_copy(m, c, m, other).start()
    send_load.wait()

    square = (own_blocks, own_blocks)
    wide = (own_blocks, LANES)
    owner = send_ref[0:1, :] // capacity
    key_row = (owner * KR + send_ref[1:2, :]) * KC + send_ref[2:3, :] - first_col
    key_row = jnp.broadcast_to(key_row, square)
    diagonal = iota(square, 0) == iota(square, 1)
    key_col = jnp.sum(jnp.where(diagonal, key_row, 0), axis=1, keepdims=True)
    same = key_row == key_col
    before = (key_row < key_col) | (same & (iota(square, 1) < iota(square, 0)))
    rank = jnp.sum(jnp.where(before, 1, 0), axis=1, keepdims=True)
    joined = jnp.sum(jnp.where(before & same, 1, 0), axis=1, keepdims=True)
    hit = rank == iota(wide, 1)
    order = jnp.sum(jnp.where(hit, iota(wide, 0), 0), axis=0, keepdims=True)
    keep = jnp.sum(jnp.where(hit & (joined > 0), 1, 0), axis=0, keepdims=True)
    table_ref[0:1, :] = order
    table_ref[1:2, :] = keep
    for g in range(pl.cdiv(cells, LANES)):
        cell = iota(wide, 1) + g * LANES
        ends = jnp.sum(jnp.where(key_col <= cell, 1, 0), axis=0, keepdims=True)
        count = jnp.sum(jnp.where(key_col == cell, 1, 0), axis=0, keepdims=True)
        table_ref[2 + g : 3 + g, :] = jnp.where(count > 0, ends, 0)
    table_copy = pltpu.make_async_copy(table_ref, table, load_sem.at[8])
    table_copy.start()

    column = iota(up_rows.shape, 1)
    rim = column - coarse_rows
    tap = jnp.where(
        column < coarse_rows, column + 2, rim % 2 + jnp.where(rim < 2 * bands, 0, coarse_rows + 2)
    )
    spot = (iota(up_rows.shape, 0).astype(F32) - 1.5) * 0.25 + 2.0
    up_rows[...] = cubic_weight(spot - tap.astype(F32)).astype(BF16)
    pan_sum[0] = jnp.zeros((size, size), BF16)
    ms_sum[0] = jnp.zeros((coarse_size, coarse_width), BF16)
    table_copy.wait()

    def running(source, sums):
        def step(p, total):
            total = total * table[1, p].astype(F32) + source[table[0, p]].astype(F32)
            sums[p + 1] = total.astype(BF16)
            return total

        start = jnp.zeros(source.shape[1:], F32)
        lax.fori_loop(0, own_blocks, step, start, unroll=2)

    ms_load.wait()
    running(ms_ref, ms_sum)
    pan_load.wait()
    running(pan_ref, pan_sum)

    def wait_nodes(k, carry):
        row = lax.rem(m + k, n)
        nodes_copy(row, c, row, c).wait()
        nodes_copy(row, other, row, other).wait()
        return carry

    lax.fori_loop(1, n, wait_nodes, 0)
    nodes_copy(m, other, m, other).wait()

    def cell_of(sums, tile, row, col):
        cell = (tile * KR + row) * KC + col
        return sums[table[2 + cell // LANES, cell % LANES]]

    def stacked(sums, tile, col):
        return jnp.concatenate([cell_of(sums, tile, row, col) for row in range(KR)], axis=0)

    def ms_part(tile):
        row_nodes, nodes = nodes_all[c, tile, 0:1], nodes_all[c, tile, 1:2]
        after = nodes_all[1, tile, 1:2, 0:1]
        x_ms = col_coord(
            nodes, after, is_last, col_nodes, 4 * iota((1, coarse_cols), 1) + 1, 0.5
        )
        x_ms = (x_ms - 1.5) * 0.25
        col = spread(x_ms, (first_col * coarse_size).astype(F32), KC * coarse_size)
        spots = (row_coord(row_nodes, 4 * iota((coarse_rows, 1), 0) + 1, 0.5) - 1.5) * 0.25
        taps = iota((coarse_rows, KR * coarse_size), 1).astype(F32)
        weight = cubic_weight(spots - taps).astype(BF16)
        rows = [
            jnp.dot(weight, stacked(ms_sum, tile, k), preferred_element_type=F32).astype(BF16)
            for k in range(KC)
        ]
        by_band = [
            jnp.concatenate(
                [row[:, b * coarse_size : (b + 1) * coarse_size] for row in rows], axis=1
            )
            for b in range(bands)
        ]
        return jnp.dot(jnp.concatenate(by_band, axis=0), col, preferred_element_type=F32)

    def pan_part(tile):
        row_nodes, nodes = nodes_all[c, tile, 0:1], nodes_all[c, tile, 1:2]
        after = nodes_all[1, tile, 1:2, 0:1]
        x_pan = col_coord(nodes, after, is_last, col_nodes, iota((1, TC), 1), 0.0)
        col = spread(x_pan, (first_col * size).astype(F32), KC * size)
        row = spread(row_coord(row_nodes, iota((1, TR), 1), 0.0), 0.0, KR * size)
        rows = []
        for k in range(0, KC, 2):
            source = jnp.concatenate(
                [stacked(pan_sum, tile, j) for j in range(k, min(k + 2, KC))], axis=1
            )
            rows.append(
                lax.dot_general(
                    row, source, (((0,), (0,)), ((), ())), preferred_element_type=F32
                ).astype(BF16)
            )
        return jnp.dot(jnp.concatenate(rows, axis=1), col, preferred_element_type=F32)

    def line_of(k):
        up = lax.rem(pair * 2 + 2 + k, lines)
        down = lax.rem(pair * 2 + lines - 1 - k, lines)
        far = jnp.where(pair % 2 == 0, down, up)
        return jnp.where(k < lines - 2, far, jnp.where(k == lines - 2, partner, z))

    def ms_y(k):
        return remote(ms_y_send.at[k], ms_y_recv.at[k], ms_y_ss.at[k], ms_y_rs.at[k], twin, c)

    def pan_y(k, h):
        part = pl.ds(h * part_rows, part_rows)
        return remote(
            pan_y_send.at[k, part],
            pan_y_recv.at[k, part],
            pan_y_ss.at[k, h],
            pan_y_rs.at[k, h],
            twin,
            c,
        )

    def route(line):
        far = line // 2 != pair
        above = line // 2 > pair
        lower = z % 2 == 0
        inner = far & jnp.logical_xor(above, lower)
        outer = far & jnp.logical_not(jnp.logical_xor(above, lower))
        target = jnp.where(outer, partner, line)
        slot = jnp.where(outer, blocks + line, pair)
        return inner, target * 2 + y, slot

    def ms_z(k, row, slot):
        return remote(
            ms_z_send.at[k], ms_z_recv.at[slot], ms_z_ss.at[k], ms_z_rs.at[slot], row, c
        )

    def pan_z(k, h, row, slot):
        part = pl.ds(h * part_rows, part_rows)
        return remote(
            pan_z_send.at[k, part],
            pan_z_recv.at[slot, part],
            pan_z_ss.at[k, h],
            pan_z_rs.at[slot, h],
            row,
            c,
        )

    def each(first, last, step):
        if last - first == 1:
            step(first)
            return

        def body(k, carry):
            step(k)
            return carry

        lax.fori_loop(first, last, body, 0)

    near_row = partner * 2 + y

    near_ms = remote(near_ms_send, near_ms_recv, near_ss, near_rs, near_row, c)

    def ms_twin_parts(k):
        return [ms_part(line_of(k + i) * 2 + 1 - y) for i in range(2)]

    def pan_twin_part(k):
        return pan_part(line_of(k) * 2 + 1 - y)

    def pan_to_twin(k):
        pan_y_send[k] = pan_twin_part(k).astype(BF16)
        for h in range(HALVES):
            pan_y(k, h).start()

    def ms_own_parts(k):
        parts = [ms_part(line_of(k + i) * 2 + y) for i in range(2)]
        for i, part in enumerate(parts):
            ms_total[i] = part

    def ms_onward(k, i):
        line = line_of(k)
        inner, row, slot = route(line)
        ms_y(k).wait_recv()
        ms_total[i] += ms_y_recv[k].astype(F32)

        @pl.when(inner)
        def _():
            ms_z(0, row, blocks + line).wait_recv()
            ms_total[i] += ms_z_recv[blocks + line].astype(F32)

        ms_z_send[k] = ms_total[i].astype(BF16)
        ms_z(k, row, slot).start()

    def pan_own_part(k):
        pan_total[...] = pan_part(line_of(k) * 2 + y)

    def pan_forward(k):
        line = line_of(k)
        inner, row, slot = route(line)
        for h in range(HALVES):
            rows = slice(h * part_rows, (h + 1) * part_rows)
            pan_y(k, h).wait_recv()
            pan_total[rows, :] += pan_y_recv[k, rows].astype(F32)

            @pl.when(inner)
            def _():
                pan_z(0, h, row, blocks + line).wait_recv()
                pan_total[rows, :] += pan_z_recv[blocks + line, rows].astype(F32)

            pan_z_send[k, rows] = pan_total[rows, :].astype(BF16)
            pan_z(k, h, row, slot).start()

    def pan_onward(k):
        pan_own_part(k)
        pan_forward(k)

    far = lines - 2
    last = lines - 1

    def ms_far_to_twin(p):
        for i, part in enumerate(ms_twin_parts(2 * p)):
            ms_y_send[2 * p + i] = part.astype(BF16)
        ms_y(2 * p).start()
        ms_y(2 * p + 1).start()

    def ms_far_onward(p):
        ms_own_parts(2 * p)
        ms_onward(2 * p, 0)
        ms_onward(2 * p + 1, 1)

    each(0, far // 2, ms_far_to_twin)
    parts = ms_twin_parts(far)
    near_ms_send[...] = parts[0].astype(BF16)
    ms_hold[...] = parts[1]
    near_ms.start()
    ms_own_parts(far)
    ms_z_send[far] = ms_total[0].astype(BF16)
    ms_z(far, near_row, pair).start()
    ms_mine[...] = ms_total[1]
    each(0, far, pan_to_twin)
    near_ms.wait_recv()
    ms_y_send[last] = (ms_hold[...] + near_ms_recv[...].astype(F32)).astype(BF16)
    ms_y(last).start()
    spot = (iota((coarse_cols, TC), 1).astype(F32) - 1.5) * 0.25 + 2.0
    tap = iota((coarse_cols, TC), 0) + 2
    up_cols[0:coarse_cols, :] = cubic_weight(spot - tap.astype(F32)).astype(BF16)
    tap = iota((LANES, TC), 0) % 2 + jnp.where(c == 0, coarse_cols + 2, 0)
    up_cols[coarse_cols : coarse_cols + LANES, :] = cubic_weight(spot - tap.astype(F32)).astype(BF16)

    each(0, far // 2, ms_far_onward)
    each(far, lines, pan_to_twin)
    each(0, far - 1, pan_onward)
    pan_mine[...] = pan_part(m)
    pan_own_part(far - 1)

    has_above, has_below = m > 0, m < n - 1

    def halo_copy(k, src, dst, row, col):
        return remote(src, dst, halo_ss.at[k], halo_rs.at[k], row, col)

    across_copy = halo_copy(0, edge_own, edge_all, m, other)
    up_copies = [
        halo_copy(1, rim_send.at[0], rim_recv.at[1], m - 1, c),
        halo_copy(2, edge_send.at[0], edge_recv.at[1], m - 1, other),
    ]
    down_copies = [
        halo_copy(3, rim_send.at[1], rim_recv.at[0], m + 1, c),
        halo_copy(4, edge_send.at[1], edge_recv.at[0], m + 1, other),
    ]
    def ms_finish():
        ms_y(last).wait_recv()
        ms_mine[...] += ms_y_recv[last].astype(F32)

        def ms_arrived(slot, carry):
            ms_z(0, m, slot).wait_recv()
            ms_mine[...] += ms_z_recv[slot].astype(F32)
            return carry

        lax.fori_loop(0, blocks, ms_arrived, 0)
        values = [ms_mine[b * coarse_rows : (b + 1) * coarse_rows, :] for b in range(bands)]
        synthetic = sum(synth_ref[b] * values[b] for b in range(bands))
        spot = iota((coarse_rows, LANES), 1) // 2
        edges = jnp.zeros((coarse_rows, LANES), F32)
        tops, bottoms = [], []
        for b in range(bands):
            result = values[b] - gain_ref[b] * synthetic
            for k in range(bands):
                result = result + mix_ref[b, k] * values[k]
            window[b] = result.astype(BF16)
            moved = pltpu.roll(result, jnp.where(c == 0, 2 * b + 2, 2 * b), 1)
            edges = jnp.where(spot == b, moved, edges)
            tops.append(result[0:2, :])
            bottoms.append(result[coarse_rows - 2 : coarse_rows, :])
        edge_own[...] = edges.astype(BF16)
        rim_send[0] = jnp.concatenate(tops, axis=0).astype(BF16)
        rim_send[1] = jnp.concatenate(bottoms, axis=0).astype(BF16)
        edge_send[0] = jnp.concatenate([edges[0:2, :]] * bands, axis=0).astype(BF16)
        bottom = edges[coarse_rows - 2 : coarse_rows, :]
        edge_send[1] = jnp.concatenate([bottom] * bands, axis=0).astype(BF16)

        across_copy.start()

        @pl.when(has_above)
        def _():
            for copy in up_copies:
                copy.start()

        @pl.when(has_below)
        def _():
            for copy in down_copies:
                copy.start()

    early = route(line_of(far - 1))[0]
    for load in late_loads:
        load.wait()
    pl.when(early)(ms_finish)
    pan_forward(far - 1)
    pan_own_part(far)
    pl.when(jnp.logical_not(early))(ms_finish)
    pan_forward(far)
    across_copy.wait()

    edges = edge_all[...]
    spot = iota(edges.shape, 1) // 2
    source = jnp.concatenate(
        [
            jnp.concatenate(
                [window[b], jnp.where(spot == b, edges, jnp.zeros_like(edges))], axis=1
            )
            for b in range(bands)
        ],
        axis=0,
    )
    across[0 : bands * coarse_rows, :] = jnp.dot(
        source, up_cols[...], preferred_element_type=F32
    ).astype(BF16)
    for b in range(bands):
        own = slice(b * coarse_rows, (b + 1) * coarse_rows)
        mixed[b, PACK : TR - PACK, :] = jnp.dot(
            up_rows[PACK : TR - PACK, 0:coarse_rows],
            across[own, :],
            preferred_element_type=F32,
        ).astype(BF16)

    @pl.when(has_above)
    def _():
        for copy in up_copies:
            copy.wait_send()
        for copy in down_copies:
            copy.wait_recv()

    @pl.when(has_below)
    def _():
        for copy in down_copies:
            copy.wait_send()
        for copy in up_copies:
            copy.wait_recv()

    blank = jnp.zeros((2 * bands, LANES), BF16)

    @pl.when(jnp.logical_not(has_above))
    def _():
        rim_recv[0] = blank
        edge_recv[0] = blank

    @pl.when(jnp.logical_not(has_below))
    def _():
        rim_recv[1] = blank
        edge_recv[1] = blank

    spot = iota((2 * bands, LANES), 1) // 2
    mine = spot == iota((2 * bands, LANES), 0) // 2
    source = jnp.concatenate(
        [
            jnp.concatenate([rim_recv[i], jnp.where(mine, edge_recv[i], blank)], axis=1)
            for i in range(2)
        ],
        axis=0,
    )
    rims = jnp.dot(source, up_cols[...], preferred_element_type=F32).astype(BF16)
    outer = jnp.concatenate([up_rows[0:PACK, :], up_rows[TR - PACK : TR, :]], axis=0)
    column = iota(outer.shape, 1)
    owner_band = (column - coarse_rows) % (2 * bands) // 2
    for b in range(bands):
        weight = jnp.where((column < coarse_rows) | (owner_band == b), outer, jnp.zeros_like(outer))
        own = slice(b * coarse_rows, (b + 1) * coarse_rows)
        ends = jnp.dot(
            weight, jnp.concatenate([across[own, :], rims], axis=0), preferred_element_type=F32
        ).astype(BF16)
        mixed[b, 0:PACK, :] = ends[0:PACK, :]
        mixed[b, TR - PACK : TR, :] = ends[PACK : 2 * PACK, :]

    store = pltpu.make_async_copy(mixed, mixed_hbm, load_sem.at[9])
    store.start()
    pan_stores = []
    for h in range(HALVES):
        rows = slice(h * part_rows, (h + 1) * part_rows)
        pan_y(last, h).wait_recv()
        pan_mine[rows, :] += pan_y_recv[last, rows].astype(F32)

        def pan_arrived(slot, carry):
            pan_z(0, h, m, slot).wait_recv()
            pan_mine[rows, :] += pan_z_recv[slot, rows].astype(F32)
            return carry

        lax.fori_loop(0, blocks, pan_arrived, 0)
        part = pl.ds(h * part_rows, part_rows)
        pan_stores.append(
            pltpu.make_async_copy(pan_mine.at[part], pan_hbm_out.at[part], load_sem.at[10 + h])
        )
        pan_stores[-1].start()

    def ms_y_sent(k, carry):
        ms_y(k).wait_send()
        return carry

    def pan_y_sent(k, carry):
        for h in range(HALVES):
            pan_y(k, h).wait_send()
        return carry

    def z_sent(k, carry):
        ms_z(k, m, 0).wait_send()
        for h in range(HALVES):
            pan_z(k, h, m, 0).wait_send()
        return carry

    near_ms.wait_send()
    lax.fori_loop(0, far, ms_y_sent, 0)
    ms_y(last).wait_send()
    lax.fori_loop(0, lines, pan_y_sent, 0)
    lax.fori_loop(0, lines - 1, z_sent, 0)
    store.wait()
    for pan_store in pan_stores:
        pan_store.wait()


def local(
    pan_blocks,
    ms_blocks,
    send_list,
    tile_list,
    row_grid,
    col_grid,
    band_mix,
    band_gain,
    synth_weight,
):
    n = lax.axis_size("mrow")
    lines = n // 2
    own_blocks, size, _ = pan_blocks.shape
    _, coarse_size, coarse_width = ms_blocks.shape
    capacity = tile_list.shape[1] // n
    bands = band_gain.shape[0]
    coarse_rows, coarse_cols = TR // 4, TC // 4
    table_rows = pl.cdiv(2 + pl.cdiv(n * KR * KC, LANES), 8) * 8
    hbm = pl.BlockSpec(memory_space=pl.ANY)
    dma = pltpu.SemaphoreType.DMA
    slots = lines // 2 + lines

    def ms_slots(count):
        return pltpu.VMEM((count, bands * coarse_rows, coarse_cols), BF16)

    def pan_slots(count):
        return pltpu.VMEM((count, TR, TC), BF16)

    mixed, pan_map = pl.pallas_call(
        functools.partial(mapping, capacity, col_grid.shape[1]),
        out_shape=(
            jax.ShapeDtypeStruct((bands, TR, TC), BF16),
            jax.ShapeDtypeStruct((TR, TC), F32),
        ),
        in_specs=[hbm] * 8,
        out_specs=(hbm, hbm),
        scratch_shapes=[
            pltpu.VMEM(send_list.shape, I32),
            pltpu.VMEM((1, row_grid.shape[0]), F32),
            pltpu.VMEM(col_grid.shape, F32),
            pltpu.SMEM(band_mix.shape, F32),
            pltpu.SMEM(band_gain.shape, F32),
            pltpu.SMEM(synth_weight.shape, F32),
            pltpu.VMEM(pan_blocks.shape, BF16),
            pltpu.VMEM(ms_blocks.shape, BF16),
            pltpu.VMEM((own_blocks + 1, size, size), BF16),
            pltpu.VMEM((own_blocks + 1, coarse_size, coarse_width), BF16),
            pltpu.VMEM((table_rows, LANES), I32),
            pltpu.SMEM((table_rows, LANES), I32),
            pltpu.VMEM((8, LANES), F32),
            pltpu.VMEM((2, n, 8, LANES), F32),
            ms_slots(lines),
            ms_slots(lines),
            pan_slots(lines),
            pan_slots(lines),
            ms_slots(lines - 1),
            ms_slots(slots),
            pan_slots(lines - 1),
            pan_slots(slots),
            pltpu.VMEM((bands * coarse_rows, coarse_cols), BF16),
            pltpu.VMEM((bands * coarse_rows, coarse_cols), BF16),
            pltpu.VMEM((TR, TC), F32),
            pltpu.VMEM((2, bands * coarse_rows, coarse_cols), F32),
            pltpu.VMEM((bands * coarse_rows, coarse_cols), F32),
            pltpu.VMEM((bands * coarse_rows, coarse_cols), F32),
            pltpu.VMEM((TR, TC), F32),
            pltpu.VMEM((bands, coarse_rows, coarse_cols), BF16),
            pltpu.VMEM((2, 2 * bands, LANES), BF16),
            pltpu.VMEM((2, 2 * bands, LANES), BF16),
            pltpu.VMEM((2, 2 * bands, LANES), BF16),
            pltpu.VMEM((2, 2 * bands, LANES), BF16),
            pltpu.VMEM((coarse_rows, LANES), BF16),
            pltpu.VMEM((coarse_rows, LANES), BF16),
            pltpu.VMEM((coarse_cols + LANES, TC), BF16),
            pltpu.VMEM((TR, coarse_rows + 4 * bands), BF16),
            pltpu.VMEM((bands * coarse_rows, TC), BF16),
            pltpu.VMEM((bands, TR, TC), BF16),
            dma((10 + HALVES,)),
            dma((2, n)),
            dma((2, n)),
            dma((lines,)),
            dma((lines,)),
            dma((lines, HALVES)),
            dma((lines, HALVES)),
            dma((lines - 1,)),
            dma((slots,)),
            dma((lines - 1, HALVES)),
            dma((slots, HALVES)),
            dma,
            dma,
            dma((5,)),
            dma((5,)),
        ],
        compiler_params=pltpu.CompilerParams(
            collective_id=0, has_side_effects=True, vmem_limit_bytes=60 * 1024 * 1024
        ),
        name="mapping",
    )(
        send_list,
        row_grid[None, :],
        col_grid,
        pan_blocks,
        ms_blocks,
        band_mix,
        band_gain,
        synth_weight,
    )
    detail = band_gain[:, None, None] * pan_map[None]
    return (mixed.astype(F32) + detail).astype(BF16)


def solution(mesh):
    return jax.shard_map(
        local,
        mesh=mesh,
        in_specs=(
            P(("scene", "mrow", "mcol"), None, None),
            P(("scene", "mrow", "mcol"), None, None),
            P(None, ("scene", "mrow", "mcol")),
            P(None, ("scene", "mrow", "mcol")),
            P(("scene", "mrow")),
            P(("scene", "mrow"), "mcol"),
            P(),
            P(),
            P(),
        ),
        out_specs=P(None, ("scene", "mrow"), "mcol"),
        check_vma=False,
    )
```

```python
import functools

import jax
import jax.numpy as jnp
from jax import lax
from jax.experimental import pallas as pl
from jax.experimental.pallas import tpu as pltpu
from jax.sharding import PartitionSpec as P

GRID = 64
TR = 128
TC = 512
KR = 2
KC = 5
LANE_BITS = 7
LANES = 1 << LANE_BITS
PACK = 16
HALVES = 2
MESH = pl.DeviceIdType.MESH
F32 = jnp.float32
BF16 = jnp.bfloat16
I32 = jnp.int32


def cubic_weight(offset):
    outer = jnp.maximum(2.0 - jnp.abs(offset), 0.0)
    shifted = outer - 1.0
    inner = jnp.maximum(shifted, 0.0)
    return outer * outer * (0.5 * shifted) + inner * inner * (1.0 - 2.0 * inner)


def iota(shape, dim):
    return lax.broadcasted_iota(I32, shape, dim)


def row_coord(nodes, position, offset):
    first = position < GRID
    a = jnp.where(first, nodes[:, 0:1], nodes[:, 1:2])
    b = jnp.where(first, nodes[:, 1:2], nodes[:, 2:3])
    within = (jnp.where(first, position, position - GRID).astype(F32) + offset) / GRID
    return a + (b - a) * within


def col_coord(nodes, after, is_last, count, position, offset):
    segment = position // GRID
    coord = jnp.zeros(position.shape, F32)
    for s in range(count):
        left, shift = nodes[:, s : s + 1], s * GRID
        if s + 1 < count:
            right = nodes[:, s + 1 : s + 2]
        else:
            right = jnp.where(is_last, left, after)
            left = jnp.where(is_last, nodes[:, s - 1 : s], left)
            shift = jnp.where(is_last, shift - GRID, shift)
        within = ((position - shift).astype(F32) + offset) / GRID
        coord = jnp.where(segment == s, left + (right - left) * within, coord)
    return coord


def spread(x, origin, size):
    base = jnp.floor(x)
    shape = (PACK, x.shape[1])
    taps = [
        jnp.broadcast_to(cubic_weight(x - (base + t)), shape).astype(BF16)
        for t in (-1.0, 0.0, 1.0, 2.0)
    ]
    groups = size // PACK
    first = base - 1.0 - origin
    group = jnp.floor(first * (1.0 / PACK))
    away = (iota(shape, 0).astype(F32) - (first - group * PACK)).astype(BF16)
    group = jnp.broadcast_to(jnp.clip(group, -2.0, groups + 1.0), shape).astype(BF16)
    none = jnp.zeros(shape, BF16)
    low, high = none, none
    for t in range(4):
        low = jnp.where(away == BF16(t), taps[t], low)
        high = jnp.where(away == BF16(t - PACK), taps[t], high)
    here = [group == BF16(g) for g in range(-1, groups)]
    return jnp.concatenate(
        [jnp.where(here[g + 1], low, jnp.where(here[g], high, none)) for g in range(groups)],
        axis=0,
    )


def mapping(
    capacity,
    col_nodes,
    send_hbm,
    row_hbm,
    col_hbm,
    pan_hbm,
    ms_hbm,
    mix_hbm,
    gain_hbm,
    synth_hbm,
    mixed_hbm,
    pan_hbm_out,
    send_ref,
    row_ref,
    col_ref,
    mix_ref,
    gain_ref,
    synth_ref,
    pan_ref,
    ms_ref,
    pan_sum,
    ms_sum,
    table_ref,
    table,
    nodes_ref,
    nodes_all,
    ms_y_send,
    ms_y_recv,
    pan_y_send,
    pan_y_recv,
    ms_z_send,
    ms_z_recv,
    pan_z_send,
    pan_z_recv,
    near_ms_send,
    near_ms_recv,
    pan_total,
    ms_total,
    ms_hold,
    ms_mine,
    pan_mine,
    window,
    rim_send,
    rim_recv,
    edge_send,
    edge_recv,
    edge_own,
    edge_all,
    up_cols,
    up_rows,
    across,
    mixed,
    load_sem,
    nodes_ss,
    nodes_rs,
    ms_y_ss,
    ms_y_rs,
    pan_y_ss,
    pan_y_rs,
    ms_z_ss,
    ms_z_rs,
    pan_z_ss,
    pan_z_rs,
    near_ss,
    near_rs,
    halo_ss,
    halo_rs,
):
    n = lax.axis_size("mrow")
    lines = n // 2
    blocks = lines // 2
    scene = lax.axis_index("scene")
    m = lax.axis_index("mrow")
    c = lax.axis_index("mcol")
    z, y = m // 2, m % 2
    twin = z * 2 + (1 - y)
    other = 1 - c
    pair = z // 2
    partner = pair * 2 + (1 - z % 2)
    own_blocks, size, _ = pan_ref.shape
    _, coarse_size, coarse_width = ms_ref.shape
    cells = n * KR * KC
    bands = mixed.shape[0]
    coarse_rows = TR // 4
    coarse_cols = TC // 4
    part_rows = TR // HALVES
    first_col = c * KC
    is_last = c == lax.axis_size("mcol") - 1

    def at(row, col):
        return (scene, row, col)

    def remote(src, dst, ss, rs, row, col):
        return pltpu.make_async_remote_copy(
            src_ref=src,
            dst_ref=dst,
            send_sem=ss,
            recv_sem=rs,
            device_id=at(row, col),
            device_id_type=MESH,
        )

    barrier = pltpu.get_barrier_semaphore()

    def greet(k, carry):
        row = lax.rem(m + k, n)
        pl.semaphore_signal(barrier, inc=1, device_id=at(row, c), device_id_type=MESH)
        pl.semaphore_signal(barrier, inc=1, device_id=at(row, other), device_id_type=MESH)
        return carry

    def greet_all():
        pl.semaphore_signal(barrier, inc=1, device_id=at(m, other), device_id_type=MESH)
        lax.fori_loop(1, n, greet, 0)

    loads = [
        pltpu.make_async_copy(src, dst, load_sem.at[k])
        for k, (src, dst) in enumerate(
            (
                (row_hbm, row_ref),
                (col_hbm, col_ref),
                (send_hbm, send_ref),
                (ms_hbm, ms_ref),
                (pan_hbm, pan_ref),
                (mix_hbm, mix_ref),
                (gain_hbm, gain_ref),
                (synth_hbm, synth_ref),
            )
        )
    ]
    row_load, col_load, send_load, ms_load, pan_load, *late_loads = loads
    row_load.start()
    col_load.start()
    greet_all()
    for load in loads[2:]:
        load.start()

    nodes_ref[...] = jnp.zeros_like(nodes_ref)
    row_load.wait()
    col_load.wait()
    nodes_ref[0:1, 0 : row_ref.shape[1]] = row_ref[...]
    nodes_ref[1:2, 0 : col_ref.shape[1]] = col_ref[...]
    nodes_all[c, m] = nodes_ref[...]
    pl.semaphore_wait(barrier, 2 * n - 1)

    def nodes_copy(slot_row, slot_col, row, col):
        return remote(
            nodes_ref,
            nodes_all.at[slot_col, slot_row],
            nodes_ss.at[col, row],
            nodes_rs.at[slot_col, slot_row],
            row,
            col,
        )

    def send_nodes(k, carry):
        row = lax.rem(m + k, n)
        nodes_copy(m, c, row, c).start()
        nodes_copy(m, c, row, other).start()
        return carry

    lax.fori_loop(1, n, send_nodes, 0)
    nodes_copy(m, c, m, other).start()
    send_load.wait()

    square = (own_blocks, own_blocks)
    wide = (own_blocks, LANES)
    owner = send_ref[0:1, :] // capacity
    key_row = (owner * KR + send_ref[1:2, :]) * KC + send_ref[2:3, :] - first_col
    key_row = jnp.broadcast_to(key_row, square)
    diagonal = iota(square, 0) == iota(square, 1)
    key_col = jnp.sum(jnp.where(diagonal, key_row, 0), axis=1, keepdims=True)
    same = key_row == key_col
    before = (key_row < key_col) | (same & (iota(square, 1) < iota(square, 0)))
    rank = jnp.sum(jnp.where(before, 1, 0), axis=1, keepdims=True)
    joined = jnp.sum(jnp.where(before & same, 1, 0), axis=1, keepdims=True)
    hit = rank == iota(wide, 1)
    order = jnp.sum(jnp.where(hit, iota(wide, 0), 0), axis=0, keepdims=True)
    keep = jnp.sum(jnp.where(hit & (joined > 0), 1, 0), axis=0, keepdims=True)
    table_ref[0:1, :] = order
    table_ref[1:2, :] = keep
    for g in range(pl.cdiv(cells, LANES)):
        cell = iota(wide, 1) + g * LANES
        ends = jnp.sum(jnp.where(key_col <= cell, 1, 0), axis=0, keepdims=True)
        count = jnp.sum(jnp.where(key_col == cell, 1, 0), axis=0, keepdims=True)
        table_ref[2 + g : 3 + g, :] = jnp.where(count > 0, ends, 0)
    table_copy = pltpu.make_async_copy(table_ref, table, load_sem.at[8])
    table_copy.start()

    column = iota(up_rows.shape, 1)
    rim = column - coarse_rows
    tap = jnp.where(
        column < coarse_rows, column + 2, rim % 2 + jnp.where(rim < 2 * bands, 0, coarse_rows + 2)
    )
    spot = (iota(up_rows.shape, 0).astype(F32) - 1.5) * 0.25 + 2.0
    up_rows[...] = cubic_weight(spot - tap.astype(F32)).astype(BF16)
    spot = (iota((1, TC), 1).astype(F32) - 1.5) * 0.25 + 2.0
    up_cols[0:coarse_cols, :] = spread(spot, 2.0, coarse_cols)
    start = jnp.where(c == 0, coarse_cols + 2, 0).astype(F32)
    shape = (PACK, TC)
    beside = [jnp.broadcast_to(cubic_weight(spot - (start + e)), shape) for e in (0.0, 1.0)]
    beside = jnp.where(iota(shape, 0) % 2 == 0, beside[0], beside[1]).astype(BF16)
    for g in range(LANES // PACK):
        up_cols[coarse_cols + g * PACK : coarse_cols + (g + 1) * PACK, :] = beside
    pan_sum[0] = jnp.zeros((size, size), BF16)
    ms_sum[0] = jnp.zeros((coarse_size, coarse_width), BF16)
    table_copy.wait()

    def running(source, sums):
        def step(p, total):
            total = total * table[1, p].astype(F32) + source[table[0, p]].astype(F32)
            sums[p + 1] = total.astype(BF16)
            return total

        start = jnp.zeros(source.shape[1:], F32)
        lax.fori_loop(0, own_blocks, step, start, unroll=2)

    ms_load.wait()
    running(ms_ref, ms_sum)
    pan_load.wait()
    running(pan_ref, pan_sum)

    def wait_nodes(k, carry):
        row = lax.rem(m + k, n)
        nodes_copy(row, c, row, c).wait()
        nodes_copy(row, other, row, other).wait()
        return carry

    lax.fori_loop(1, n, wait_nodes, 0)
    nodes_copy(m, other, m, other).wait()

    def cell_of(sums, tile, row, col):
        cell = tile * (KR * KC) + (row * KC + col)
        if cells <= LANES:
            return sums[table[2, cell]]
        return sums[table[2 + (cell >> LANE_BITS), cell & (LANES - 1)]]

    def stacked(sums, tile, col):
        return jnp.concatenate([cell_of(sums, tile, row, col) for row in range(KR)], axis=0)

    def ms_part(tile):
        row_nodes, nodes = nodes_all[c, tile, 0:1], nodes_all[c, tile, 1:2]
        after = nodes_all[1, tile, 1:2, 0:1]
        x_ms = col_coord(
            nodes, after, is_last, col_nodes, 4 * iota((1, coarse_cols), 1) + 1, 0.5
        )
        x_ms = (x_ms - 1.5) * 0.25
        col = spread(x_ms, (first_col * coarse_size).astype(F32), KC * coarse_size)
        spots = (row_coord(row_nodes, 4 * iota((coarse_rows, 1), 0) + 1, 0.5) - 1.5) * 0.25
        taps = iota((coarse_rows, KR * coarse_size), 1).astype(F32)
        weight = cubic_weight(spots - taps).astype(BF16)
        rows = [
            jnp.dot(weight, stacked(ms_sum, tile, k), preferred_element_type=F32).astype(BF16)
            for k in range(KC)
        ]
        by_band = [
            jnp.concatenate(
                [row[:, b * coarse_size : (b + 1) * coarse_size] for row in rows], axis=1
            )
            for b in range(bands)
        ]
        return jnp.dot(jnp.concatenate(by_band, axis=0), col, preferred_element_type=F32)

    def pan_part(tile):
        row_nodes, nodes = nodes_all[c, tile, 0:1], nodes_all[c, tile, 1:2]
        after = nodes_all[1, tile, 1:2, 0:1]
        x_pan = col_coord(nodes, after, is_last, col_nodes, iota((1, TC), 1), 0.0)
        col = spread(x_pan, (first_col * size).astype(F32), KC * size)
        row = spread(row_coord(row_nodes, iota((1, TR), 1), 0.0), 0.0, KR * size)
        rows = []
        for k in range(0, KC, 2):
            source = jnp.concatenate(
                [stacked(pan_sum, tile, j) for j in range(k, min(k + 2, KC))], axis=1
            )
            rows.append(
                lax.dot_general(
                    row, source, (((0,), (0,)), ((), ())), preferred_element_type=F32
                ).astype(BF16)
            )
        return jnp.dot(jnp.concatenate(rows, axis=1), col, preferred_element_type=F32)

    def line_of(k):
        up = lax.rem(pair * 2 + 2 + k, lines)
        down = lax.rem(pair * 2 + lines - 1 - k, lines)
        far = jnp.where(pair % 2 == 0, down, up)
        return jnp.where(k < lines - 2, far, jnp.where(k == lines - 2, partner, z))

    def ms_y(k):
        return remote(ms_y_send.at[k], ms_y_recv.at[k], ms_y_ss.at[k], ms_y_rs.at[k], twin, c)

    def pan_y(k, h):
        part = pl.ds(h * part_rows, part_rows)
        return remote(
            pan_y_send.at[k, part],
            pan_y_recv.at[k, part],
            pan_y_ss.at[k, h],
            pan_y_rs.at[k, h],
            twin,
            c,
        )

    def route(line):
        far = line // 2 != pair
        above = line // 2 > pair
        lower = z % 2 == 0
        inner = far & jnp.logical_xor(above, lower)
        outer = far & jnp.logical_not(jnp.logical_xor(above, lower))
        target = jnp.where(outer, partner, line)
        slot = jnp.where(outer, blocks + line, pair)
        return inner, target * 2 + y, slot

    def ms_z(k, row, slot):
        return remote(
            ms_z_send.at[k], ms_z_recv.at[slot], ms_z_ss.at[k], ms_z_rs.at[slot], row, c
        )

    def pan_z(k, h, row, slot):
        part = pl.ds(h * part_rows, part_rows)
        return remote(
            pan_z_send.at[k, part],
            pan_z_recv.at[slot, part],
            pan_z_ss.at[k, h],
            pan_z_rs.at[slot, h],
            row,
            c,
        )

    def each(first, last, step):
        if last - first == 1:
            step(first)
            return

        def body(k, carry):
            step(k)
            return carry

        lax.fori_loop(first, last, body, 0)

    near_row = partner * 2 + y

    near_ms = remote(near_ms_send, near_ms_recv, near_ss, near_rs, near_row, c)

    def ms_twin_parts(k):
        return [ms_part(line_of(k + i) * 2 + 1 - y) for i in range(2)]

    def pan_pair_to_twin(p):
        parts = [pan_part(line_of(2 * p + i) * 2 + 1 - y) for i in range(2)]
        for i, part in enumerate(parts):
            pan_y_send[2 * p + i] = part.astype(BF16)
        for i in range(2):
            for h in range(HALVES):
                pan_y(2 * p + i, h).start()

    def ms_own_parts(k):
        parts = [ms_part(line_of(k + i) * 2 + y) for i in range(2)]
        for i, part in enumerate(parts):
            ms_total[i] = part

    def ms_onward(k, i):
        line = line_of(k)
        inner, row, slot = route(line)
        ms_y(k).wait_recv()

        @pl.when(inner)
        def _():
            ms_z(0, row, blocks + line).wait_recv()
            relayed = ms_z_recv[blocks + line].astype(F32)
            total = ms_total[i] + ms_y_recv[k].astype(F32)
            ms_z_send[k] = (total + relayed).astype(BF16)

        @pl.when(jnp.logical_not(inner))
        def _():
            ms_z_send[k] = (ms_total[i] + ms_y_recv[k].astype(F32)).astype(BF16)

        ms_z(k, row, slot).start()

    def pan_own_part(k):
        pan_total[...] = pan_part(line_of(k) * 2 + y)

    def pan_forward(k):
        line = line_of(k)
        inner, row, slot = route(line)
        for h in range(HALVES):
            rows = slice(h * part_rows, (h + 1) * part_rows)
            pan_y(k, h).wait_recv()

            @pl.when(inner)
            def _():
                pan_z(0, h, row, blocks + line).wait_recv()
                relayed = pan_z_recv[blocks + line, rows].astype(F32)
                total = pan_total[rows, :] + pan_y_recv[k, rows].astype(F32)
                pan_z_send[k, rows] = (total + relayed).astype(BF16)

            @pl.when(jnp.logical_not(inner))
            def _():
                total = pan_total[rows, :] + pan_y_recv[k, rows].astype(F32)
                pan_z_send[k, rows] = total.astype(BF16)

            pan_z(k, h, row, slot).start()

    def pan_onward(k):
        pan_own_part(k)
        pan_forward(k)

    far = lines - 2
    last = lines - 1

    def ms_far_to_twin(p):
        for i, part in enumerate(ms_twin_parts(2 * p)):
            ms_y_send[2 * p + i] = part.astype(BF16)
        ms_y(2 * p).start()
        ms_y(2 * p + 1).start()

    def ms_far_onward(p):
        ms_own_parts(2 * p)
        ms_onward(2 * p, 0)
        ms_onward(2 * p + 1, 1)

    each(0, far // 2, ms_far_to_twin)
    parts = ms_twin_parts(far)
    near_ms_send[...] = parts[0].astype(BF16)
    ms_hold[...] = parts[1]
    near_ms.start()
    each(0, far // 2, pan_pair_to_twin)
    ms_own_parts(far)
    ms_z_send[far] = ms_total[0].astype(BF16)
    ms_z(far, near_row, pair).start()
    ms_mine[...] = ms_total[1]
    each(0, far // 2, ms_far_onward)
    near_ms.wait_recv()
    ms_y_send[last] = (ms_hold[...] + near_ms_recv[...].astype(F32)).astype(BF16)
    ms_y(last).start()
    pan_pair_to_twin(far // 2)
    each(0, far - 1, pan_onward)
    pan_mine[...] = pan_part(m)
    pan_own_part(far - 1)

    has_above, has_below = m > 0, m < n - 1

    def halo_copy(k, src, dst, row, col):
        return remote(src, dst, halo_ss.at[k], halo_rs.at[k], row, col)

    across_copy = halo_copy(0, edge_own, edge_all, m, other)
    up_copies = [
        halo_copy(1, rim_send.at[0], rim_recv.at[1], m - 1, c),
        halo_copy(2, edge_send.at[0], edge_recv.at[1], m - 1, other),
    ]
    down_copies = [
        halo_copy(3, rim_send.at[1], rim_recv.at[0], m + 1, c),
        halo_copy(4, edge_send.at[1], edge_recv.at[0], m + 1, other),
    ]
    def ms_finish():
        ms_y(last).wait_recv()
        ms_mine[...] += ms_y_recv[last].astype(F32)

        def ms_arrived(slot, carry):
            ms_z(0, m, slot).wait_recv()
            ms_mine[...] += ms_z_recv[slot].astype(F32)
            return carry

        lax.fori_loop(0, blocks, ms_arrived, 0)
        values = [ms_mine[b * coarse_rows : (b + 1) * coarse_rows, :] for b in range(bands)]
        synthetic = sum(synth_ref[b] * values[b] for b in range(bands))
        spot = iota((coarse_rows, LANES), 1) // 2
        edges = jnp.zeros((coarse_rows, LANES), F32)
        tops, bottoms = [], []
        for b in range(bands):
            result = values[b] - gain_ref[b] * synthetic
            for k in range(bands):
                result = result + mix_ref[b, k] * values[k]
            window[b] = result.astype(BF16)
            moved = pltpu.roll(result, jnp.where(c == 0, 2 * b + 2, 2 * b), 1)
            edges = jnp.where(spot == b, moved, edges)
            tops.append(result[0:2, :])
            bottoms.append(result[coarse_rows - 2 : coarse_rows, :])
        edge_own[...] = edges.astype(BF16)
        rim_send[0] = jnp.concatenate(tops, axis=0).astype(BF16)
        rim_send[1] = jnp.concatenate(bottoms, axis=0).astype(BF16)
        edge_send[0] = jnp.concatenate([edges[0:2, :]] * bands, axis=0).astype(BF16)
        bottom = edges[coarse_rows - 2 : coarse_rows, :]
        edge_send[1] = jnp.concatenate([bottom] * bands, axis=0).astype(BF16)

        across_copy.start()

        @pl.when(has_above)
        def _():
            for copy in up_copies:
                copy.start()

        @pl.when(has_below)
        def _():
            for copy in down_copies:
                copy.start()

    early = route(line_of(far - 1))[0]
    for load in late_loads:
        load.wait()
    pl.when(early)(ms_finish)
    pan_forward(far - 1)
    pan_own_part(far)
    pl.when(jnp.logical_not(early))(ms_finish)
    pan_forward(far)
    across_copy.wait()

    edges = edge_all[...]
    spot = iota(edges.shape, 1) // 2
    source = jnp.concatenate(
        [
            jnp.concatenate(
                [window[b], jnp.where(spot == b, edges, jnp.zeros_like(edges))], axis=1
            )
            for b in range(bands)
        ],
        axis=0,
    )
    across[0 : bands * coarse_rows, :] = jnp.dot(
        source, up_cols[...], preferred_element_type=F32
    ).astype(BF16)
    for b in range(bands):
        own = slice(b * coarse_rows, (b + 1) * coarse_rows)
        mixed[b, PACK : TR - PACK, :] = jnp.dot(
            up_rows[PACK : TR - PACK, 0:coarse_rows],
            across[own, :],
            preferred_element_type=F32,
        ).astype(BF16)

    @pl.when(has_above)
    def _():
        for copy in up_copies:
            copy.wait_send()
        for copy in down_copies:
            copy.wait_recv()

    @pl.when(has_below)
    def _():
        for copy in down_copies:
            copy.wait_send()
        for copy in up_copies:
            copy.wait_recv()

    blank = jnp.zeros((2 * bands, LANES), BF16)

    @pl.when(jnp.logical_not(has_above))
    def _():
        rim_recv[0] = blank
        edge_recv[0] = blank

    @pl.when(jnp.logical_not(has_below))
    def _():
        rim_recv[1] = blank
        edge_recv[1] = blank

    spot = iota((2 * bands, LANES), 1) // 2
    mine = spot == iota((2 * bands, LANES), 0) // 2
    source = jnp.concatenate(
        [
            jnp.concatenate([rim_recv[i], jnp.where(mine, edge_recv[i], blank)], axis=1)
            for i in range(2)
        ],
        axis=0,
    )
    rims = jnp.dot(source, up_cols[...], preferred_element_type=F32).astype(BF16)
    outer = jnp.concatenate([up_rows[0:PACK, :], up_rows[TR - PACK : TR, :]], axis=0)
    column = iota(outer.shape, 1)
    owner_band = (column - coarse_rows) % (2 * bands) // 2
    for b in range(bands):
        weight = jnp.where((column < coarse_rows) | (owner_band == b), outer, jnp.zeros_like(outer))
        own = slice(b * coarse_rows, (b + 1) * coarse_rows)
        ends = jnp.dot(
            weight, jnp.concatenate([across[own, :], rims], axis=0), preferred_element_type=F32
        ).astype(BF16)
        mixed[b, 0:PACK, :] = ends[0:PACK, :]
        mixed[b, TR - PACK : TR, :] = ends[PACK : 2 * PACK, :]

    store = pltpu.make_async_copy(mixed, mixed_hbm, load_sem.at[9])
    store.start()
    pan_stores = []
    for h in range(HALVES):
        rows = slice(h * part_rows, (h + 1) * part_rows)
        pan_y(last, h).wait_recv()
        pan_mine[rows, :] += pan_y_recv[last, rows].astype(F32)

        def pan_arrived(slot, carry):
            pan_z(0, h, m, slot).wait_recv()
            pan_mine[rows, :] += pan_z_recv[slot, rows].astype(F32)
            return carry

        lax.fori_loop(0, blocks, pan_arrived, 0)
        part = pl.ds(h * part_rows, part_rows)
        pan_stores.append(
            pltpu.make_async_copy(pan_mine.at[part], pan_hbm_out.at[part], load_sem.at[10 + h])
        )
        pan_stores[-1].start()

    def ms_y_sent(k, carry):
        ms_y(k).wait_send()
        return carry

    def pan_y_sent(k, carry):
        for h in range(HALVES):
            pan_y(k, h).wait_send()
        return carry

    def z_sent(k, carry):
        ms_z(k, m, 0).wait_send()
        for h in range(HALVES):
            pan_z(k, h, m, 0).wait_send()
        return carry

    near_ms.wait_send()
    lax.fori_loop(0, far, ms_y_sent, 0)
    ms_y(last).wait_send()
    lax.fori_loop(0, lines, pan_y_sent, 0)
    lax.fori_loop(0, lines - 1, z_sent, 0)
    store.wait()
    for pan_store in pan_stores:
        pan_store.wait()


def local(
    pan_blocks,
    ms_blocks,
    send_list,
    tile_list,
    row_grid,
    col_grid,
    band_mix,
    band_gain,
    synth_weight,
):
    n = lax.axis_size("mrow")
    lines = n // 2
    own_blocks, size, _ = pan_blocks.shape
    _, coarse_size, coarse_width = ms_blocks.shape
    capacity = tile_list.shape[1] // n
    bands = band_gain.shape[0]
    coarse_rows, coarse_cols = TR // 4, TC // 4
    table_rows = pl.cdiv(2 + pl.cdiv(n * KR * KC, LANES), 8) * 8
    hbm = pl.BlockSpec(memory_space=pl.ANY)
    dma = pltpu.SemaphoreType.DMA
    slots = lines // 2 + lines

    def ms_slots(count):
        return pltpu.VMEM((count, bands * coarse_rows, coarse_cols), BF16)

    def pan_slots(count):
        return pltpu.VMEM((count, TR, TC), BF16)

    mixed, pan_map = pl.pallas_call(
        functools.partial(mapping, capacity, col_grid.shape[1]),
        out_shape=(
            jax.ShapeDtypeStruct((bands, TR, TC), BF16),
            jax.ShapeDtypeStruct((TR, TC), F32),
        ),
        in_specs=[hbm] * 8,
        out_specs=(hbm, hbm),
        scratch_shapes=[
            pltpu.VMEM(send_list.shape, I32),
            pltpu.VMEM((1, row_grid.shape[0]), F32),
            pltpu.VMEM(col_grid.shape, F32),
            pltpu.SMEM(band_mix.shape, F32),
            pltpu.SMEM(band_gain.shape, F32),
            pltpu.SMEM(synth_weight.shape, F32),
            pltpu.VMEM(pan_blocks.shape, BF16),
            pltpu.VMEM(ms_blocks.shape, BF16),
            pltpu.VMEM((own_blocks + 1, size, size), BF16),
            pltpu.VMEM((own_blocks + 1, coarse_size, coarse_width), BF16),
            pltpu.VMEM((table_rows, LANES), I32),
            pltpu.SMEM((table_rows, LANES), I32),
            pltpu.VMEM((8, LANES), F32),
            pltpu.VMEM((2, n, 8, LANES), F32),
            ms_slots(lines),
            ms_slots(lines),
            pan_slots(lines),
            pan_slots(lines),
            ms_slots(lines - 1),
            ms_slots(slots),
            pan_slots(lines - 1),
            pan_slots(slots),
            pltpu.VMEM((bands * coarse_rows, coarse_cols), BF16),
            pltpu.VMEM((bands * coarse_rows, coarse_cols), BF16),
            pltpu.VMEM((TR, TC), F32),
            pltpu.VMEM((2, bands * coarse_rows, coarse_cols), F32),
            pltpu.VMEM((bands * coarse_rows, coarse_cols), F32),
            pltpu.VMEM((bands * coarse_rows, coarse_cols), F32),
            pltpu.VMEM((TR, TC), F32),
            pltpu.VMEM((bands, coarse_rows, coarse_cols), BF16),
            pltpu.VMEM((2, 2 * bands, LANES), BF16),
            pltpu.VMEM((2, 2 * bands, LANES), BF16),
            pltpu.VMEM((2, 2 * bands, LANES), BF16),
            pltpu.VMEM((2, 2 * bands, LANES), BF16),
            pltpu.VMEM((coarse_rows, LANES), BF16),
            pltpu.VMEM((coarse_rows, LANES), BF16),
            pltpu.VMEM((coarse_cols + LANES, TC), BF16),
            pltpu.VMEM((TR, coarse_rows + 4 * bands), BF16),
            pltpu.VMEM((bands * coarse_rows, TC), BF16),
            pltpu.VMEM((bands, TR, TC), BF16),
            dma((10 + HALVES,)),
            dma((2, n)),
            dma((2, n)),
            dma((lines,)),
            dma((lines,)),
            dma((lines, HALVES)),
            dma((lines, HALVES)),
            dma((lines - 1,)),
            dma((slots,)),
            dma((lines - 1, HALVES)),
            dma((slots, HALVES)),
            dma,
            dma,
            dma((5,)),
            dma((5,)),
        ],
        compiler_params=pltpu.CompilerParams(
            collective_id=0, has_side_effects=True, vmem_limit_bytes=60 * 1024 * 1024
        ),
        name="mapping",
    )(
        send_list,
        row_grid[None, :],
        col_grid,
        pan_blocks,
        ms_blocks,
        band_mix,
        band_gain,
        synth_weight,
    )
    detail = band_gain[:, None, None] * pan_map[None]
    return (mixed.astype(F32) + detail).astype(BF16)


def solution(mesh):
    return jax.shard_map(
        local,
        mesh=mesh,
        in_specs=(
            P(("scene", "mrow", "mcol"), None, None),
            P(("scene", "mrow", "mcol"), None, None),
            P(None, ("scene", "mrow", "mcol")),
            P(None, ("scene", "mrow", "mcol")),
            P(("scene", "mrow")),
            P(("scene", "mrow"), "mcol"),
            P(),
            P(),
            P(),
        ),
        out_specs=P(None, ("scene", "mrow"), "mcol"),
        check_vma=False,
    )
```

```python
import functools

import jax
import jax.numpy as jnp
from jax import lax
from jax.experimental import pallas as pl
from jax.experimental.pallas import tpu as pltpu
from jax.sharding import PartitionSpec as P

GRID = 64
TR = 128
TC = 512
KR = 2
KC = 5
LANE_BITS = 7
LANES = 1 << LANE_BITS
PACK = 16
HALVES = 2
MESH = pl.DeviceIdType.MESH
F32 = jnp.float32
BF16 = jnp.bfloat16
I32 = jnp.int32


def cubic_weight(offset):
    outer = jnp.maximum(2.0 - jnp.abs(offset), 0.0)
    shifted = outer - 1.0
    inner = jnp.maximum(shifted, 0.0)
    return outer * outer * (0.5 * shifted) + inner * inner * (1.0 - 2.0 * inner)


def iota(shape, dim):
    return lax.broadcasted_iota(I32, shape, dim)


def row_coord(nodes, position, offset):
    first = position < GRID
    a = jnp.where(first, nodes[:, 0:1], nodes[:, 1:2])
    b = jnp.where(first, nodes[:, 1:2], nodes[:, 2:3])
    within = (jnp.where(first, position, position - GRID).astype(F32) + offset) / GRID
    return a + (b - a) * within


def col_coord(nodes, after, is_last, count, position, offset):
    segment = position // GRID
    coord = jnp.zeros(position.shape, F32)
    for s in range(count):
        left, shift = nodes[:, s : s + 1], s * GRID
        if s + 1 < count:
            right = nodes[:, s + 1 : s + 2]
        else:
            right = jnp.where(is_last, left, after)
            left = jnp.where(is_last, nodes[:, s - 1 : s], left)
            shift = jnp.where(is_last, shift - GRID, shift)
        within = ((position - shift).astype(F32) + offset) / GRID
        coord = jnp.where(segment == s, left + (right - left) * within, coord)
    return coord


def spread(x, origin, size):
    base = jnp.floor(x)
    shape = (PACK, x.shape[1])
    taps = [
        jnp.broadcast_to(cubic_weight(x - (base + t)), shape).astype(BF16)
        for t in (-1.0, 0.0, 1.0, 2.0)
    ]
    groups = size // PACK
    first = base - 1.0 - origin
    group = jnp.floor(first * (1.0 / PACK))
    away = (iota(shape, 0).astype(F32) - (first - group * PACK)).astype(BF16)
    group = jnp.broadcast_to(jnp.clip(group, -2.0, groups + 1.0), shape).astype(BF16)
    none = jnp.zeros(shape, BF16)
    low, high = none, none
    for t in range(4):
        low = jnp.where(away == BF16(t), taps[t], low)
        high = jnp.where(away == BF16(t - PACK), taps[t], high)
    here = [group == BF16(g) for g in range(-1, groups)]
    return jnp.concatenate(
        [jnp.where(here[g + 1], low, jnp.where(here[g], high, none)) for g in range(groups)],
        axis=0,
    )


def mapping(
    capacity,
    col_nodes,
    send_hbm,
    row_hbm,
    col_hbm,
    pan_hbm,
    ms_hbm,
    mix_hbm,
    gain_hbm,
    synth_hbm,
    mixed_hbm,
    pan_hbm_out,
    send_ref,
    row_ref,
    col_ref,
    mix_ref,
    gain_ref,
    synth_ref,
    pan_ref,
    ms_ref,
    pan_sum,
    ms_sum,
    table_ref,
    table,
    nodes_ref,
    nodes_all,
    ms_y_send,
    ms_y_recv,
    pan_y_send,
    pan_y_recv,
    ms_z_send,
    ms_z_recv,
    pan_z_send,
    pan_z_recv,
    near_ms_send,
    near_ms_recv,
    pan_total,
    ms_total,
    ms_hold,
    ms_mine,
    pan_mine,
    window,
    rim_send,
    rim_recv,
    edge_send,
    edge_recv,
    edge_own,
    edge_all,
    up_cols,
    up_rows,
    across,
    mixed,
    load_sem,
    nodes_ss,
    nodes_rs,
    ms_y_ss,
    ms_y_rs,
    pan_y_ss,
    pan_y_rs,
    ms_z_ss,
    ms_z_rs,
    pan_z_ss,
    pan_z_rs,
    near_ss,
    near_rs,
    halo_ss,
    halo_rs,
):
    n = lax.axis_size("mrow")
    lines = n // 2
    blocks = lines // 2
    scene = lax.axis_index("scene")
    m = lax.axis_index("mrow")
    c = lax.axis_index("mcol")
    z, y = m // 2, m % 2
    twin = z * 2 + (1 - y)
    other = 1 - c
    pair = z // 2
    partner = pair * 2 + (1 - z % 2)
    own_blocks, size, _ = pan_ref.shape
    _, coarse_size, coarse_width = ms_ref.shape
    cells = n * KR * KC
    bands = mixed.shape[0]
    coarse_rows = TR // 4
    coarse_cols = TC // 4
    part_rows = TR // HALVES
    first_col = c * KC
    is_last = c == lax.axis_size("mcol") - 1

    def at(row, col):
        return (scene, row, col)

    def remote(src, dst, ss, rs, row, col):
        return pltpu.make_async_remote_copy(
            src_ref=src,
            dst_ref=dst,
            send_sem=ss,
            recv_sem=rs,
            device_id=at(row, col),
            device_id_type=MESH,
        )

    barrier = pltpu.get_barrier_semaphore()

    def greet(k, carry):
        row = lax.rem(m + k, n)
        pl.semaphore_signal(barrier, inc=1, device_id=at(row, c), device_id_type=MESH)
        pl.semaphore_signal(barrier, inc=1, device_id=at(row, other), device_id_type=MESH)
        return carry

    def greet_all():
        pl.semaphore_signal(barrier, inc=1, device_id=at(m, other), device_id_type=MESH)
        lax.fori_loop(1, n, greet, 0)

    loads = [
        pltpu.make_async_copy(src, dst, load_sem.at[k])
        for k, (src, dst) in enumerate(
            (
                (row_hbm, row_ref),
                (col_hbm, col_ref),
                (send_hbm, send_ref),
                (ms_hbm, ms_ref),
                (pan_hbm, pan_ref),
                (mix_hbm, mix_ref),
                (gain_hbm, gain_ref),
                (synth_hbm, synth_ref),
            )
        )
    ]
    row_load, col_load, send_load, ms_load, pan_load, *late_loads = loads
    row_load.start()
    col_load.start()
    greet_all()
    for load in loads[2:]:
        load.start()

    nodes_ref[...] = jnp.zeros_like(nodes_ref)
    row_load.wait()
    col_load.wait()
    nodes_ref[0:1, 0 : row_ref.shape[1]] = row_ref[...]
    nodes_ref[1:2, 0 : col_ref.shape[1]] = col_ref[...]
    nodes_all[c, m] = nodes_ref[...]
    pl.semaphore_wait(barrier, 2 * n - 1)

    def nodes_copy(slot_row, slot_col, row, col):
        return remote(
            nodes_ref,
            nodes_all.at[slot_col, slot_row],
            nodes_ss.at[col, row],
            nodes_rs.at[slot_col, slot_row],
            row,
            col,
        )

    def send_nodes(k, carry):
        row = lax.rem(m + k, n)
        nodes_copy(m, c, row, c).start()
        nodes_copy(m, c, row, other).start()
        return carry

    lax.fori_loop(1, n, send_nodes, 0)
    nodes_copy(m, c, m, other).start()
    send_load.wait()

    square = (own_blocks, own_blocks)
    wide = (own_blocks, LANES)
    owner = send_ref[0:1, :] // capacity
    key_row = (owner * KR + send_ref[1:2, :]) * KC + send_ref[2:3, :] - first_col
    key_row = jnp.broadcast_to(key_row, square)
    diagonal = iota(square, 0) == iota(square, 1)
    key_col = jnp.sum(jnp.where(diagonal, key_row, 0), axis=1, keepdims=True)
    same = key_row == key_col
    before = (key_row < key_col) | (same & (iota(square, 1) < iota(square, 0)))
    rank = jnp.sum(jnp.where(before, 1, 0), axis=1, keepdims=True)
    joined = jnp.sum(jnp.where(before & same, 1, 0), axis=1, keepdims=True)
    hit = rank == iota(wide, 1)
    order = jnp.sum(jnp.where(hit, iota(wide, 0), 0), axis=0, keepdims=True)
    keep = jnp.sum(jnp.where(hit & (joined > 0), 1, 0), axis=0, keepdims=True)
    table_ref[0:1, :] = order
    table_ref[1:2, :] = keep
    for g in range(pl.cdiv(cells, LANES)):
        cell = iota(wide, 1) + g * LANES
        ends = jnp.sum(jnp.where(key_col <= cell, 1, 0), axis=0, keepdims=True)
        count = jnp.sum(jnp.where(key_col == cell, 1, 0), axis=0, keepdims=True)
        table_ref[2 + g : 3 + g, :] = jnp.where(count > 0, ends, 0)
    table_copy = pltpu.make_async_copy(table_ref, table, load_sem.at[8])
    table_copy.start()

    column = iota(up_rows.shape, 1)
    rim = column - coarse_rows
    tap = jnp.where(
        column < coarse_rows, column + 2, rim % 2 + jnp.where(rim < 2 * bands, 0, coarse_rows + 2)
    )
    spot = (iota(up_rows.shape, 0).astype(F32) - 1.5) * 0.25 + 2.0
    up_rows[...] = cubic_weight(spot - tap.astype(F32)).astype(BF16)
    spot = (iota((1, TC), 1).astype(F32) - 1.5) * 0.25 + 2.0
    up_cols[0:coarse_cols, :] = spread(spot, 2.0, coarse_cols)
    start = jnp.where(c == 0, coarse_cols + 2, 0).astype(F32)
    shape = (PACK, TC)
    beside = [jnp.broadcast_to(cubic_weight(spot - (start + e)), shape) for e in (0.0, 1.0)]
    beside = jnp.where(iota(shape, 0) % 2 == 0, beside[0], beside[1]).astype(BF16)
    for g in range(LANES // PACK):
        up_cols[coarse_cols + g * PACK : coarse_cols + (g + 1) * PACK, :] = beside
    pan_sum[0] = jnp.zeros((size, size), BF16)
    ms_sum[0] = jnp.zeros((coarse_size, coarse_width), BF16)
    table_copy.wait()

    def running(source, sums):
        def step(p, total):
            total = total * table[1, p].astype(F32) + source[table[0, p]].astype(F32)
            sums[p + 1] = total.astype(BF16)
            return total

        start = jnp.zeros(source.shape[1:], F32)
        lax.fori_loop(0, own_blocks, step, start, unroll=2)

    ms_load.wait()
    running(ms_ref, ms_sum)
    pan_load.wait()
    running(pan_ref, pan_sum)

    def wait_nodes(k, carry):
        row = lax.rem(m + k, n)
        nodes_copy(row, c, row, c).wait()
        nodes_copy(row, other, row, other).wait()
        return carry

    lax.fori_loop(1, n, wait_nodes, 0)
    nodes_copy(m, other, m, other).wait()

    def cell_of(sums, tile, row, col):
        cell = tile * (KR * KC) + (row * KC + col)
        if cells <= LANES:
            return sums[table[2, cell]]
        return sums[table[2 + (cell >> LANE_BITS), cell & (LANES - 1)]]

    def stacked(sums, tile, col):
        return jnp.concatenate([cell_of(sums, tile, row, col) for row in range(KR)], axis=0)

    def ms_part(tile):
        row_nodes, nodes = nodes_all[c, tile, 0:1], nodes_all[c, tile, 1:2]
        after = nodes_all[1, tile, 1:2, 0:1]
        x_ms = col_coord(
            nodes, after, is_last, col_nodes, 4 * iota((1, coarse_cols), 1) + 1, 0.5
        )
        x_ms = (x_ms - 1.5) * 0.25
        col = spread(x_ms, (first_col * coarse_size).astype(F32), KC * coarse_size)
        spots = (row_coord(row_nodes, 4 * iota((coarse_rows, 1), 0) + 1, 0.5) - 1.5) * 0.25
        taps = iota((coarse_rows, KR * coarse_size), 1).astype(F32)
        weight = cubic_weight(spots - taps).astype(BF16)
        rows = [
            jnp.dot(weight, stacked(ms_sum, tile, k), preferred_element_type=F32).astype(BF16)
            for k in range(KC)
        ]
        by_band = [
            jnp.concatenate(
                [row[:, b * coarse_size : (b + 1) * coarse_size] for row in rows], axis=1
            )
            for b in range(bands)
        ]
        return jnp.dot(jnp.concatenate(by_band, axis=0), col, preferred_element_type=F32)

    def pan_part(tile):
        row_nodes, nodes = nodes_all[c, tile, 0:1], nodes_all[c, tile, 1:2]
        after = nodes_all[1, tile, 1:2, 0:1]
        x_pan = col_coord(nodes, after, is_last, col_nodes, iota((1, TC), 1), 0.0)
        col = spread(x_pan, (first_col * size).astype(F32), KC * size)
        row = spread(row_coord(row_nodes, iota((1, TR), 1), 0.0), 0.0, KR * size)
        rows = []
        for k in range(0, KC, 2):
            source = jnp.concatenate(
                [stacked(pan_sum, tile, j) for j in range(k, min(k + 2, KC))], axis=1
            )
            rows.append(
                lax.dot_general(
                    row, source, (((0,), (0,)), ((), ())), preferred_element_type=F32
                ).astype(BF16)
            )
        return jnp.dot(jnp.concatenate(rows, axis=1), col, preferred_element_type=F32)

    def line_of(k):
        up = lax.rem(pair * 2 + 2 + k, lines)
        down = lax.rem(pair * 2 + lines - 1 - k, lines)
        far = jnp.where(pair % 2 == 0, down, up)
        return jnp.where(k < lines - 2, far, jnp.where(k == lines - 2, partner, z))

    def ms_y(k):
        return remote(ms_y_send.at[k], ms_y_recv.at[k], ms_y_ss.at[k], ms_y_rs.at[k], twin, c)

    def pan_y(k, h):
        part = pl.ds(h * part_rows, part_rows)
        return remote(
            pan_y_send.at[k, part],
            pan_y_recv.at[k, part],
            pan_y_ss.at[k, h],
            pan_y_rs.at[k, h],
            twin,
            c,
        )

    def route(line):
        far = line // 2 != pair
        above = line // 2 > pair
        lower = z % 2 == 0
        inner = far & jnp.logical_xor(above, lower)
        outer = far & jnp.logical_not(jnp.logical_xor(above, lower))
        target = jnp.where(outer, partner, line)
        slot = jnp.where(outer, blocks + line, pair)
        return inner, target * 2 + y, slot

    def ms_z(k, row, slot):
        return remote(
            ms_z_send.at[k], ms_z_recv.at[slot], ms_z_ss.at[k], ms_z_rs.at[slot], row, c
        )

    def pan_z(k, h, row, slot):
        part = pl.ds(h * part_rows, part_rows)
        return remote(
            pan_z_send.at[k, part],
            pan_z_recv.at[slot, part],
            pan_z_ss.at[k, h],
            pan_z_rs.at[slot, h],
            row,
            c,
        )

    def each(first, last, step):
        if last - first == 1:
            step(first)
            return

        def body(k, carry):
            step(k)
            return carry

        lax.fori_loop(first, last, body, 0)

    near_row = partner * 2 + y

    near_ms = remote(near_ms_send, near_ms_recv, near_ss, near_rs, near_row, c)

    def ms_twin_parts(k):
        return [ms_part(line_of(k + i) * 2 + 1 - y) for i in range(2)]

    swap = route(line_of(lines - 3))[0]

    def pan_turn(k):
        first = jnp.where(swap, lines - 2, lines - 3)
        second = jnp.where(swap, lines - 3, lines - 2)
        return jnp.where(k == lines - 3, first, jnp.where(k == lines - 2, second, k))

    def pan_pair_to_twin(p):
        keys = [pan_turn(2 * p + i) for i in range(2)]
        parts = [pan_part(line_of(k) * 2 + 1 - y) for k in keys]
        for k, part in zip(keys, parts):
            pan_y_send[k] = part.astype(BF16)
        for k in keys:
            for h in range(HALVES):
                pan_y(k, h).start()

    def ms_own_parts(k):
        parts = [ms_part(line_of(k + i) * 2 + y) for i in range(2)]
        for i, part in enumerate(parts):
            ms_total[i] = part

    def ms_onward(k, i):
        line = line_of(k)
        inner, row, slot = route(line)
        ms_y(k).wait_recv()

        @pl.when(inner)
        def _():
            ms_z(0, row, blocks + line).wait_recv()
            relayed = ms_z_recv[blocks + line].astype(F32)
            total = ms_total[i] + ms_y_recv[k].astype(F32)
            ms_z_send[k] = (total + relayed).astype(BF16)

        @pl.when(jnp.logical_not(inner))
        def _():
            ms_z_send[k] = (ms_total[i] + ms_y_recv[k].astype(F32)).astype(BF16)

        ms_z(k, row, slot).start()

    def pan_own_part(k):
        pan_total[...] = pan_part(line_of(k) * 2 + y)

    def pan_forward(k):
        line = line_of(k)
        inner, row, slot = route(line)
        for h in range(HALVES):
            rows = slice(h * part_rows, (h + 1) * part_rows)
            pan_y(k, h).wait_recv()

            @pl.when(inner)
            def _():
                pan_z(0, h, row, blocks + line).wait_recv()
                relayed = pan_z_recv[blocks + line, rows].astype(F32)
                total = pan_total[rows, :] + pan_y_recv[k, rows].astype(F32)
                pan_z_send[k, rows] = (total + relayed).astype(BF16)

            @pl.when(jnp.logical_not(inner))
            def _():
                total = pan_total[rows, :] + pan_y_recv[k, rows].astype(F32)
                pan_z_send[k, rows] = total.astype(BF16)

            pan_z(k, h, row, slot).start()

    def pan_onward(k):
        pan_own_part(k)
        pan_forward(k)

    far = lines - 2
    last = lines - 1

    def ms_far_to_twin(p):
        for i, part in enumerate(ms_twin_parts(2 * p)):
            ms_y_send[2 * p + i] = part.astype(BF16)
        ms_y(2 * p).start()
        ms_y(2 * p + 1).start()

    def ms_far_onward(p):
        ms_own_parts(2 * p)
        ms_onward(2 * p, 0)
        ms_onward(2 * p + 1, 1)

    each(0, far // 2, ms_far_to_twin)
    parts = ms_twin_parts(far)
    near_ms_send[...] = parts[0].astype(BF16)
    ms_hold[...] = parts[1]
    near_ms.start()
    each(0, far // 2, pan_pair_to_twin)
    ms_own_parts(far)
    ms_z_send[far] = ms_total[0].astype(BF16)
    ms_z(far, near_row, pair).start()
    ms_mine[...] = ms_total[1]
    each(0, far // 2, ms_far_onward)
    near_ms.wait_recv()
    ms_y_send[last] = (ms_hold[...] + near_ms_recv[...].astype(F32)).astype(BF16)
    ms_y(last).start()
    pan_pair_to_twin(far // 2)
    each(0, far - 1, pan_onward)
    pan_mine[...] = pan_part(m)
    pan_own_part(pan_turn(far - 1))

    has_above, has_below = m > 0, m < n - 1

    def halo_copy(k, src, dst, row, col):
        return remote(src, dst, halo_ss.at[k], halo_rs.at[k], row, col)

    across_copy = halo_copy(0, edge_own, edge_all, m, other)
    up_copies = [
        halo_copy(1, rim_send.at[0], rim_recv.at[1], m - 1, c),
        halo_copy(2, edge_send.at[0], edge_recv.at[1], m - 1, other),
    ]
    down_copies = [
        halo_copy(3, rim_send.at[1], rim_recv.at[0], m + 1, c),
        halo_copy(4, edge_send.at[1], edge_recv.at[0], m + 1, other),
    ]
    def ms_finish():
        ms_y(last).wait_recv()
        ms_mine[...] += ms_y_recv[last].astype(F32)

        def ms_arrived(slot, carry):
            ms_z(0, m, slot).wait_recv()
            ms_mine[...] += ms_z_recv[slot].astype(F32)
            return carry

        lax.fori_loop(0, blocks, ms_arrived, 0)
        values = [ms_mine[b * coarse_rows : (b + 1) * coarse_rows, :] for b in range(bands)]
        synthetic = sum(synth_ref[b] * values[b] for b in range(bands))
        spot = iota((coarse_rows, LANES), 1) // 2
        edges = jnp.zeros((coarse_rows, LANES), F32)
        tops, bottoms = [], []
        for b in range(bands):
            result = values[b] - gain_ref[b] * synthetic
            for k in range(bands):
                result = result + mix_ref[b, k] * values[k]
            window[b] = result.astype(BF16)
            moved = pltpu.roll(result, jnp.where(c == 0, 2 * b + 2, 2 * b), 1)
            edges = jnp.where(spot == b, moved, edges)
            tops.append(result[0:2, :])
            bottoms.append(result[coarse_rows - 2 : coarse_rows, :])
        edge_own[...] = edges.astype(BF16)
        rim_send[0] = jnp.concatenate(tops, axis=0).astype(BF16)
        rim_send[1] = jnp.concatenate(bottoms, axis=0).astype(BF16)
        edge_send[0] = jnp.concatenate([edges[0:2, :]] * bands, axis=0).astype(BF16)
        bottom = edges[coarse_rows - 2 : coarse_rows, :]
        edge_send[1] = jnp.concatenate([bottom] * bands, axis=0).astype(BF16)

        across_copy.start()

        @pl.when(has_above)
        def _():
            for copy in up_copies:
                copy.start()

        @pl.when(has_below)
        def _():
            for copy in down_copies:
                copy.start()

    for load in late_loads:
        load.wait()
    pan_forward(pan_turn(far - 1))
    pan_own_part(pan_turn(far))
    ms_finish()
    pan_forward(pan_turn(far))
    across_copy.wait()

    edges = edge_all[...]
    spot = iota(edges.shape, 1) // 2
    source = jnp.concatenate(
        [
            jnp.concatenate(
                [window[b], jnp.where(spot == b, edges, jnp.zeros_like(edges))], axis=1
            )
            for b in range(bands)
        ],
        axis=0,
    )
    across[0 : bands * coarse_rows, :] = jnp.dot(
        source, up_cols[...], preferred_element_type=F32
    ).astype(BF16)
    for b in range(bands):
        own = slice(b * coarse_rows, (b + 1) * coarse_rows)
        mixed[b, PACK : TR - PACK, :] = jnp.dot(
            up_rows[PACK : TR - PACK, 0:coarse_rows],
            across[own, :],
            preferred_element_type=F32,
        ).astype(BF16)

    @pl.when(has_above)
    def _():
        for copy in up_copies:
            copy.wait_send()
        for copy in down_copies:
            copy.wait_recv()

    @pl.when(has_below)
    def _():
        for copy in down_copies:
            copy.wait_send()
        for copy in up_copies:
            copy.wait_recv()

    blank = jnp.zeros((2 * bands, LANES), BF16)

    @pl.when(jnp.logical_not(has_above))
    def _():
        rim_recv[0] = blank
        edge_recv[0] = blank

    @pl.when(jnp.logical_not(has_below))
    def _():
        rim_recv[1] = blank
        edge_recv[1] = blank

    spot = iota((2 * bands, LANES), 1) // 2
    mine = spot == iota((2 * bands, LANES), 0) // 2
    source = jnp.concatenate(
        [
            jnp.concatenate([rim_recv[i], jnp.where(mine, edge_recv[i], blank)], axis=1)
            for i in range(2)
        ],
        axis=0,
    )
    rims = jnp.dot(source, up_cols[...], preferred_element_type=F32).astype(BF16)
    outer = jnp.concatenate([up_rows[0:PACK, :], up_rows[TR - PACK : TR, :]], axis=0)
    column = iota(outer.shape, 1)
    owner_band = (column - coarse_rows) % (2 * bands) // 2
    for b in range(bands):
        weight = jnp.where((column < coarse_rows) | (owner_band == b), outer, jnp.zeros_like(outer))
        own = slice(b * coarse_rows, (b + 1) * coarse_rows)
        ends = jnp.dot(
            weight, jnp.concatenate([across[own, :], rims], axis=0), preferred_element_type=F32
        ).astype(BF16)
        mixed[b, 0:PACK, :] = ends[0:PACK, :]
        mixed[b, TR - PACK : TR, :] = ends[PACK : 2 * PACK, :]

    store = pltpu.make_async_copy(mixed, mixed_hbm, load_sem.at[9])
    store.start()
    pan_stores = []
    for h in range(HALVES):
        rows = slice(h * part_rows, (h + 1) * part_rows)
        pan_y(last, h).wait_recv()
        pan_mine[rows, :] += pan_y_recv[last, rows].astype(F32)

        def pan_arrived(slot, carry):
            pan_z(0, h, m, slot).wait_recv()
            pan_mine[rows, :] += pan_z_recv[slot, rows].astype(F32)
            return carry

        lax.fori_loop(0, blocks, pan_arrived, 0)
        part = pl.ds(h * part_rows, part_rows)
        pan_stores.append(
            pltpu.make_async_copy(pan_mine.at[part], pan_hbm_out.at[part], load_sem.at[10 + h])
        )
        pan_stores[-1].start()

    def ms_y_sent(k, carry):
        ms_y(k).wait_send()
        return carry

    def pan_y_sent(k, carry):
        for h in range(HALVES):
            pan_y(k, h).wait_send()
        return carry

    def z_sent(k, carry):
        ms_z(k, m, 0).wait_send()
        for h in range(HALVES):
            pan_z(k, h, m, 0).wait_send()
        return carry

    near_ms.wait_send()
    lax.fori_loop(0, far, ms_y_sent, 0)
    ms_y(last).wait_send()
    lax.fori_loop(0, lines, pan_y_sent, 0)
    lax.fori_loop(0, lines - 1, z_sent, 0)
    store.wait()
    for pan_store in pan_stores:
        pan_store.wait()


def local(
    pan_blocks,
    ms_blocks,
    send_list,
    tile_list,
    row_grid,
    col_grid,
    band_mix,
    band_gain,
    synth_weight,
):
    n = lax.axis_size("mrow")
    lines = n // 2
    own_blocks, size, _ = pan_blocks.shape
    _, coarse_size, coarse_width = ms_blocks.shape
    capacity = tile_list.shape[1] // n
    bands = band_gain.shape[0]
    coarse_rows, coarse_cols = TR // 4, TC // 4
    table_rows = pl.cdiv(2 + pl.cdiv(n * KR * KC, LANES), 8) * 8
    hbm = pl.BlockSpec(memory_space=pl.ANY)
    dma = pltpu.SemaphoreType.DMA
    slots = lines // 2 + lines

    def ms_slots(count):
        return pltpu.VMEM((count, bands * coarse_rows, coarse_cols), BF16)

    def pan_slots(count):
        return pltpu.VMEM((count, TR, TC), BF16)

    mixed, pan_map = pl.pallas_call(
        functools.partial(mapping, capacity, col_grid.shape[1]),
        out_shape=(
            jax.ShapeDtypeStruct((bands, TR, TC), BF16),
            jax.ShapeDtypeStruct((TR, TC), F32),
        ),
        in_specs=[hbm] * 8,
        out_specs=(hbm, hbm),
        scratch_shapes=[
            pltpu.VMEM(send_list.shape, I32),
            pltpu.VMEM((1, row_grid.shape[0]), F32),
            pltpu.VMEM(col_grid.shape, F32),
            pltpu.SMEM(band_mix.shape, F32),
            pltpu.SMEM(band_gain.shape, F32),
            pltpu.SMEM(synth_weight.shape, F32),
            pltpu.VMEM(pan_blocks.shape, BF16),
            pltpu.VMEM(ms_blocks.shape, BF16),
            pltpu.VMEM((own_blocks + 1, size, size), BF16),
            pltpu.VMEM((own_blocks + 1, coarse_size, coarse_width), BF16),
            pltpu.VMEM((table_rows, LANES), I32),
            pltpu.SMEM((table_rows, LANES), I32),
            pltpu.VMEM((8, LANES), F32),
            pltpu.VMEM((2, n, 8, LANES), F32),
            ms_slots(lines),
            ms_slots(lines),
            pan_slots(lines),
            pan_slots(lines),
            ms_slots(lines - 1),
            ms_slots(slots),
            pan_slots(lines - 1),
            pan_slots(slots),
            pltpu.VMEM((bands * coarse_rows, coarse_cols), BF16),
            pltpu.VMEM((bands * coarse_rows, coarse_cols), BF16),
            pltpu.VMEM((TR, TC), F32),
            pltpu.VMEM((2, bands * coarse_rows, coarse_cols), F32),
            pltpu.VMEM((bands * coarse_rows, coarse_cols), F32),
            pltpu.VMEM((bands * coarse_rows, coarse_cols), F32),
            pltpu.VMEM((TR, TC), F32),
            pltpu.VMEM((bands, coarse_rows, coarse_cols), BF16),
            pltpu.VMEM((2, 2 * bands, LANES), BF16),
            pltpu.VMEM((2, 2 * bands, LANES), BF16),
            pltpu.VMEM((2, 2 * bands, LANES), BF16),
            pltpu.VMEM((2, 2 * bands, LANES), BF16),
            pltpu.VMEM((coarse_rows, LANES), BF16),
            pltpu.VMEM((coarse_rows, LANES), BF16),
            pltpu.VMEM((coarse_cols + LANES, TC), BF16),
            pltpu.VMEM((TR, coarse_rows + 4 * bands), BF16),
            pltpu.VMEM((bands * coarse_rows, TC), BF16),
            pltpu.VMEM((bands, TR, TC), BF16),
            dma((10 + HALVES,)),
            dma((2, n)),
            dma((2, n)),
            dma((lines,)),
            dma((lines,)),
            dma((lines, HALVES)),
            dma((lines, HALVES)),
            dma((lines - 1,)),
            dma((slots,)),
            dma((lines - 1, HALVES)),
            dma((slots, HALVES)),
            dma,
            dma,
            dma((5,)),
            dma((5,)),
        ],
        compiler_params=pltpu.CompilerParams(
            collective_id=0, has_side_effects=True, vmem_limit_bytes=60 * 1024 * 1024
        ),
        name="mapping",
    )(
        send_list,
        row_grid[None, :],
        col_grid,
        pan_blocks,
        ms_blocks,
        band_mix,
        band_gain,
        synth_weight,
    )
    detail = band_gain[:, None, None] * pan_map[None]
    return (mixed.astype(F32) + detail).astype(BF16)


def solution(mesh):
    return jax.shard_map(
        local,
        mesh=mesh,
        in_specs=(
            P(("scene", "mrow", "mcol"), None, None),
            P(("scene", "mrow", "mcol"), None, None),
            P(None, ("scene", "mrow", "mcol")),
            P(None, ("scene", "mrow", "mcol")),
            P(("scene", "mrow")),
            P(("scene", "mrow"), "mcol"),
            P(),
            P(),
            P(),
        ),
        out_specs=P(None, ("scene", "mrow"), "mcol"),
        check_vma=False,
    )
```

```python
import functools

import jax
import jax.numpy as jnp
from jax import lax
from jax.experimental import pallas as pl
from jax.experimental.pallas import tpu as pltpu
from jax.sharding import PartitionSpec as P

GRID = 64
TR = 128
TC = 512
KR = 2
KC = 5
LANE_BITS = 7
LANES = 1 << LANE_BITS
PACK = 16
HALVES = 2
MESH = pl.DeviceIdType.MESH
F32 = jnp.float32
BF16 = jnp.bfloat16
I32 = jnp.int32


def cubic_weight(offset):
    outer = jnp.maximum(2.0 - jnp.abs(offset), 0.0)
    shifted = outer - 1.0
    inner = jnp.maximum(shifted, 0.0)
    return outer * outer * (0.5 * shifted) + inner * inner * (1.0 - 2.0 * inner)


def iota(shape, dim):
    return lax.broadcasted_iota(I32, shape, dim)


def row_coord(nodes, position, offset):
    first = position < GRID
    a = jnp.where(first, nodes[:, 0:1], nodes[:, 1:2])
    b = jnp.where(first, nodes[:, 1:2], nodes[:, 2:3])
    within = (jnp.where(first, position, position - GRID).astype(F32) + offset) / GRID
    return a + (b - a) * within


def col_coord(nodes, after, is_last, count, position, offset):
    segment = position // GRID
    coord = jnp.zeros(position.shape, F32)
    for s in range(count):
        left, shift = nodes[:, s : s + 1], s * GRID
        if s + 1 < count:
            right = nodes[:, s + 1 : s + 2]
        else:
            right = jnp.where(is_last, left, after)
            left = jnp.where(is_last, nodes[:, s - 1 : s], left)
            shift = jnp.where(is_last, shift - GRID, shift)
        within = ((position - shift).astype(F32) + offset) / GRID
        coord = jnp.where(segment == s, left + (right - left) * within, coord)
    return coord


def spread(x, origin, size):
    base = jnp.floor(x)
    shape = (PACK, x.shape[1])
    taps = [
        jnp.broadcast_to(cubic_weight(x - (base + t)), shape).astype(BF16)
        for t in (-1.0, 0.0, 1.0, 2.0)
    ]
    groups = size // PACK
    first = base - 1.0 - origin
    group = jnp.floor(first * (1.0 / PACK))
    away = (iota(shape, 0).astype(F32) - (first - group * PACK)).astype(BF16)
    group = jnp.broadcast_to(jnp.clip(group, -2.0, groups + 1.0), shape).astype(BF16)
    none = jnp.zeros(shape, BF16)
    low, high = none, none
    for t in range(4):
        low = jnp.where(away == BF16(t), taps[t], low)
        high = jnp.where(away == BF16(t - PACK), taps[t], high)
    here = [group == BF16(g) for g in range(-1, groups)]
    return jnp.concatenate(
        [jnp.where(here[g + 1], low, jnp.where(here[g], high, none)) for g in range(groups)],
        axis=0,
    )


def mapping(
    capacity,
    col_nodes,
    send_hbm,
    row_hbm,
    col_hbm,
    pan_hbm,
    ms_hbm,
    mix_hbm,
    gain_hbm,
    synth_hbm,
    mixed_hbm,
    pan_hbm_out,
    send_ref,
    row_ref,
    col_ref,
    mix_ref,
    gain_ref,
    synth_ref,
    pan_ref,
    ms_ref,
    pan_sum,
    ms_sum,
    table_ref,
    table,
    nodes_ref,
    nodes_all,
    ms_y_send,
    ms_y_recv,
    pan_y_send,
    pan_y_recv,
    ms_z_send,
    ms_z_recv,
    pan_z_send,
    pan_z_recv,
    near_ms_send,
    near_ms_recv,
    pan_total,
    ms_total,
    ms_hold,
    ms_mine,
    pan_mine,
    window,
    rim_send,
    rim_recv,
    edge_send,
    edge_recv,
    edge_own,
    edge_all,
    up_cols,
    up_rows,
    across,
    mixed,
    load_sem,
    nodes_ss,
    nodes_rs,
    ms_y_ss,
    ms_y_rs,
    pan_y_ss,
    pan_y_rs,
    ms_z_ss,
    ms_z_rs,
    pan_z_ss,
    pan_z_rs,
    near_ss,
    near_rs,
    halo_ss,
    halo_rs,
):
    n = lax.axis_size("mrow")
    lines = n // 2
    blocks = lines // 2
    scene = lax.axis_index("scene")
    m = lax.axis_index("mrow")
    c = lax.axis_index("mcol")
    z, y = m // 2, m % 2
    twin = z * 2 + (1 - y)
    other = 1 - c
    pair = z // 2
    partner = pair * 2 + (1 - z % 2)
    own_blocks, size, _ = pan_ref.shape
    _, coarse_size, coarse_width = ms_ref.shape
    cells = n * KR * KC
    bands = mixed.shape[0]
    coarse_rows = TR // 4
    coarse_cols = TC // 4
    part_rows = TR // HALVES
    first_col = c * KC
    is_last = c == lax.axis_size("mcol") - 1

    def at(row, col):
        return (scene, row, col)

    def remote(src, dst, ss, rs, row, col):
        return pltpu.make_async_remote_copy(
            src_ref=src,
            dst_ref=dst,
            send_sem=ss,
            recv_sem=rs,
            device_id=at(row, col),
            device_id_type=MESH,
        )

    barrier = pltpu.get_barrier_semaphore()

    def greet(k, carry):
        row = lax.rem(m + k, n)
        pl.semaphore_signal(barrier, inc=1, device_id=at(row, c), device_id_type=MESH)
        pl.semaphore_signal(barrier, inc=1, device_id=at(row, other), device_id_type=MESH)
        return carry

    def greet_all():
        pl.semaphore_signal(barrier, inc=1, device_id=at(m, other), device_id_type=MESH)
        lax.fori_loop(1, n, greet, 0)

    loads = [
        pltpu.make_async_copy(src, dst, load_sem.at[k])
        for k, (src, dst) in enumerate(
            (
                (row_hbm, row_ref),
                (col_hbm, col_ref),
                (send_hbm, send_ref),
                (ms_hbm, ms_ref),
                (pan_hbm, pan_ref),
                (mix_hbm, mix_ref),
                (gain_hbm, gain_ref),
                (synth_hbm, synth_ref),
            )
        )
    ]
    row_load, col_load, send_load, ms_load, pan_load, *late_loads = loads
    row_load.start()
    col_load.start()
    greet_all()
    for load in loads[2:]:
        load.start()

    nodes_ref[...] = jnp.zeros_like(nodes_ref)
    row_load.wait()
    col_load.wait()
    nodes_ref[0:1, 0 : row_ref.shape[1]] = row_ref[...]
    nodes_ref[1:2, 0 : col_ref.shape[1]] = col_ref[...]
    nodes_all[c, m] = nodes_ref[...]
    pl.semaphore_wait(barrier, 2 * n - 1)

    def nodes_copy(slot_row, slot_col, row, col):
        return remote(
            nodes_ref,
            nodes_all.at[slot_col, slot_row],
            nodes_ss.at[col, row],
            nodes_rs.at[slot_col, slot_row],
            row,
            col,
        )

    def send_nodes(k, carry):
        row = lax.rem(m + k, n)
        nodes_copy(m, c, row, c).start()
        nodes_copy(m, c, row, other).start()
        return carry

    lax.fori_loop(1, n, send_nodes, 0)
    nodes_copy(m, c, m, other).start()
    send_load.wait()

    square = (own_blocks, own_blocks)
    wide = (own_blocks, LANES)
    owner = send_ref[0:1, :] // capacity
    key_row = (owner * KR + send_ref[1:2, :]) * KC + send_ref[2:3, :] - first_col
    key_row = jnp.broadcast_to(key_row, square)
    diagonal = iota(square, 0) == iota(square, 1)
    key_col = jnp.sum(jnp.where(diagonal, key_row, 0), axis=1, keepdims=True)
    same = key_row == key_col
    before = (key_row < key_col) | (same & (iota(square, 1) < iota(square, 0)))
    rank = jnp.sum(jnp.where(before, 1, 0), axis=1, keepdims=True)
    joined = jnp.sum(jnp.where(before & same, 1, 0), axis=1, keepdims=True)
    hit = rank == iota(wide, 1)
    order = jnp.sum(jnp.where(hit, iota(wide, 0), 0), axis=0, keepdims=True)
    keep = jnp.sum(jnp.where(hit & (joined > 0), 1, 0), axis=0, keepdims=True)
    table_ref[0:1, :] = order
    table_ref[1:2, :] = keep
    for g in range(pl.cdiv(cells, LANES)):
        cell = iota(wide, 1) + g * LANES
        ends = jnp.sum(jnp.where(key_col <= cell, 1, 0), axis=0, keepdims=True)
        count = jnp.sum(jnp.where(key_col == cell, 1, 0), axis=0, keepdims=True)
        table_ref[2 + g : 3 + g, :] = jnp.where(count > 0, ends, 0)
    table_copy = pltpu.make_async_copy(table_ref, table, load_sem.at[8])
    table_copy.start()

    column = iota(up_rows.shape, 1)
    rim = column - coarse_rows
    tap = jnp.where(
        column < coarse_rows, column + 2, rim % 2 + jnp.where(rim < 2 * bands, 0, coarse_rows + 2)
    )
    spot = (iota(up_rows.shape, 0).astype(F32) - 1.5) * 0.25 + 2.0
    up_rows[...] = cubic_weight(spot - tap.astype(F32)).astype(BF16)
    spot = (iota((1, TC), 1).astype(F32) - 1.5) * 0.25 + 2.0
    up_cols[0:coarse_cols, :] = spread(spot, 2.0, coarse_cols)
    start = jnp.where(c == 0, coarse_cols + 2, 0).astype(F32)
    shape = (PACK, TC)
    beside = [jnp.broadcast_to(cubic_weight(spot - (start + e)), shape) for e in (0.0, 1.0)]
    beside = jnp.where(iota(shape, 0) % 2 == 0, beside[0], beside[1]).astype(BF16)
    for g in range(LANES // PACK):
        up_cols[coarse_cols + g * PACK : coarse_cols + (g + 1) * PACK, :] = beside
    pan_sum[0] = jnp.zeros((size, size), BF16)
    ms_sum[0] = jnp.zeros((coarse_size, coarse_width), BF16)
    table_copy.wait()

    def running(source, sums):
        def step(p, total):
            total = total * table[1, p].astype(F32) + source[table[0, p]].astype(F32)
            sums[p + 1] = total.astype(BF16)
            return total

        start = jnp.zeros(source.shape[1:], F32)
        lax.fori_loop(0, own_blocks, step, start, unroll=2)

    ms_load.wait()
    running(ms_ref, ms_sum)
    pan_load.wait()
    running(pan_ref, pan_sum)

    def wait_nodes(k, carry):
        row = lax.rem(m + k, n)
        nodes_copy(row, c, row, c).wait()
        nodes_copy(row, other, row, other).wait()
        return carry

    lax.fori_loop(1, n, wait_nodes, 0)
    nodes_copy(m, other, m, other).wait()

    def cell_of(sums, tile, row, col):
        cell = tile * (KR * KC) + (row * KC + col)
        if cells <= LANES:
            return sums[table[2, cell]]
        return sums[table[2 + (cell >> LANE_BITS), cell & (LANES - 1)]]

    def stacked(sums, tile, col):
        return jnp.concatenate([cell_of(sums, tile, row, col) for row in range(KR)], axis=0)

    def ms_part(tile):
        row_nodes, nodes = nodes_all[c, tile, 0:1], nodes_all[c, tile, 1:2]
        after = nodes_all[1, tile, 1:2, 0:1]
        x_ms = col_coord(
            nodes, after, is_last, col_nodes, 4 * iota((1, coarse_cols), 1) + 1, 0.5
        )
        x_ms = (x_ms - 1.5) * 0.25
        col = spread(x_ms, (first_col * coarse_size).astype(F32), KC * coarse_size)
        spots = (row_coord(row_nodes, 4 * iota((coarse_rows, 1), 0) + 1, 0.5) - 1.5) * 0.25
        taps = iota((coarse_rows, KR * coarse_size), 1).astype(F32)
        weight = cubic_weight(spots - taps).astype(BF16)
        rows = [
            jnp.dot(weight, stacked(ms_sum, tile, k), preferred_element_type=F32).astype(BF16)
            for k in range(KC)
        ]
        by_band = [
            jnp.concatenate(
                [row[:, b * coarse_size : (b + 1) * coarse_size] for row in rows], axis=1
            )
            for b in range(bands)
        ]
        return jnp.dot(jnp.concatenate(by_band, axis=0), col, preferred_element_type=F32)

    def pan_part(tile):
        row_nodes, nodes = nodes_all[c, tile, 0:1], nodes_all[c, tile, 1:2]
        after = nodes_all[1, tile, 1:2, 0:1]
        x_pan = col_coord(nodes, after, is_last, col_nodes, iota((1, TC), 1), 0.0)
        col = spread(x_pan, (first_col * size).astype(F32), KC * size)
        row = spread(row_coord(row_nodes, iota((1, TR), 1), 0.0), 0.0, KR * size)
        rows = []
        for k in range(0, KC, 2):
            source = jnp.concatenate(
                [stacked(pan_sum, tile, j) for j in range(k, min(k + 2, KC))], axis=1
            )
            rows.append(
                lax.dot_general(
                    row, source, (((0,), (0,)), ((), ())), preferred_element_type=F32
                ).astype(BF16)
            )
        return jnp.dot(jnp.concatenate(rows, axis=1), col, preferred_element_type=F32)

    def line_of(k):
        up = lax.rem(pair * 2 + 2 + k, lines)
        down = lax.rem(pair * 2 + lines - 1 - k, lines)
        far = jnp.where(pair % 2 == 0, down, up)
        return jnp.where(k < lines - 2, far, jnp.where(k == lines - 2, partner, z))

    def ms_y(k):
        return remote(ms_y_send.at[k], ms_y_recv.at[k], ms_y_ss.at[k], ms_y_rs.at[k], twin, c)

    def pan_y(k, h):
        part = pl.ds(h * part_rows, part_rows)
        return remote(
            pan_y_send.at[k, part],
            pan_y_recv.at[k, part],
            pan_y_ss.at[k, h],
            pan_y_rs.at[k, h],
            twin,
            c,
        )

    def route(line):
        far = line // 2 != pair
        above = line // 2 > pair
        lower = z % 2 == 0
        inner = far & jnp.logical_xor(above, lower)
        outer = far & jnp.logical_not(jnp.logical_xor(above, lower))
        target = jnp.where(outer, partner, line)
        slot = jnp.where(outer, blocks + line, pair)
        return inner, target * 2 + y, slot

    def ms_z(k, row, slot):
        return remote(
            ms_z_send.at[k], ms_z_recv.at[slot], ms_z_ss.at[k], ms_z_rs.at[slot], row, c
        )

    def pan_z(k, h, row, slot):
        part = pl.ds(h * part_rows, part_rows)
        return remote(
            pan_z_send.at[k, part],
            pan_z_recv.at[slot, part],
            pan_z_ss.at[k, h],
            pan_z_rs.at[slot, h],
            row,
            c,
        )

    def each(first, last, step):
        if last - first == 1:
            step(first)
            return

        def body(k, carry):
            step(k)
            return carry

        lax.fori_loop(first, last, body, 0)

    near_row = partner * 2 + y

    near_ms = remote(near_ms_send, near_ms_recv, near_ss, near_rs, near_row, c)

    def ms_twin_parts(k):
        return [ms_part(line_of(k + i) * 2 + 1 - y) for i in range(2)]

    swap = route(line_of(lines - 3))[0]

    def pan_turn(k):
        first = jnp.where(swap, lines - 2, lines - 3)
        second = jnp.where(swap, lines - 3, lines - 2)
        return jnp.where(k == lines - 3, first, jnp.where(k == lines - 2, second, k))

    def pan_pair_to_twin(p):
        keys = [pan_turn(2 * p + i) for i in range(2)]
        parts = [pan_part(line_of(k) * 2 + 1 - y) for k in keys]
        for k, part in zip(keys, parts):
            pan_y_send[k] = part.astype(BF16)
        for k in keys:
            for h in range(HALVES):
                pan_y(k, h).start()

    def ms_own_parts(k):
        parts = [ms_part(line_of(k + i) * 2 + y) for i in range(2)]
        for i, part in enumerate(parts):
            ms_total[i] = part

    def ms_onward(k, i):
        line = line_of(k)
        inner, row, slot = route(line)
        ms_y(k).wait_recv()

        @pl.when(inner)
        def _():
            ms_z(0, row, blocks + line).wait_recv()
            relayed = ms_z_recv[blocks + line].astype(F32)
            total = ms_total[i] + ms_y_recv[k].astype(F32)
            ms_z_send[k] = (total + relayed).astype(BF16)

        @pl.when(jnp.logical_not(inner))
        def _():
            ms_z_send[k] = (ms_total[i] + ms_y_recv[k].astype(F32)).astype(BF16)

        ms_z(k, row, slot).start()

    def pan_own_part(k):
        pan_total[...] = pan_part(line_of(k) * 2 + y)

    def pan_forward(k):
        line = line_of(k)
        inner, row, slot = route(line)
        for h in range(HALVES):
            rows = slice(h * part_rows, (h + 1) * part_rows)
            pan_y(k, h).wait_recv()

            @pl.when(inner)
            def _():
                pan_z(0, h, row, blocks + line).wait_recv()
                relayed = pan_z_recv[blocks + line, rows].astype(F32)
                total = pan_total[rows, :] + pan_y_recv[k, rows].astype(F32)
                pan_z_send[k, rows] = (total + relayed).astype(BF16)

            @pl.when(jnp.logical_not(inner))
            def _():
                total = pan_total[rows, :] + pan_y_recv[k, rows].astype(F32)
                pan_z_send[k, rows] = total.astype(BF16)

            pan_z(k, h, row, slot).start()

    def pan_onward(k):
        pan_own_part(k)
        pan_forward(k)

    far = lines - 2
    last = lines - 1

    def ms_far_to_twin(p):
        for i, part in enumerate(ms_twin_parts(2 * p)):
            ms_y_send[2 * p + i] = part.astype(BF16)
        ms_y(2 * p).start()
        ms_y(2 * p + 1).start()

    def ms_far_onward(p):
        ms_own_parts(2 * p)
        ms_onward(2 * p, 0)
        ms_onward(2 * p + 1, 1)

    each(0, far // 2, ms_far_to_twin)
    parts = ms_twin_parts(far)
    near_ms_send[...] = parts[0].astype(BF16)
    ms_hold[...] = parts[1]
    near_ms.start()
    each(0, far // 2, pan_pair_to_twin)
    ms_own_parts(far)
    ms_z_send[far] = ms_total[0].astype(BF16)
    ms_z(far, near_row, pair).start()
    ms_mine[...] = ms_total[1]
    each(0, far // 2, ms_far_onward)
    near_ms.wait_recv()
    ms_y_send[last] = (ms_hold[...] + near_ms_recv[...].astype(F32)).astype(BF16)
    ms_y(last).start()
    pan_pair_to_twin(far // 2)
    each(0, far - 1, pan_onward)
    pan_mine[...] = pan_part(m)
    pan_own_part(pan_turn(far - 1))

    has_above, has_below = m > 0, m < n - 1

    def halo_copy(k, src, dst, row, col):
        return remote(src, dst, halo_ss.at[k], halo_rs.at[k], row, col)

    across_copy = halo_copy(0, edge_own, edge_all, m, other)
    up_copies = [
        halo_copy(1, rim_send.at[0], rim_recv.at[1], m - 1, c),
        halo_copy(2, edge_send.at[0], edge_recv.at[1], m - 1, other),
    ]
    down_copies = [
        halo_copy(3, rim_send.at[1], rim_recv.at[0], m + 1, c),
        halo_copy(4, edge_send.at[1], edge_recv.at[0], m + 1, other),
    ]
    def ms_finish():
        ms_y(last).wait_recv()
        ms_mine[...] += ms_y_recv[last].astype(F32)

        def ms_arrived(slot, carry):
            ms_z(0, m, slot).wait_recv()
            ms_mine[...] += ms_z_recv[slot].astype(F32)
            return carry

        lax.fori_loop(0, blocks, ms_arrived, 0)
        values = [ms_mine[b * coarse_rows : (b + 1) * coarse_rows, :] for b in range(bands)]
        synthetic = sum(synth_ref[b] * values[b] for b in range(bands))
        spot = iota((coarse_rows, LANES), 1) // 2
        edges = jnp.zeros((coarse_rows, LANES), F32)
        tops, bottoms = [], []
        for b in range(bands):
            result = values[b] - gain_ref[b] * synthetic
            for k in range(bands):
                result = result + mix_ref[b, k] * values[k]
            window[b] = result.astype(BF16)
            moved = pltpu.roll(result, jnp.where(c == 0, 2 * b + 2, 2 * b), 1)
            edges = jnp.where(spot == b, moved, edges)
            tops.append(result[0:2, :])
            bottoms.append(result[coarse_rows - 2 : coarse_rows, :])
        edge_own[...] = edges.astype(BF16)
        rim_send[0] = jnp.concatenate(tops, axis=0).astype(BF16)
        rim_send[1] = jnp.concatenate(bottoms, axis=0).astype(BF16)
        edge_send[0] = jnp.concatenate([edges[0:2, :]] * bands, axis=0).astype(BF16)
        bottom = edges[coarse_rows - 2 : coarse_rows, :]
        edge_send[1] = jnp.concatenate([bottom] * bands, axis=0).astype(BF16)

        across_copy.start()

        @pl.when(has_above)
        def _():
            for copy in up_copies:
                copy.start()

        @pl.when(has_below)
        def _():
            for copy in down_copies:
                copy.start()

    for load in late_loads:
        load.wait()
    pan_forward(pan_turn(far - 1))
    pan_own_part(pan_turn(far))
    ms_finish()
    pan_forward(pan_turn(far))
    across_copy.wait()

    edges = edge_all[...]
    spot = iota(edges.shape, 1) // 2
    source = jnp.concatenate(
        [
            jnp.concatenate(
                [window[b], jnp.where(spot == b, edges, jnp.zeros_like(edges))], axis=1
            )
            for b in range(bands)
        ],
        axis=0,
    )
    across[0 : bands * coarse_rows, :] = jnp.dot(
        source, up_cols[...], preferred_element_type=F32
    ).astype(BF16)
    for b in range(bands):
        own = slice(b * coarse_rows, (b + 1) * coarse_rows)
        mixed[b, PACK : TR - PACK, :] = jnp.dot(
            up_rows[PACK : TR - PACK, 0:coarse_rows],
            across[own, :],
            preferred_element_type=F32,
        ).astype(BF16)

    spans = ((PACK, TR - 2 * PACK), (0, PACK), (TR - PACK, PACK))
    stores = []
    for k, (begin, count) in enumerate(spans):
        span = pl.ds(begin, count)
        stores.append(
            pltpu.make_async_copy(
                mixed.at[:, span], mixed_hbm.at[:, span], load_sem.at[9 + k]
            )
        )
    stores[0].start()

    @pl.when(has_above)
    def _():
        for copy in up_copies:
            copy.wait_send()
        for copy in down_copies:
            copy.wait_recv()

    @pl.when(has_below)
    def _():
        for copy in down_copies:
            copy.wait_send()
        for copy in up_copies:
            copy.wait_recv()

    blank = jnp.zeros((2 * bands, LANES), BF16)

    @pl.when(jnp.logical_not(has_above))
    def _():
        rim_recv[0] = blank
        edge_recv[0] = blank

    @pl.when(jnp.logical_not(has_below))
    def _():
        rim_recv[1] = blank
        edge_recv[1] = blank

    spot = iota((2 * bands, LANES), 1) // 2
    mine = spot == iota((2 * bands, LANES), 0) // 2
    source = jnp.concatenate(
        [
            jnp.concatenate([rim_recv[i], jnp.where(mine, edge_recv[i], blank)], axis=1)
            for i in range(2)
        ],
        axis=0,
    )
    rims = jnp.dot(source, up_cols[...], preferred_element_type=F32).astype(BF16)
    outer = jnp.concatenate([up_rows[0:PACK, :], up_rows[TR - PACK : TR, :]], axis=0)
    column = iota(outer.shape, 1)
    owner_band = (column - coarse_rows) % (2 * bands) // 2
    for b in range(bands):
        weight = jnp.where((column < coarse_rows) | (owner_band == b), outer, jnp.zeros_like(outer))
        own = slice(b * coarse_rows, (b + 1) * coarse_rows)
        ends = jnp.dot(
            weight, jnp.concatenate([across[own, :], rims], axis=0), preferred_element_type=F32
        ).astype(BF16)
        mixed[b, 0:PACK, :] = ends[0:PACK, :]
        mixed[b, TR - PACK : TR, :] = ends[PACK : 2 * PACK, :]

    for k in (1, 2):
        stores[k].start()
    pan_stores = []
    for h in range(HALVES):
        rows = slice(h * part_rows, (h + 1) * part_rows)
        pan_y(last, h).wait_recv()
        pan_mine[rows, :] += pan_y_recv[last, rows].astype(F32)

        def pan_arrived(slot, carry):
            pan_z(0, h, m, slot).wait_recv()
            pan_mine[rows, :] += pan_z_recv[slot, rows].astype(F32)
            return carry

        lax.fori_loop(0, blocks, pan_arrived, 0)
        part = pl.ds(h * part_rows, part_rows)
        pan_stores.append(
            pltpu.make_async_copy(pan_mine.at[part], pan_hbm_out.at[part], load_sem.at[12 + h])
        )
        pan_stores[-1].start()

    def ms_y_sent(k, carry):
        ms_y(k).wait_send()
        return carry

    def pan_y_sent(k, carry):
        for h in range(HALVES):
            pan_y(k, h).wait_send()
        return carry

    def z_sent(k, carry):
        ms_z(k, m, 0).wait_send()
        for h in range(HALVES):
            pan_z(k, h, m, 0).wait_send()
        return carry

    near_ms.wait_send()
    lax.fori_loop(0, far, ms_y_sent, 0)
    ms_y(last).wait_send()
    lax.fori_loop(0, lines, pan_y_sent, 0)
    lax.fori_loop(0, lines - 1, z_sent, 0)
    for store in stores:
        store.wait()
    for pan_store in pan_stores:
        pan_store.wait()


def local(
    pan_blocks,
    ms_blocks,
    send_list,
    tile_list,
    row_grid,
    col_grid,
    band_mix,
    band_gain,
    synth_weight,
):
    n = lax.axis_size("mrow")
    lines = n // 2
    own_blocks, size, _ = pan_blocks.shape
    _, coarse_size, coarse_width = ms_blocks.shape
    capacity = tile_list.shape[1] // n
    bands = band_gain.shape[0]
    coarse_rows, coarse_cols = TR // 4, TC // 4
    table_rows = pl.cdiv(2 + pl.cdiv(n * KR * KC, LANES), 8) * 8
    hbm = pl.BlockSpec(memory_space=pl.ANY)
    dma = pltpu.SemaphoreType.DMA
    slots = lines // 2 + lines

    def ms_slots(count):
        return pltpu.VMEM((count, bands * coarse_rows, coarse_cols), BF16)

    def pan_slots(count):
        return pltpu.VMEM((count, TR, TC), BF16)

    mixed, pan_map = pl.pallas_call(
        functools.partial(mapping, capacity, col_grid.shape[1]),
        out_shape=(
            jax.ShapeDtypeStruct((bands, TR, TC), BF16),
            jax.ShapeDtypeStruct((TR, TC), F32),
        ),
        in_specs=[hbm] * 8,
        out_specs=(hbm, hbm),
        scratch_shapes=[
            pltpu.VMEM(send_list.shape, I32),
            pltpu.VMEM((1, row_grid.shape[0]), F32),
            pltpu.VMEM(col_grid.shape, F32),
            pltpu.SMEM(band_mix.shape, F32),
            pltpu.SMEM(band_gain.shape, F32),
            pltpu.SMEM(synth_weight.shape, F32),
            pltpu.VMEM(pan_blocks.shape, BF16),
            pltpu.VMEM(ms_blocks.shape, BF16),
            pltpu.VMEM((own_blocks + 1, size, size), BF16),
            pltpu.VMEM((own_blocks + 1, coarse_size, coarse_width), BF16),
            pltpu.VMEM((table_rows, LANES), I32),
            pltpu.SMEM((table_rows, LANES), I32),
            pltpu.VMEM((2, LANES), F32),
            pltpu.VMEM((2, n, 2, LANES), F32),
            ms_slots(lines),
            ms_slots(lines),
            pan_slots(lines),
            pan_slots(lines),
            ms_slots(lines - 1),
            ms_slots(slots),
            pan_slots(lines - 1),
            pan_slots(slots),
            pltpu.VMEM((bands * coarse_rows, coarse_cols), BF16),
            pltpu.VMEM((bands * coarse_rows, coarse_cols), BF16),
            pltpu.VMEM((TR, TC), F32),
            pltpu.VMEM((2, bands * coarse_rows, coarse_cols), F32),
            pltpu.VMEM((bands * coarse_rows, coarse_cols), F32),
            pltpu.VMEM((bands * coarse_rows, coarse_cols), F32),
            pltpu.VMEM((TR, TC), F32),
            pltpu.VMEM((bands, coarse_rows, coarse_cols), BF16),
            pltpu.VMEM((2, 2 * bands, LANES), BF16),
            pltpu.VMEM((2, 2 * bands, LANES), BF16),
            pltpu.VMEM((2, 2 * bands, LANES), BF16),
            pltpu.VMEM((2, 2 * bands, LANES), BF16),
            pltpu.VMEM((coarse_rows, LANES), BF16),
            pltpu.VMEM((coarse_rows, LANES), BF16),
            pltpu.VMEM((coarse_cols + LANES, TC), BF16),
            pltpu.VMEM((TR, coarse_rows + 4 * bands), BF16),
            pltpu.VMEM((bands * coarse_rows, TC), BF16),
            pltpu.VMEM((bands, TR, TC), BF16),
            dma((12 + HALVES,)),
            dma((2, n)),
            dma((2, n)),
            dma((lines,)),
            dma((lines,)),
            dma((lines, HALVES)),
            dma((lines, HALVES)),
            dma((lines - 1,)),
            dma((slots,)),
            dma((lines - 1, HALVES)),
            dma((slots, HALVES)),
            dma,
            dma,
            dma((5,)),
            dma((5,)),
        ],
        compiler_params=pltpu.CompilerParams(
            collective_id=0, has_side_effects=True, vmem_limit_bytes=60 * 1024 * 1024
        ),
        name="mapping",
    )(
        send_list,
        row_grid[None, :],
        col_grid,
        pan_blocks,
        ms_blocks,
        band_mix,
        band_gain,
        synth_weight,
    )
    detail = band_gain[:, None, None] * pan_map[None]
    return (mixed.astype(F32) + detail).astype(BF16)


def solution(mesh):
    return jax.shard_map(
        local,
        mesh=mesh,
        in_specs=(
            P(("scene", "mrow", "mcol"), None, None),
            P(("scene", "mrow", "mcol"), None, None),
            P(None, ("scene", "mrow", "mcol")),
            P(None, ("scene", "mrow", "mcol")),
            P(("scene", "mrow")),
            P(("scene", "mrow"), "mcol"),
            P(),
            P(),
            P(),
        ),
        out_specs=P(None, ("scene", "mrow"), "mcol"),
        check_vma=False,
    )
```

```python
import functools

import jax
import jax.numpy as jnp
from jax import lax
from jax.experimental import pallas as pl
from jax.experimental.pallas import tpu as pltpu
from jax.sharding import PartitionSpec as P

GRID = 64
TR = 128
TC = 512
KR = 2
KC = 5
LANE_BITS = 7
LANES = 1 << LANE_BITS
PACK = 16
HALVES = 2
MESH = pl.DeviceIdType.MESH
F32 = jnp.float32
BF16 = jnp.bfloat16
I32 = jnp.int32


def cubic_weight(offset):
    outer = jnp.maximum(2.0 - jnp.abs(offset), 0.0)
    shifted = outer - 1.0
    inner = jnp.maximum(shifted, 0.0)
    return outer * outer * (0.5 * shifted) + inner * inner * (1.0 - 2.0 * inner)


def iota(shape, dim):
    return lax.broadcasted_iota(I32, shape, dim)


def row_coord(nodes, position, offset):
    first = position < GRID
    a = jnp.where(first, nodes[:, 0:1], nodes[:, 1:2])
    b = jnp.where(first, nodes[:, 1:2], nodes[:, 2:3])
    within = (jnp.where(first, position, position - GRID).astype(F32) + offset) / GRID
    return a + (b - a) * within


def col_coord(nodes, after, is_last, count, position, offset):
    segment = position // GRID
    coord = jnp.zeros(position.shape, F32)
    for s in range(count):
        left, shift = nodes[:, s : s + 1], s * GRID
        if s + 1 < count:
            right = nodes[:, s + 1 : s + 2]
        else:
            right = jnp.where(is_last, left, after)
            left = jnp.where(is_last, nodes[:, s - 1 : s], left)
            shift = jnp.where(is_last, shift - GRID, shift)
        within = ((position - shift).astype(F32) + offset) / GRID
        coord = jnp.where(segment == s, left + (right - left) * within, coord)
    return coord


def spread(x, origin, size):
    base = jnp.floor(x)
    shape = (PACK, x.shape[1])
    taps = [
        jnp.broadcast_to(cubic_weight(x - (base + t)), shape).astype(BF16)
        for t in (-1.0, 0.0, 1.0, 2.0)
    ]
    groups = size // PACK
    first = base - 1.0 - origin
    group = jnp.floor(first * (1.0 / PACK))
    away = (iota(shape, 0).astype(F32) - (first - group * PACK)).astype(BF16)
    group = jnp.broadcast_to(jnp.clip(group, -2.0, groups + 1.0), shape).astype(BF16)
    none = jnp.zeros(shape, BF16)
    low, high = none, none
    for t in range(4):
        low = jnp.where(away == BF16(t), taps[t], low)
        high = jnp.where(away == BF16(t - PACK), taps[t], high)
    here = [group == BF16(g) for g in range(-1, groups)]
    return jnp.concatenate(
        [jnp.where(here[g + 1], low, jnp.where(here[g], high, none)) for g in range(groups)],
        axis=0,
    )


def mapping(
    capacity,
    col_nodes,
    send_hbm,
    row_hbm,
    col_hbm,
    pan_hbm,
    ms_hbm,
    mix_hbm,
    gain_hbm,
    synth_hbm,
    mixed_hbm,
    pan_hbm_out,
    send_ref,
    row_ref,
    col_ref,
    mix_ref,
    gain_ref,
    synth_ref,
    pan_ref,
    ms_ref,
    pan_sum,
    ms_sum,
    table_ref,
    table,
    nodes_ref,
    nodes_all,
    ms_y_send,
    ms_y_recv,
    pan_y_send,
    pan_y_recv,
    ms_z_send,
    ms_z_recv,
    pan_z_send,
    pan_z_recv,
    near_ms_send,
    near_ms_recv,
    pan_total,
    ms_total,
    ms_hold,
    ms_mine,
    pan_mine,
    window,
    rim_send,
    rim_recv,
    edge_send,
    edge_recv,
    edge_own,
    edge_all,
    up_cols,
    up_rows,
    across,
    mixed,
    load_sem,
    nodes_ss,
    nodes_rs,
    ms_y_ss,
    ms_y_rs,
    pan_y_ss,
    pan_y_rs,
    ms_z_ss,
    ms_z_rs,
    pan_z_ss,
    pan_z_rs,
    near_ss,
    near_rs,
    halo_ss,
    halo_rs,
):
    n = lax.axis_size("mrow")
    lines = n // 2
    blocks = lines // 2
    scene = lax.axis_index("scene")
    m = lax.axis_index("mrow")
    c = lax.axis_index("mcol")
    z, y = m // 2, m % 2
    twin = z * 2 + (1 - y)
    other = 1 - c
    pair = z // 2
    partner = pair * 2 + (1 - z % 2)
    own_blocks, size, _ = pan_ref.shape
    _, coarse_size, coarse_width = ms_ref.shape
    cells = n * KR * KC
    bands = mixed.shape[0]
    coarse_rows = TR // 4
    coarse_cols = TC // 4
    part_rows = TR // HALVES
    first_col = c * KC
    is_last = c == lax.axis_size("mcol") - 1

    def at(row, col):
        return (scene, row, col)

    def remote(src, dst, ss, rs, row, col):
        return pltpu.make_async_remote_copy(
            src_ref=src,
            dst_ref=dst,
            send_sem=ss,
            recv_sem=rs,
            device_id=at(row, col),
            device_id_type=MESH,
        )

    barrier = pltpu.get_barrier_semaphore()

    def greet(k, carry):
        row = lax.rem(m + k, n)
        pl.semaphore_signal(barrier, inc=1, device_id=at(row, c), device_id_type=MESH)
        pl.semaphore_signal(barrier, inc=1, device_id=at(row, other), device_id_type=MESH)
        return carry

    def greet_all():
        pl.semaphore_signal(barrier, inc=1, device_id=at(m, other), device_id_type=MESH)
        lax.fori_loop(1, n, greet, 0)

    loads = [
        pltpu.make_async_copy(src, dst, load_sem.at[k])
        for k, (src, dst) in enumerate(
            (
                (row_hbm, row_ref),
                (col_hbm, col_ref),
                (send_hbm, send_ref),
                (ms_hbm, ms_ref),
                (pan_hbm, pan_ref),
                (mix_hbm, mix_ref),
                (gain_hbm, gain_ref),
                (synth_hbm, synth_ref),
            )
        )
    ]
    row_load, col_load, send_load, ms_load, pan_load, *late_loads = loads
    row_load.start()
    col_load.start()
    greet_all()
    for load in loads[2:]:
        load.start()

    nodes_ref[...] = jnp.zeros_like(nodes_ref)
    row_load.wait()
    col_load.wait()
    nodes_ref[0:1, 0 : row_ref.shape[1]] = row_ref[...]
    nodes_ref[1:2, 0 : col_ref.shape[1]] = col_ref[...]
    nodes_all[c, m] = nodes_ref[...]
    pl.semaphore_wait(barrier, 2 * n - 1)

    def nodes_copy(slot_row, slot_col, row, col):
        return remote(
            nodes_ref,
            nodes_all.at[slot_col, slot_row],
            nodes_ss.at[col, row],
            nodes_rs.at[slot_col, slot_row],
            row,
            col,
        )

    def send_nodes(k, carry):
        row = lax.rem(m + k, n)
        nodes_copy(m, c, row, c).start()

        @pl.when(is_last)
        def _():
            nodes_copy(m, c, row, other).start()

        return carry

    lax.fori_loop(1, n, send_nodes, 0)

    @pl.when(is_last)
    def _():
        nodes_copy(m, c, m, other).start()

    send_load.wait()

    square = (own_blocks, own_blocks)
    wide = (own_blocks, LANES)
    owner = send_ref[0:1, :] // capacity
    key_row = (owner * KR + send_ref[1:2, :]) * KC + send_ref[2:3, :] - first_col
    key_row = jnp.broadcast_to(key_row, square)
    diagonal = iota(square, 0) == iota(square, 1)
    key_col = jnp.sum(jnp.where(diagonal, key_row, 0), axis=1, keepdims=True)
    same = key_row == key_col
    before = (key_row < key_col) | (same & (iota(square, 1) < iota(square, 0)))
    rank = jnp.sum(jnp.where(before, 1, 0), axis=1, keepdims=True)
    joined = jnp.sum(jnp.where(before & same, 1, 0), axis=1, keepdims=True)
    hit = rank == iota(wide, 1)
    order = jnp.sum(jnp.where(hit, iota(wide, 0), 0), axis=0, keepdims=True)
    keep = jnp.sum(jnp.where(hit & (joined > 0), 1, 0), axis=0, keepdims=True)
    table_ref[0:1, :] = order
    table_ref[1:2, :] = keep
    for g in range(pl.cdiv(cells, LANES)):
        cell = iota(wide, 1) + g * LANES
        ends = jnp.sum(jnp.where(key_col <= cell, 1, 0), axis=0, keepdims=True)
        count = jnp.sum(jnp.where(key_col == cell, 1, 0), axis=0, keepdims=True)
        table_ref[2 + g : 3 + g, :] = jnp.where(count > 0, ends, 0)
    table_copy = pltpu.make_async_copy(table_ref, table, load_sem.at[8])
    table_copy.start()

    column = iota(up_rows.shape, 1)
    rim = column - coarse_rows
    tap = jnp.where(
        column < coarse_rows, column + 2, rim % 2 + jnp.where(rim < 2 * bands, 0, coarse_rows + 2)
    )
    spot = (iota(up_rows.shape, 0).astype(F32) - 1.5) * 0.25 + 2.0
    up_rows[...] = cubic_weight(spot - tap.astype(F32)).astype(BF16)
    spot = (iota((1, TC), 1).astype(F32) - 1.5) * 0.25 + 2.0
    up_cols[0:coarse_cols, :] = spread(spot, 2.0, coarse_cols)
    start = jnp.where(c == 0, coarse_cols + 2, 0).astype(F32)
    shape = (PACK, TC)
    beside = [jnp.broadcast_to(cubic_weight(spot - (start + e)), shape) for e in (0.0, 1.0)]
    beside = jnp.where(iota(shape, 0) % 2 == 0, beside[0], beside[1]).astype(BF16)
    for g in range(LANES // PACK):
        up_cols[coarse_cols + g * PACK : coarse_cols + (g + 1) * PACK, :] = beside
    pan_sum[0] = jnp.zeros((size, size), BF16)
    ms_sum[0] = jnp.zeros((coarse_size, coarse_width), BF16)
    table_copy.wait()

    def running(source, sums):
        def step(p, total):
            total = total * table[1, p].astype(F32) + source[table[0, p]].astype(F32)
            sums[p + 1] = total.astype(BF16)
            return total

        start = jnp.zeros(source.shape[1:], F32)
        lax.fori_loop(0, own_blocks, step, start, unroll=2)

    ms_load.wait()
    running(ms_ref, ms_sum)
    pan_load.wait()
    running(pan_ref, pan_sum)

    def wait_beside(row):
        @pl.when(is_last)
        def _():
            nodes_copy(row, other, row, other).wait_send()

        @pl.when(jnp.logical_not(is_last))
        def _():
            nodes_copy(row, other, row, other).wait_recv()

    def wait_nodes(k, carry):
        row = lax.rem(m + k, n)
        nodes_copy(row, c, row, c).wait()
        wait_beside(row)
        return carry

    lax.fori_loop(1, n, wait_nodes, 0)
    wait_beside(m)

    def cell_of(sums, tile, row, col):
        cell = tile * (KR * KC) + (row * KC + col)
        if cells <= LANES:
            return sums[table[2, cell]]
        return sums[table[2 + (cell >> LANE_BITS), cell & (LANES - 1)]]

    def stacked(sums, tile, col):
        return jnp.concatenate([cell_of(sums, tile, row, col) for row in range(KR)], axis=0)

    def ms_part(tile):
        row_nodes, nodes = nodes_all[c, tile, 0:1], nodes_all[c, tile, 1:2]
        after = nodes_all[1, tile, 1:2, 0:1]
        x_ms = col_coord(
            nodes, after, is_last, col_nodes, 4 * iota((1, coarse_cols), 1) + 1, 0.5
        )
        x_ms = (x_ms - 1.5) * 0.25
        col = spread(x_ms, (first_col * coarse_size).astype(F32), KC * coarse_size)
        spots = (row_coord(row_nodes, 4 * iota((coarse_rows, 1), 0) + 1, 0.5) - 1.5) * 0.25
        taps = iota((coarse_rows, KR * coarse_size), 1).astype(F32)
        weight = cubic_weight(spots - taps).astype(BF16)
        rows = [
            jnp.dot(weight, stacked(ms_sum, tile, k), preferred_element_type=F32).astype(BF16)
            for k in range(KC)
        ]
        by_band = [
            jnp.concatenate(
                [row[:, b * coarse_size : (b + 1) * coarse_size] for row in rows], axis=1
            )
            for b in range(bands)
        ]
        return jnp.dot(jnp.concatenate(by_band, axis=0), col, preferred_element_type=F32)

    def pan_part(tile):
        row_nodes, nodes = nodes_all[c, tile, 0:1], nodes_all[c, tile, 1:2]
        after = nodes_all[1, tile, 1:2, 0:1]
        x_pan = col_coord(nodes, after, is_last, col_nodes, iota((1, TC), 1), 0.0)
        col = spread(x_pan, (first_col * size).astype(F32), KC * size)
        row = spread(row_coord(row_nodes, iota((1, TR), 1), 0.0), 0.0, KR * size)
        rows = []
        for k in range(0, KC, 2):
            source = jnp.concatenate(
                [stacked(pan_sum, tile, j) for j in range(k, min(k + 2, KC))], axis=1
            )
            rows.append(
                lax.dot_general(
                    row, source, (((0,), (0,)), ((), ())), preferred_element_type=F32
                ).astype(BF16)
            )
        return jnp.dot(jnp.concatenate(rows, axis=1), col, preferred_element_type=F32)

    def line_of(k):
        up = lax.rem(pair * 2 + 2 + k, lines)
        down = lax.rem(pair * 2 + lines - 1 - k, lines)
        far = jnp.where(pair % 2 == 0, down, up)
        return jnp.where(k < lines - 2, far, jnp.where(k == lines - 2, partner, z))

    def ms_y(k):
        return remote(ms_y_send.at[k], ms_y_recv.at[k], ms_y_ss.at[k], ms_y_rs.at[k], twin, c)

    def pan_y(k, h):
        part = pl.ds(h * part_rows, part_rows)
        return remote(
            pan_y_send.at[k, part],
            pan_y_recv.at[k, part],
            pan_y_ss.at[k, h],
            pan_y_rs.at[k, h],
            twin,
            c,
        )

    def route(line):
        far = line // 2 != pair
        above = line // 2 > pair
        lower = z % 2 == 0
        inner = far & jnp.logical_xor(above, lower)
        outer = far & jnp.logical_not(jnp.logical_xor(above, lower))
        target = jnp.where(outer, partner, line)
        slot = jnp.where(outer, blocks + line, pair)
        return inner, target * 2 + y, slot

    def ms_z(k, row, slot):
        return remote(
            ms_z_send.at[k], ms_z_recv.at[slot], ms_z_ss.at[k], ms_z_rs.at[slot], row, c
        )

    def pan_z(k, h, row, slot):
        part = pl.ds(h * part_rows, part_rows)
        return remote(
            pan_z_send.at[k, part],
            pan_z_recv.at[slot, part],
            pan_z_ss.at[k, h],
            pan_z_rs.at[slot, h],
            row,
            c,
        )

    def each(first, last, step):
        if last - first == 1:
            step(first)
            return

        def body(k, carry):
            step(k)
            return carry

        lax.fori_loop(first, last, body, 0)

    near_row = partner * 2 + y

    near_ms = remote(near_ms_send, near_ms_recv, near_ss, near_rs, near_row, c)

    def ms_twin_parts(k):
        return [ms_part(line_of(k + i) * 2 + 1 - y) for i in range(2)]

    swap = route(line_of(lines - 3))[0]

    def pan_turn(k):
        first = jnp.where(swap, lines - 2, lines - 3)
        second = jnp.where(swap, lines - 3, lines - 2)
        return jnp.where(k == lines - 3, first, jnp.where(k == lines - 2, second, k))

    def pan_pair_to_twin(p):
        keys = [pan_turn(2 * p + i) for i in range(2)]
        parts = [pan_part(line_of(k) * 2 + 1 - y) for k in keys]
        for k, part in zip(keys, parts):
            pan_y_send[k] = part.astype(BF16)
        for k in keys:
            for h in range(HALVES):
                pan_y(k, h).start()

    def ms_own_parts(k):
        parts = [ms_part(line_of(k + i) * 2 + y) for i in range(2)]
        for i, part in enumerate(parts):
            ms_total[i] = part

    def ms_onward(k, i):
        line = line_of(k)
        inner, row, slot = route(line)
        ms_y(k).wait_recv()

        @pl.when(inner)
        def _():
            ms_z(0, row, blocks + line).wait_recv()
            relayed = ms_z_recv[blocks + line].astype(F32)
            total = ms_total[i] + ms_y_recv[k].astype(F32)
            ms_z_send[k] = (total + relayed).astype(BF16)

        @pl.when(jnp.logical_not(inner))
        def _():
            ms_z_send[k] = (ms_total[i] + ms_y_recv[k].astype(F32)).astype(BF16)

        ms_z(k, row, slot).start()

    def pan_own_part(k):
        pan_total[...] = pan_part(line_of(k) * 2 + y)

    def pan_forward(k):
        line = line_of(k)
        inner, row, slot = route(line)
        for h in range(HALVES):
            rows = slice(h * part_rows, (h + 1) * part_rows)
            pan_y(k, h).wait_recv()

            @pl.when(inner)
            def _():
                pan_z(0, h, row, blocks + line).wait_recv()
                relayed = pan_z_recv[blocks + line, rows].astype(F32)
                total = pan_total[rows, :] + pan_y_recv[k, rows].astype(F32)
                pan_z_send[k, rows] = (total + relayed).astype(BF16)

            @pl.when(jnp.logical_not(inner))
            def _():
                total = pan_total[rows, :] + pan_y_recv[k, rows].astype(F32)
                pan_z_send[k, rows] = total.astype(BF16)

            pan_z(k, h, row, slot).start()

    def pan_onward(k):
        pan_own_part(k)
        pan_forward(k)

    far = lines - 2
    last = lines - 1

    def ms_far_to_twin(p):
        for i, part in enumerate(ms_twin_parts(2 * p)):
            ms_y_send[2 * p + i] = part.astype(BF16)
        ms_y(2 * p).start()
        ms_y(2 * p + 1).start()

    def ms_far_onward(p):
        ms_own_parts(2 * p)
        ms_onward(2 * p, 0)
        ms_onward(2 * p + 1, 1)

    each(0, far // 2, ms_far_to_twin)
    parts = ms_twin_parts(far)
    near_ms_send[...] = parts[0].astype(BF16)
    ms_hold[...] = parts[1]
    near_ms.start()
    ms_own_parts(far)
    ms_z_send[far] = ms_total[0].astype(BF16)
    ms_z(far, near_row, pair).start()
    ms_mine[...] = ms_total[1]
    each(0, far // 2, pan_pair_to_twin)
    each(0, far // 2, ms_far_onward)
    near_ms.wait_recv()
    ms_y_send[last] = (ms_hold[...] + near_ms_recv[...].astype(F32)).astype(BF16)
    ms_y(last).start()
    pan_pair_to_twin(far // 2)
    each(0, far - 1, pan_onward)
    pan_mine[...] = pan_part(m)
    pan_own_part(pan_turn(far - 1))

    has_above, has_below = m > 0, m < n - 1

    def halo_copy(k, src, dst, row, col):
        return remote(src, dst, halo_ss.at[k], halo_rs.at[k], row, col)

    across_copy = halo_copy(0, edge_own, edge_all, m, other)
    up_copies = [
        halo_copy(1, rim_send.at[0], rim_recv.at[1], m - 1, c),
        halo_copy(2, edge_send.at[0], edge_recv.at[1], m - 1, other),
    ]
    down_copies = [
        halo_copy(3, rim_send.at[1], rim_recv.at[0], m + 1, c),
        halo_copy(4, edge_send.at[1], edge_recv.at[0], m + 1, other),
    ]
    def ms_finish():
        ms_y(last).wait_recv()
        ms_mine[...] += ms_y_recv[last].astype(F32)

        def ms_arrived(slot, carry):
            ms_z(0, m, slot).wait_recv()
            ms_mine[...] += ms_z_recv[slot].astype(F32)
            return carry

        lax.fori_loop(0, blocks, ms_arrived, 0)
        values = [ms_mine[b * coarse_rows : (b + 1) * coarse_rows, :] for b in range(bands)]
        synthetic = sum(synth_ref[b] * values[b] for b in range(bands))
        spot = iota((coarse_rows, LANES), 1) // 2
        edges = jnp.zeros((coarse_rows, LANES), F32)
        tops, bottoms = [], []
        for b in range(bands):
            result = values[b] - gain_ref[b] * synthetic
            for k in range(bands):
                result = result + mix_ref[b, k] * values[k]
            window[b] = result.astype(BF16)
            moved = pltpu.roll(result, jnp.where(c == 0, 2 * b + 2, 2 * b), 1)
            edges = jnp.where(spot == b, moved, edges)
            tops.append(result[0:2, :])
            bottoms.append(result[coarse_rows - 2 : coarse_rows, :])
        edge_own[...] = edges.astype(BF16)
        rim_send[0] = jnp.concatenate(tops, axis=0).astype(BF16)
        rim_send[1] = jnp.concatenate(bottoms, axis=0).astype(BF16)
        edge_send[0] = jnp.concatenate([edges[0:2, :]] * bands, axis=0).astype(BF16)
        bottom = edges[coarse_rows - 2 : coarse_rows, :]
        edge_send[1] = jnp.concatenate([bottom] * bands, axis=0).astype(BF16)

        across_copy.start()

        @pl.when(has_above)
        def _():
            for copy in up_copies:
                copy.start()

        @pl.when(has_below)
        def _():
            for copy in down_copies:
                copy.start()

    for load in late_loads:
        load.wait()
    pan_forward(pan_turn(far - 1))
    pan_own_part(pan_turn(far))
    ms_finish()
    pan_forward(pan_turn(far))
    across_copy.wait()

    edges = edge_all[...]
    spot = iota(edges.shape, 1) // 2
    source = jnp.concatenate(
        [
            jnp.concatenate(
                [window[b], jnp.where(spot == b, edges, jnp.zeros_like(edges))], axis=1
            )
            for b in range(bands)
        ],
        axis=0,
    )
    across[0 : bands * coarse_rows, :] = jnp.dot(
        source, up_cols[...], preferred_element_type=F32
    ).astype(BF16)
    for b in range(bands):
        own = slice(b * coarse_rows, (b + 1) * coarse_rows)
        mixed[b, PACK : TR - PACK, :] = jnp.dot(
            up_rows[PACK : TR - PACK, 0:coarse_rows],
            across[own, :],
            preferred_element_type=F32,
        ).astype(BF16)

    spans = ((PACK, TR - 2 * PACK), (0, PACK), (TR - PACK, PACK))
    stores = []
    for k, (begin, count) in enumerate(spans):
        span = pl.ds(begin, count)
        stores.append(
            pltpu.make_async_copy(
                mixed.at[:, span], mixed_hbm.at[:, span], load_sem.at[9 + k]
            )
        )
    stores[0].start()

    @pl.when(has_above)
    def _():
        for copy in up_copies:
            copy.wait_send()
        for copy in down_copies:
            copy.wait_recv()

    @pl.when(has_below)
    def _():
        for copy in down_copies:
            copy.wait_send()
        for copy in up_copies:
            copy.wait_recv()

    blank = jnp.zeros((2 * bands, LANES), BF16)

    @pl.when(jnp.logical_not(has_above))
    def _():
        rim_recv[0] = blank
        edge_recv[0] = blank

    @pl.when(jnp.logical_not(has_below))
    def _():
        rim_recv[1] = blank
        edge_recv[1] = blank

    spot = iota((2 * bands, LANES), 1) // 2
    mine = spot == iota((2 * bands, LANES), 0) // 2
    source = jnp.concatenate(
        [
            jnp.concatenate([rim_recv[i], jnp.where(mine, edge_recv[i], blank)], axis=1)
            for i in range(2)
        ],
        axis=0,
    )
    rims = jnp.dot(source, up_cols[...], preferred_element_type=F32).astype(BF16)
    outer = jnp.concatenate([up_rows[0:PACK, :], up_rows[TR - PACK : TR, :]], axis=0)
    column = iota(outer.shape, 1)
    owner_band = (column - coarse_rows) % (2 * bands) // 2
    for b in range(bands):
        weight = jnp.where((column < coarse_rows) | (owner_band == b), outer, jnp.zeros_like(outer))
        own = slice(b * coarse_rows, (b + 1) * coarse_rows)
        ends = jnp.dot(
            weight, jnp.concatenate([across[own, :], rims], axis=0), preferred_element_type=F32
        ).astype(BF16)
        mixed[b, 0:PACK, :] = ends[0:PACK, :]
        mixed[b, TR - PACK : TR, :] = ends[PACK : 2 * PACK, :]

    for k in (1, 2):
        stores[k].start()
    pan_stores = []
    for h in range(HALVES):
        rows = slice(h * part_rows, (h + 1) * part_rows)
        pan_y(last, h).wait_recv()
        pan_mine[rows, :] += pan_y_recv[last, rows].astype(F32)

        def pan_arrived(slot, carry):
            pan_z(0, h, m, slot).wait_recv()
            pan_mine[rows, :] += pan_z_recv[slot, rows].astype(F32)
            return carry

        lax.fori_loop(0, blocks, pan_arrived, 0)
        part = pl.ds(h * part_rows, part_rows)
        pan_stores.append(
            pltpu.make_async_copy(pan_mine.at[part], pan_hbm_out.at[part], load_sem.at[12 + h])
        )
        pan_stores[-1].start()

    def ms_y_sent(k, carry):
        ms_y(k).wait_send()
        return carry

    def pan_y_sent(k, carry):
        for h in range(HALVES):
            pan_y(k, h).wait_send()
        return carry

    def z_sent(k, carry):
        ms_z(k, m, 0).wait_send()
        for h in range(HALVES):
            pan_z(k, h, m, 0).wait_send()
        return carry

    near_ms.wait_send()
    lax.fori_loop(0, far, ms_y_sent, 0)
    ms_y(last).wait_send()
    lax.fori_loop(0, lines, pan_y_sent, 0)
    lax.fori_loop(0, lines - 1, z_sent, 0)
    for store in stores:
        store.wait()
    for pan_store in pan_stores:
        pan_store.wait()


def local(
    pan_blocks,
    ms_blocks,
    send_list,
    tile_list,
    row_grid,
    col_grid,
    band_mix,
    band_gain,
    synth_weight,
):
    n = lax.axis_size("mrow")
    lines = n // 2
    own_blocks, size, _ = pan_blocks.shape
    _, coarse_size, coarse_width = ms_blocks.shape
    capacity = tile_list.shape[1] // n
    bands = band_gain.shape[0]
    coarse_rows, coarse_cols = TR // 4, TC // 4
    table_rows = pl.cdiv(2 + pl.cdiv(n * KR * KC, LANES), 8) * 8
    hbm = pl.BlockSpec(memory_space=pl.ANY)
    dma = pltpu.SemaphoreType.DMA
    slots = lines // 2 + lines

    def ms_slots(count):
        return pltpu.VMEM((count, bands * coarse_rows, coarse_cols), BF16)

    def pan_slots(count):
        return pltpu.VMEM((count, TR, TC), BF16)

    mixed, pan_map = pl.pallas_call(
        functools.partial(mapping, capacity, col_grid.shape[1]),
        out_shape=(
            jax.ShapeDtypeStruct((bands, TR, TC), BF16),
            jax.ShapeDtypeStruct((TR, TC), F32),
        ),
        in_specs=[hbm] * 8,
        out_specs=(hbm, hbm),
        scratch_shapes=[
            pltpu.VMEM(send_list.shape, I32),
            pltpu.VMEM((1, row_grid.shape[0]), F32),
            pltpu.VMEM(col_grid.shape, F32),
            pltpu.SMEM(band_mix.shape, F32),
            pltpu.SMEM(band_gain.shape, F32),
            pltpu.SMEM(synth_weight.shape, F32),
            pltpu.VMEM(pan_blocks.shape, BF16),
            pltpu.VMEM(ms_blocks.shape, BF16),
            pltpu.VMEM((own_blocks + 1, size, size), BF16),
            pltpu.VMEM((own_blocks + 1, coarse_size, coarse_width), BF16),
            pltpu.VMEM((table_rows, LANES), I32),
            pltpu.SMEM((table_rows, LANES), I32),
            pltpu.VMEM((2, LANES), F32),
            pltpu.VMEM((2, n, 2, LANES), F32),
            ms_slots(lines),
            ms_slots(lines),
            pan_slots(lines),
            pan_slots(lines),
            ms_slots(lines - 1),
            ms_slots(slots),
            pan_slots(lines - 1),
            pan_slots(slots),
            pltpu.VMEM((bands * coarse_rows, coarse_cols), BF16),
            pltpu.VMEM((bands * coarse_rows, coarse_cols), BF16),
            pltpu.VMEM((TR, TC), F32),
            pltpu.VMEM((2, bands * coarse_rows, coarse_cols), F32),
            pltpu.VMEM((bands * coarse_rows, coarse_cols), F32),
            pltpu.VMEM((bands * coarse_rows, coarse_cols), F32),
            pltpu.VMEM((TR, TC), F32),
            pltpu.VMEM((bands, coarse_rows, coarse_cols), BF16),
            pltpu.VMEM((2, 2 * bands, LANES), BF16),
            pltpu.VMEM((2, 2 * bands, LANES), BF16),
            pltpu.VMEM((2, 2 * bands, LANES), BF16),
            pltpu.VMEM((2, 2 * bands, LANES), BF16),
            pltpu.VMEM((coarse_rows, LANES), BF16),
            pltpu.VMEM((coarse_rows, LANES), BF16),
            pltpu.VMEM((coarse_cols + LANES, TC), BF16),
            pltpu.VMEM((TR, coarse_rows + 4 * bands), BF16),
            pltpu.VMEM((bands * coarse_rows, TC), BF16),
            pltpu.VMEM((bands, TR, TC), BF16),
            dma((12 + HALVES,)),
            dma((2, n)),
            dma((2, n)),
            dma((lines,)),
            dma((lines,)),
            dma((lines, HALVES)),
            dma((lines, HALVES)),
            dma((lines - 1,)),
            dma((slots,)),
            dma((lines - 1, HALVES)),
            dma((slots, HALVES)),
            dma,
            dma,
            dma((5,)),
            dma((5,)),
        ],
        compiler_params=pltpu.CompilerParams(
            collective_id=0, has_side_effects=True, vmem_limit_bytes=60 * 1024 * 1024
        ),
        name="mapping",
    )(
        send_list,
        row_grid[None, :],
        col_grid,
        pan_blocks,
        ms_blocks,
        band_mix,
        band_gain,
        synth_weight,
    )
    detail = band_gain[:, None, None] * pan_map[None]
    return (mixed.astype(F32) + detail).astype(BF16)


def solution(mesh):
    return jax.shard_map(
        local,
        mesh=mesh,
        in_specs=(
            P(("scene", "mrow", "mcol"), None, None),
            P(("scene", "mrow", "mcol"), None, None),
            P(None, ("scene", "mrow", "mcol")),
            P(None, ("scene", "mrow", "mcol")),
            P(("scene", "mrow")),
            P(("scene", "mrow"), "mcol"),
            P(),
            P(),
            P(),
        ),
        out_specs=P(None, ("scene", "mrow"), "mcol"),
        check_vma=False,
    )
```

```python
import functools

import jax
import jax.numpy as jnp
from jax import lax
from jax.experimental import pallas as pl
from jax.experimental.pallas import tpu as pltpu
from jax.sharding import PartitionSpec as P

GRID = 64
TR = 128
TC = 512
KR = 2
KC = 5
LANE_BITS = 7
LANES = 1 << LANE_BITS
PACK = 16
HALVES = 2
MESH = pl.DeviceIdType.MESH
F32 = jnp.float32
BF16 = jnp.bfloat16
I32 = jnp.int32


def cubic_weight(offset):
    outer = jnp.maximum(2.0 - jnp.abs(offset), 0.0)
    shifted = outer - 1.0
    inner = jnp.maximum(shifted, 0.0)
    return outer * outer * (0.5 * shifted) + inner * inner * (1.0 - 2.0 * inner)


def iota(shape, dim):
    return lax.broadcasted_iota(I32, shape, dim)


def row_coord(nodes, position, offset):
    first = position < GRID
    a = jnp.where(first, nodes[:, 0:1], nodes[:, 1:2])
    b = jnp.where(first, nodes[:, 1:2], nodes[:, 2:3])
    within = (jnp.where(first, position, position - GRID).astype(F32) + offset) / GRID
    return a + (b - a) * within


def col_coord(nodes, after, is_last, count, position, offset):
    segment = position // GRID
    coord = jnp.zeros(position.shape, F32)
    for s in range(count):
        left, shift = nodes[:, s : s + 1], s * GRID
        if s + 1 < count:
            right = nodes[:, s + 1 : s + 2]
        else:
            right = jnp.where(is_last, left, after)
            left = jnp.where(is_last, nodes[:, s - 1 : s], left)
            shift = jnp.where(is_last, shift - GRID, shift)
        within = ((position - shift).astype(F32) + offset) / GRID
        coord = jnp.where(segment == s, left + (right - left) * within, coord)
    return coord


def spread(x, origin, size):
    base = jnp.floor(x)
    shape = (PACK, x.shape[1])
    taps = [
        jnp.broadcast_to(cubic_weight(x - (base + t)), shape).astype(BF16)
        for t in (-1.0, 0.0, 1.0, 2.0)
    ]
    groups = size // PACK
    first = base - 1.0 - origin
    group = jnp.floor(first * (1.0 / PACK))
    away = (iota(shape, 0).astype(F32) - (first - group * PACK)).astype(BF16)
    group = jnp.broadcast_to(jnp.clip(group, -2.0, groups + 1.0), shape).astype(BF16)
    none = jnp.zeros(shape, BF16)
    low, high = none, none
    for t in range(4):
        low = jnp.where(away == BF16(t), taps[t], low)
        high = jnp.where(away == BF16(t - PACK), taps[t], high)
    here = [group == BF16(g) for g in range(-1, groups)]
    return jnp.concatenate(
        [jnp.where(here[g + 1], low, jnp.where(here[g], high, none)) for g in range(groups)],
        axis=0,
    )


def mapping(
    capacity,
    col_nodes,
    send_hbm,
    row_hbm,
    col_hbm,
    pan_hbm,
    ms_hbm,
    mix_hbm,
    gain_hbm,
    synth_hbm,
    mixed_hbm,
    pan_hbm_out,
    send_ref,
    row_ref,
    col_ref,
    mix_ref,
    gain_ref,
    synth_ref,
    pan_ref,
    ms_ref,
    pan_sum,
    ms_sum,
    table_ref,
    table,
    nodes_ref,
    nodes_all,
    ms_y_send,
    ms_y_recv,
    pan_y_send,
    pan_y_recv,
    ms_z_send,
    ms_z_recv,
    pan_z_send,
    pan_z_recv,
    near_ms_send,
    near_ms_recv,
    pan_total,
    ms_total,
    ms_hold,
    ms_mine,
    pan_mine,
    window,
    rim_send,
    rim_recv,
    edge_send,
    edge_recv,
    edge_own,
    edge_all,
    up_cols,
    up_rows,
    across,
    mixed,
    load_sem,
    nodes_ss,
    nodes_rs,
    ms_y_ss,
    ms_y_rs,
    pan_y_ss,
    pan_y_rs,
    ms_z_ss,
    ms_z_rs,
    pan_z_ss,
    pan_z_rs,
    near_ss,
    near_rs,
    halo_ss,
    halo_rs,
):
    n = lax.axis_size("mrow")
    lines = n // 2
    blocks = lines // 2
    scene = lax.axis_index("scene")
    m = lax.axis_index("mrow")
    c = lax.axis_index("mcol")
    z, y = m // 2, m % 2
    twin = z * 2 + (1 - y)
    other = 1 - c
    pair = z // 2
    partner = pair * 2 + (1 - z % 2)
    own_blocks, size, _ = pan_ref.shape
    _, coarse_size, coarse_width = ms_ref.shape
    cells = n * KR * KC
    bands = mixed.shape[0]
    coarse_rows = TR // 4
    coarse_cols = TC // 4
    part_rows = TR // HALVES
    first_col = c * KC
    is_last = c == lax.axis_size("mcol") - 1

    def at(row, col):
        return (scene, row, col)

    def remote(src, dst, ss, rs, row, col):
        return pltpu.make_async_remote_copy(
            src_ref=src,
            dst_ref=dst,
            send_sem=ss,
            recv_sem=rs,
            device_id=at(row, col),
            device_id_type=MESH,
        )

    barrier = pltpu.get_barrier_semaphore()

    def greet(k, carry):
        row = lax.rem(m + k, n)
        pl.semaphore_signal(barrier, inc=1, device_id=at(row, c), device_id_type=MESH)
        pl.semaphore_signal(barrier, inc=1, device_id=at(row, other), device_id_type=MESH)
        return carry

    def greet_all():
        pl.semaphore_signal(barrier, inc=1, device_id=at(m, other), device_id_type=MESH)
        lax.fori_loop(1, n, greet, 0)

    loads = [
        pltpu.make_async_copy(src, dst, load_sem.at[k])
        for k, (src, dst) in enumerate(
            (
                (row_hbm, row_ref),
                (col_hbm, col_ref),
                (send_hbm, send_ref),
                (ms_hbm, ms_ref),
                (pan_hbm, pan_ref),
                (mix_hbm, mix_ref),
                (gain_hbm, gain_ref),
                (synth_hbm, synth_ref),
            )
        )
    ]
    row_load, col_load, send_load, ms_load, pan_load, *late_loads = loads
    row_load.start()
    col_load.start()
    greet_all()
    for load in loads[2:]:
        load.start()

    nodes_ref[...] = jnp.zeros_like(nodes_ref)
    row_load.wait()
    col_load.wait()
    nodes_ref[0:1, 0 : row_ref.shape[1]] = row_ref[...]
    nodes_ref[1:2, 0 : col_ref.shape[1]] = col_ref[...]
    nodes_all[c, m] = nodes_ref[...]
    pl.semaphore_wait(barrier, 2 * n - 1)

    def nodes_copy(slot_row, slot_col, row, col):
        return remote(
            nodes_ref,
            nodes_all.at[slot_col, slot_row],
            nodes_ss.at[col, row],
            nodes_rs.at[slot_col, slot_row],
            row,
            col,
        )

    def send_nodes(k, carry):
        row = lax.rem(m + k, n)

        @pl.when(is_last)
        def _():
            nodes_copy(m, c, row, other).start()

        nodes_copy(m, c, row, c).start()

        return carry

    lax.fori_loop(1, n, send_nodes, 0)

    @pl.when(is_last)
    def _():
        nodes_copy(m, c, m, other).start()

    send_load.wait()

    square = (own_blocks, own_blocks)
    wide = (own_blocks, LANES)
    owner = send_ref[0:1, :] // capacity
    key_row = (owner * KR + send_ref[1:2, :]) * KC + send_ref[2:3, :] - first_col
    key_row = jnp.broadcast_to(key_row, square)
    diagonal = iota(square, 0) == iota(square, 1)
    key_col = jnp.sum(jnp.where(diagonal, key_row, 0), axis=1, keepdims=True)
    same = key_row == key_col
    before = (key_row < key_col) | (same & (iota(square, 1) < iota(square, 0)))
    rank = jnp.sum(jnp.where(before, 1, 0), axis=1, keepdims=True)
    joined = jnp.sum(jnp.where(before & same, 1, 0), axis=1, keepdims=True)
    hit = rank == iota(wide, 1)
    order = jnp.sum(jnp.where(hit, iota(wide, 0), 0), axis=0, keepdims=True)
    keep = jnp.sum(jnp.where(hit & (joined > 0), 1, 0), axis=0, keepdims=True)
    table_ref[0:1, :] = order
    table_ref[1:2, :] = keep
    for g in range(pl.cdiv(cells, LANES)):
        cell = iota(wide, 1) + g * LANES
        ends = jnp.sum(jnp.where(key_col <= cell, 1, 0), axis=0, keepdims=True)
        count = jnp.sum(jnp.where(key_col == cell, 1, 0), axis=0, keepdims=True)
        table_ref[2 + g : 3 + g, :] = jnp.where(count > 0, ends, 0)
    table_copy = pltpu.make_async_copy(table_ref, table, load_sem.at[8])
    table_copy.start()

    column = iota(up_rows.shape, 1)
    rim = column - coarse_rows
    tap = jnp.where(
        column < coarse_rows, column + 2, rim % 2 + jnp.where(rim < 2 * bands, 0, coarse_rows + 2)
    )
    spot = (iota(up_rows.shape, 0).astype(F32) - 1.5) * 0.25 + 2.0
    up_rows[...] = cubic_weight(spot - tap.astype(F32)).astype(BF16)
    spot = (iota((1, TC), 1).astype(F32) - 1.5) * 0.25 + 2.0
    up_cols[0:coarse_cols, :] = spread(spot, 2.0, coarse_cols)
    start = jnp.where(c == 0, coarse_cols + 2, 0).astype(F32)
    shape = (PACK, TC)
    beside = [jnp.broadcast_to(cubic_weight(spot - (start + e)), shape) for e in (0.0, 1.0)]
    beside = jnp.where(iota(shape, 0) % 2 == 0, beside[0], beside[1]).astype(BF16)
    for g in range(LANES // PACK):
        up_cols[coarse_cols + g * PACK : coarse_cols + (g + 1) * PACK, :] = beside
    pan_sum[0] = jnp.zeros((size, size), BF16)
    ms_sum[0] = jnp.zeros((coarse_size, coarse_width), BF16)
    table_copy.wait()

    def running(source, sums):
        def step(p, total):
            total = total * table[1, p].astype(F32) + source[table[0, p]].astype(F32)
            sums[p + 1] = total.astype(BF16)
            return total

        start = jnp.zeros(source.shape[1:], F32)
        lax.fori_loop(0, own_blocks, step, start, unroll=2)

    ms_load.wait()
    running(ms_ref, ms_sum)
    pan_load.wait()
    running(pan_ref, pan_sum)

    def wait_beside(row):
        @pl.when(is_last)
        def _():
            nodes_copy(row, other, row, other).wait_send()

        @pl.when(jnp.logical_not(is_last))
        def _():
            nodes_copy(row, other, row, other).wait_recv()

    def wait_nodes(k, carry):
        row = lax.rem(m + k, n)
        nodes_copy(row, c, row, c).wait()
        wait_beside(row)
        return carry

    lax.fori_loop(1, n, wait_nodes, 0)
    wait_beside(m)

    def cell_of(sums, tile, row, col):
        cell = tile * (KR * KC) + (row * KC + col)
        if cells <= LANES:
            return sums[table[2, cell]]
        return sums[table[2 + (cell >> LANE_BITS), cell & (LANES - 1)]]

    def stacked(sums, tile, col):
        return jnp.concatenate([cell_of(sums, tile, row, col) for row in range(KR)], axis=0)

    def ms_part(tile):
        row_nodes, nodes = nodes_all[c, tile, 0:1], nodes_all[c, tile, 1:2]
        after = nodes_all[1, tile, 1:2, 0:1]
        x_ms = col_coord(
            nodes, after, is_last, col_nodes, 4 * iota((1, coarse_cols), 1) + 1, 0.5
        )
        x_ms = (x_ms - 1.5) * 0.25
        col = spread(x_ms, (first_col * coarse_size).astype(F32), KC * coarse_size)
        spots = (row_coord(row_nodes, 4 * iota((coarse_rows, 1), 0) + 1, 0.5) - 1.5) * 0.25
        taps = iota((coarse_rows, KR * coarse_size), 1).astype(F32)
        weight = cubic_weight(spots - taps).astype(BF16)
        rows = [
            jnp.dot(weight, stacked(ms_sum, tile, k), preferred_element_type=F32).astype(BF16)
            for k in range(KC)
        ]
        by_band = [
            jnp.concatenate(
                [row[:, b * coarse_size : (b + 1) * coarse_size] for row in rows], axis=1
            )
            for b in range(bands)
        ]
        return jnp.dot(jnp.concatenate(by_band, axis=0), col, preferred_element_type=F32)

    def pan_part(tile):
        row_nodes, nodes = nodes_all[c, tile, 0:1], nodes_all[c, tile, 1:2]
        after = nodes_all[1, tile, 1:2, 0:1]
        x_pan = col_coord(nodes, after, is_last, col_nodes, iota((1, TC), 1), 0.0)
        col = spread(x_pan, (first_col * size).astype(F32), KC * size)
        row = spread(row_coord(row_nodes, iota((1, TR), 1), 0.0), 0.0, KR * size)
        rows = []
        for k in range(0, KC, 2):
            source = jnp.concatenate(
                [stacked(pan_sum, tile, j) for j in range(k, min(k + 2, KC))], axis=1
            )
            rows.append(
                lax.dot_general(
                    row, source, (((0,), (0,)), ((), ())), preferred_element_type=F32
                ).astype(BF16)
            )
        return jnp.dot(jnp.concatenate(rows, axis=1), col, preferred_element_type=F32)

    def line_of(k):
        up = lax.rem(pair * 2 + 2 + k, lines)
        down = lax.rem(pair * 2 + lines - 1 - k, lines)
        far = jnp.where(pair % 2 == 0, down, up)
        return jnp.where(k < lines - 2, far, jnp.where(k == lines - 2, partner, z))

    def ms_y(k):
        return remote(ms_y_send.at[k], ms_y_recv.at[k], ms_y_ss.at[k], ms_y_rs.at[k], twin, c)

    def pan_y(k, h):
        part = pl.ds(h * part_rows, part_rows)
        return remote(
            pan_y_send.at[k, part],
            pan_y_recv.at[k, part],
            pan_y_ss.at[k, h],
            pan_y_rs.at[k, h],
            twin,
            c,
        )

    def route(line):
        far = line // 2 != pair
        above = line // 2 > pair
        lower = z % 2 == 0
        inner = far & jnp.logical_xor(above, lower)
        outer = far & jnp.logical_not(jnp.logical_xor(above, lower))
        target = jnp.where(outer, partner, line)
        slot = jnp.where(outer, blocks + line, pair)
        return inner, target * 2 + y, slot

    def ms_z(k, row, slot):
        return remote(
            ms_z_send.at[k], ms_z_recv.at[slot], ms_z_ss.at[k], ms_z_rs.at[slot], row, c
        )

    def pan_z(k, h, row, slot):
        part = pl.ds(h * part_rows, part_rows)
        return remote(
            pan_z_send.at[k, part],
            pan_z_recv.at[slot, part],
            pan_z_ss.at[k, h],
            pan_z_rs.at[slot, h],
            row,
            c,
        )

    def each(first, last, step):
        if last - first == 1:
            step(first)
            return

        def body(k, carry):
            step(k)
            return carry

        lax.fori_loop(first, last, body, 0)

    near_row = partner * 2 + y

    near_ms = remote(near_ms_send, near_ms_recv, near_ss, near_rs, near_row, c)

    def ms_twin_parts(k):
        return [ms_part(line_of(k + i) * 2 + 1 - y) for i in range(2)]

    swap = route(line_of(lines - 3))[0]

    def pan_turn(k):
        first = jnp.where(swap, lines - 2, lines - 3)
        second = jnp.where(swap, lines - 3, lines - 2)
        return jnp.where(k == lines - 3, first, jnp.where(k == lines - 2, second, k))

    def pan_pair_to_twin(p):
        keys = [pan_turn(2 * p + i) for i in range(2)]
        parts = [pan_part(line_of(k) * 2 + 1 - y) for k in keys]
        for k, part in zip(keys, parts):
            pan_y_send[k] = part.astype(BF16)
        for k in keys:
            for h in range(HALVES):
                pan_y(k, h).start()

    def ms_own_parts(k):
        parts = [ms_part(line_of(k + i) * 2 + y) for i in range(2)]
        for i, part in enumerate(parts):
            ms_total[i] = part

    def ms_onward(k, i):
        line = line_of(k)
        inner, row, slot = route(line)
        ms_y(k).wait_recv()

        @pl.when(inner)
        def _():
            ms_z(0, row, blocks + line).wait_recv()
            relayed = ms_z_recv[blocks + line].astype(F32)
            total = ms_total[i] + ms_y_recv[k].astype(F32)
            ms_z_send[k] = (total + relayed).astype(BF16)

        @pl.when(jnp.logical_not(inner))
        def _():
            ms_z_send[k] = (ms_total[i] + ms_y_recv[k].astype(F32)).astype(BF16)

        ms_z(k, row, slot).start()

    def pan_own_part(k):
        pan_total[...] = pan_part(line_of(k) * 2 + y)

    def pan_forward(k):
        line = line_of(k)
        inner, row, slot = route(line)
        for h in range(HALVES):
            rows = slice(h * part_rows, (h + 1) * part_rows)
            pan_y(k, h).wait_recv()

            @pl.when(inner)
            def _():
                pan_z(0, h, row, blocks + line).wait_recv()
                relayed = pan_z_recv[blocks + line, rows].astype(F32)
                total = pan_total[rows, :] + pan_y_recv[k, rows].astype(F32)
                pan_z_send[k, rows] = (total + relayed).astype(BF16)

            @pl.when(jnp.logical_not(inner))
            def _():
                total = pan_total[rows, :] + pan_y_recv[k, rows].astype(F32)
                pan_z_send[k, rows] = total.astype(BF16)

            pan_z(k, h, row, slot).start()

    def pan_onward(k):
        pan_own_part(k)
        pan_forward(k)

    far = lines - 2
    last = lines - 1

    def ms_far_to_twin(p):
        for i, part in enumerate(ms_twin_parts(2 * p)):
            ms_y_send[2 * p + i] = part.astype(BF16)
        ms_y(2 * p).start()
        ms_y(2 * p + 1).start()

    def ms_far_onward(p):
        ms_own_parts(2 * p)
        ms_onward(2 * p, 0)
        ms_onward(2 * p + 1, 1)

    each(0, far // 2, ms_far_to_twin)
    parts = ms_twin_parts(far)
    near_ms_send[...] = parts[0].astype(BF16)
    ms_hold[...] = parts[1]
    near_ms.start()
    ms_own_parts(far)
    ms_z_send[far] = ms_total[0].astype(BF16)
    ms_z(far, near_row, pair).start()
    ms_mine[...] = ms_total[1]
    each(0, far // 2, pan_pair_to_twin)
    each(0, far // 2, ms_far_onward)
    near_ms.wait_recv()
    ms_y_send[last] = (ms_hold[...] + near_ms_recv[...].astype(F32)).astype(BF16)
    ms_y(last).start()
    pan_pair_to_twin(far // 2)
    each(0, far - 1, pan_onward)
    pan_mine[...] = pan_part(m)
    pan_own_part(pan_turn(far - 1))

    has_above, has_below = m > 0, m < n - 1

    def halo_copy(k, src, dst, row, col):
        return remote(src, dst, halo_ss.at[k], halo_rs.at[k], row, col)

    across_copy = halo_copy(0, edge_own, edge_all, m, other)
    up_copies = [
        halo_copy(1, rim_send.at[0], rim_recv.at[1], m - 1, c),
        halo_copy(2, edge_send.at[0], edge_recv.at[1], m - 1, other),
    ]
    down_copies = [
        halo_copy(3, rim_send.at[1], rim_recv.at[0], m + 1, c),
        halo_copy(4, edge_send.at[1], edge_recv.at[0], m + 1, other),
    ]
    def ms_finish():
        ms_y(last).wait_recv()
        ms_mine[...] += ms_y_recv[last].astype(F32)

        def ms_arrived(slot, carry):
            ms_z(0, m, slot).wait_recv()
            ms_mine[...] += ms_z_recv[slot].astype(F32)
            return carry

        lax.fori_loop(0, blocks, ms_arrived, 0)
        values = [ms_mine[b * coarse_rows : (b + 1) * coarse_rows, :] for b in range(bands)]
        synthetic = sum(synth_ref[b] * values[b] for b in range(bands))
        spot = iota((coarse_rows, LANES), 1) // 2
        edges = jnp.zeros((coarse_rows, LANES), F32)
        tops, bottoms = [], []
        for b in range(bands):
            result = values[b] - gain_ref[b] * synthetic
            for k in range(bands):
                result = result + mix_ref[b, k] * values[k]
            window[b] = result.astype(BF16)
            moved = pltpu.roll(result, jnp.where(c == 0, 2 * b + 2, 2 * b), 1)
            edges = jnp.where(spot == b, moved, edges)
            tops.append(result[0:2, :])
            bottoms.append(result[coarse_rows - 2 : coarse_rows, :])
        edge_own[...] = edges.astype(BF16)
        rim_send[0] = jnp.concatenate(tops, axis=0).astype(BF16)
        rim_send[1] = jnp.concatenate(bottoms, axis=0).astype(BF16)
        edge_send[0] = jnp.concatenate([edges[0:2, :]] * bands, axis=0).astype(BF16)
        bottom = edges[coarse_rows - 2 : coarse_rows, :]
        edge_send[1] = jnp.concatenate([bottom] * bands, axis=0).astype(BF16)

        across_copy.start()

        @pl.when(has_above)
        def _():
            for copy in up_copies:
                copy.start()

        @pl.when(has_below)
        def _():
            for copy in down_copies:
                copy.start()

    for load in late_loads:
        load.wait()
    pan_forward(pan_turn(far - 1))
    pan_own_part(pan_turn(far))
    ms_finish()
    pan_forward(pan_turn(far))
    across_copy.wait()

    edges = edge_all[...]
    spot = iota(edges.shape, 1) // 2
    source = jnp.concatenate(
        [
            jnp.concatenate(
                [window[b], jnp.where(spot == b, edges, jnp.zeros_like(edges))], axis=1
            )
            for b in range(bands)
        ],
        axis=0,
    )
    across[0 : bands * coarse_rows, :] = jnp.dot(
        source, up_cols[...], preferred_element_type=F32
    ).astype(BF16)
    for b in range(bands):
        own = slice(b * coarse_rows, (b + 1) * coarse_rows)
        mixed[b, PACK : TR - PACK, :] = jnp.dot(
            up_rows[PACK : TR - PACK, 0:coarse_rows],
            across[own, :],
            preferred_element_type=F32,
        ).astype(BF16)

    spans = ((PACK, TR - 2 * PACK), (0, PACK), (TR - PACK, PACK))
    stores = []
    for k, (begin, count) in enumerate(spans):
        span = pl.ds(begin, count)
        stores.append(
            pltpu.make_async_copy(
                mixed.at[:, span], mixed_hbm.at[:, span], load_sem.at[9 + k]
            )
        )
    stores[0].start()

    @pl.when(has_above)
    def _():
        for copy in up_copies:
            copy.wait_send()
        for copy in down_copies:
            copy.wait_recv()

    @pl.when(has_below)
    def _():
        for copy in down_copies:
            copy.wait_send()
        for copy in up_copies:
            copy.wait_recv()

    blank = jnp.zeros((2 * bands, LANES), BF16)

    @pl.when(jnp.logical_not(has_above))
    def _():
        rim_recv[0] = blank
        edge_recv[0] = blank

    @pl.when(jnp.logical_not(has_below))
    def _():
        rim_recv[1] = blank
        edge_recv[1] = blank

    spot = iota((2 * bands, LANES), 1) // 2
    mine = spot == iota((2 * bands, LANES), 0) // 2
    source = jnp.concatenate(
        [
            jnp.concatenate([rim_recv[i], jnp.where(mine, edge_recv[i], blank)], axis=1)
            for i in range(2)
        ],
        axis=0,
    )
    rims = jnp.dot(source, up_cols[...], preferred_element_type=F32).astype(BF16)
    outer = jnp.concatenate([up_rows[0:PACK, :], up_rows[TR - PACK : TR, :]], axis=0)
    column = iota(outer.shape, 1)
    owner_band = (column - coarse_rows) % (2 * bands) // 2
    for b in range(bands):
        weight = jnp.where((column < coarse_rows) | (owner_band == b), outer, jnp.zeros_like(outer))
        own = slice(b * coarse_rows, (b + 1) * coarse_rows)
        ends = jnp.dot(
            weight, jnp.concatenate([across[own, :], rims], axis=0), preferred_element_type=F32
        ).astype(BF16)
        mixed[b, 0:PACK, :] = ends[0:PACK, :]
        mixed[b, TR - PACK : TR, :] = ends[PACK : 2 * PACK, :]

    for k in (1, 2):
        stores[k].start()
    pan_stores = []
    for h in range(HALVES):
        rows = slice(h * part_rows, (h + 1) * part_rows)
        pan_y(last, h).wait_recv()
        pan_mine[rows, :] += pan_y_recv[last, rows].astype(F32)

        def pan_arrived(slot, carry):
            pan_z(0, h, m, slot).wait_recv()
            pan_mine[rows, :] += pan_z_recv[slot, rows].astype(F32)
            return carry

        lax.fori_loop(0, blocks, pan_arrived, 0)
        part = pl.ds(h * part_rows, part_rows)
        pan_stores.append(
            pltpu.make_async_copy(pan_mine.at[part], pan_hbm_out.at[part], load_sem.at[12 + h])
        )
        pan_stores[-1].start()

    def ms_y_sent(k, carry):
        ms_y(k).wait_send()
        return carry

    def pan_y_sent(k, carry):
        for h in range(HALVES):
            pan_y(k, h).wait_send()
        return carry

    def z_sent(k, carry):
        ms_z(k, m, 0).wait_send()
        for h in range(HALVES):
            pan_z(k, h, m, 0).wait_send()
        return carry

    near_ms.wait_send()
    lax.fori_loop(0, far, ms_y_sent, 0)
    ms_y(last).wait_send()
    lax.fori_loop(0, lines, pan_y_sent, 0)
    lax.fori_loop(0, lines - 1, z_sent, 0)
    for store in stores:
        store.wait()
    for pan_store in pan_stores:
        pan_store.wait()


def local(
    pan_blocks,
    ms_blocks,
    send_list,
    tile_list,
    row_grid,
    col_grid,
    band_mix,
    band_gain,
    synth_weight,
):
    n = lax.axis_size("mrow")
    lines = n // 2
    own_blocks, size, _ = pan_blocks.shape
    _, coarse_size, coarse_width = ms_blocks.shape
    capacity = tile_list.shape[1] // n
    bands = band_gain.shape[0]
    coarse_rows, coarse_cols = TR // 4, TC // 4
    table_rows = pl.cdiv(2 + pl.cdiv(n * KR * KC, LANES), 8) * 8
    hbm = pl.BlockSpec(memory_space=pl.ANY)
    dma = pltpu.SemaphoreType.DMA
    slots = lines // 2 + lines

    def ms_slots(count):
        return pltpu.VMEM((count, bands * coarse_rows, coarse_cols), BF16)

    def pan_slots(count):
        return pltpu.VMEM((count, TR, TC), BF16)

    mixed, pan_map = pl.pallas_call(
        functools.partial(mapping, capacity, col_grid.shape[1]),
        out_shape=(
            jax.ShapeDtypeStruct((bands, TR, TC), BF16),
            jax.ShapeDtypeStruct((TR, TC), F32),
        ),
        in_specs=[hbm] * 8,
        out_specs=(hbm, hbm),
        scratch_shapes=[
            pltpu.VMEM(send_list.shape, I32),
            pltpu.VMEM((1, row_grid.shape[0]), F32),
            pltpu.VMEM(col_grid.shape, F32),
            pltpu.SMEM(band_mix.shape, F32),
            pltpu.SMEM(band_gain.shape, F32),
            pltpu.SMEM(synth_weight.shape, F32),
            pltpu.VMEM(pan_blocks.shape, BF16),
            pltpu.VMEM(ms_blocks.shape, BF16),
            pltpu.VMEM((own_blocks + 1, size, size), BF16),
            pltpu.VMEM((own_blocks + 1, coarse_size, coarse_width), BF16),
            pltpu.VMEM((table_rows, LANES), I32),
            pltpu.SMEM((table_rows, LANES), I32),
            pltpu.VMEM((2, LANES), F32),
            pltpu.VMEM((2, n, 2, LANES), F32),
            ms_slots(lines),
            ms_slots(lines),
            pan_slots(lines),
            pan_slots(lines),
            ms_slots(lines - 1),
            ms_slots(slots),
            pan_slots(lines - 1),
            pan_slots(slots),
            pltpu.VMEM((bands * coarse_rows, coarse_cols), BF16),
            pltpu.VMEM((bands * coarse_rows, coarse_cols), BF16),
            pltpu.VMEM((TR, TC), F32),
            pltpu.VMEM((2, bands * coarse_rows, coarse_cols), F32),
            pltpu.VMEM((bands * coarse_rows, coarse_cols), F32),
            pltpu.VMEM((bands * coarse_rows, coarse_cols), F32),
            pltpu.VMEM((TR, TC), F32),
            pltpu.VMEM((bands, coarse_rows, coarse_cols), BF16),
            pltpu.VMEM((2, 2 * bands, LANES), BF16),
            pltpu.VMEM((2, 2 * bands, LANES), BF16),
            pltpu.VMEM((2, 2 * bands, LANES), BF16),
            pltpu.VMEM((2, 2 * bands, LANES), BF16),
            pltpu.VMEM((coarse_rows, LANES), BF16),
            pltpu.VMEM((coarse_rows, LANES), BF16),
            pltpu.VMEM((coarse_cols + LANES, TC), BF16),
            pltpu.VMEM((TR, coarse_rows + 4 * bands), BF16),
            pltpu.VMEM((bands * coarse_rows, TC), BF16),
            pltpu.VMEM((bands, TR, TC), BF16),
            dma((12 + HALVES,)),
            dma((2, n)),
            dma((2, n)),
            dma((lines,)),
            dma((lines,)),
            dma((lines, HALVES)),
            dma((lines, HALVES)),
            dma((lines - 1,)),
            dma((slots,)),
            dma((lines - 1, HALVES)),
            dma((slots, HALVES)),
            dma,
            dma,
            dma((5,)),
            dma((5,)),
        ],
        compiler_params=pltpu.CompilerParams(
            collective_id=0, has_side_effects=True, vmem_limit_bytes=60 * 1024 * 1024
        ),
        name="mapping",
    )(
        send_list,
        row_grid[None, :],
        col_grid,
        pan_blocks,
        ms_blocks,
        band_mix,
        band_gain,
        synth_weight,
    )
    detail = band_gain[:, None, None] * pan_map[None]
    return (mixed.astype(F32) + detail).astype(BF16)


def solution(mesh):
    return jax.shard_map(
        local,
        mesh=mesh,
        in_specs=(
            P(("scene", "mrow", "mcol"), None, None),
            P(("scene", "mrow", "mcol"), None, None),
            P(None, ("scene", "mrow", "mcol")),
            P(None, ("scene", "mrow", "mcol")),
            P(("scene", "mrow")),
            P(("scene", "mrow"), "mcol"),
            P(),
            P(),
            P(),
        ),
        out_specs=P(None, ("scene", "mrow"), "mcol"),
        check_vma=False,
    )
```
